32 devices in a mesh: dp: 8 (over y, x, core), tp: 4 (over z).
Axes of the slice: x: 2, y: 2, z: 4, core: 2. Of those that a mesh axis runs over, the one named last changes fastest.
Arguments:
- frames_in: bfloat16 [65536, 160], P('dp'), may hold values from -6 to 6
- out_grad: bfloat16 [65536, 160], P('dp'), may hold values from -6 to 6
- logdet_grad: float32 [64], P('dp'), may hold values from -6 to 6
- lengths: int32 [64], P('dp'), may hold values from 200 to 1000, as said below
- offsets: int32 [64], P('dp'), may hold values from 2 to 7990, as said below
- owners: int32 [8], replicated, may hold values from 0 to 7, each once
- small_params: float32 [3, 160], replicated, may hold values from -0.3 to 0.3
- small_moment: float32 [3, 160], replicated, may hold values from -1280 to 1280
- small_square: float32 [3, 160], replicated, may hold values from 41943.04 to 167772.16
- mix: float32 [4, 4], replicated, as said below
- mix_moment: float32 [4, 4], replicated, may hold values from -10240 to 10240
- mix_square: float32 [4, 4], replicated, may hold values from 2621440 to 10485760
- pre_weight: float32 [80, 192], replicated, may hold values from -0.625 to 0.625
- pre_moment: float32 [80, 192], replicated, may hold values from -256 to 256
- pre_square: float32 [80, 192], replicated, may hold values from 1966.08 to 7864.32
- conv_weight: float32 [4, 960, 2, 192], P(None, 'dp', None, 'tp'), may hold values from -0.1875 to 0.1875
- conv_moment: float32 [4, 960, 384], P(None, 'dp', 'tp'), may hold values from -160 to 160
- conv_square: float32 [4, 960, 384], P(None, 'dp', 'tp'), may hold values from 655.36 to 2621.44
- conv_basis: float32 [4, 2, 192, 384], P(None, None, None, 'tp'), as said below
- conv_bias: float32 [4, 2, 192], P(None, None, 'tp'), may hold values from -3 to 3
- conv_bias_moment: float32 [4, 2, 192], P(None, None, 'tp'), may hold values from -160 to 160
- conv_bias_square: float32 [4, 2, 192], P(None, None, 'tp'), may hold values from 655.36 to 2621.44
- res_skip: float32 [7, 192, 192], P(None, 'tp'), may hold values from -0.4375 to 0.4375
- res_skip_moment: float32 [7, 192, 192], P(None, 'tp'), may hold values from -160 to 160
- res_skip_square: float32 [7, 192, 192], P(None, 'tp'), may hold values from 655.36 to 2621.44
- end_weight: float32 [192, 160], P('tp'), may hold values from -0.21875 to 0.21875
- end_moment: float32 [192, 160], P('tp'), may hold values from -768 to 768
- end_square: float32 [192, 160], P('tp'), may hold values from 16384 to 65536
Outputs:
- frames_out: float32 [65536, 160], P('dp')
- logdet: float32 [64], P('dp')
- frames_grad: float32 [65536, 160], P('dp')
- small_new: float32 [3, 160], replicated
- small_moment_new: float32 [3, 160], replicated
- small_square_new: float32 [3, 160], replicated
- mix_new: float32 [4, 4], replicated
- mix_moment_new: float32 [4, 4], replicated
- mix_square_new: float32 [4, 4], replicated
- pre_new: float32 [80, 192], replicated
- pre_moment_new: float32 [80, 192], replicated
- pre_square_new: float32 [80, 192], replicated
- conv_new: float32 [4, 960, 2, 192], P(None, 'dp', None, 'tp')
- conv_moment_new: float32 [4, 960, 384], P(None, 'dp', 'tp')
- conv_square_new: float32 [4, 960, 384], P(None, 'dp', 'tp')
- conv_bias_new: float32 [4, 2, 192], P(None, None, 'tp')
- conv_bias_moment_new: float32 [4, 2, 192], P(None, None, 'tp')
- conv_bias_square_new: float32 [4, 2, 192], P(None, None, 'tp')
- res_skip_new: float32 [7, 192, 192], P(None, 'tp')
- res_skip_moment_new: float32 [7, 192, 192], P(None, 'tp')
- res_skip_square_new: float32 [7, 192, 192], P(None, 'tp')
- end_new: float32 [192, 160], P('tp')
- end_moment_new: float32 [192, 160], P('tp')
- end_square_new: float32 [192, 160], P('tp')
The draws below stay inside these ranges and needn't reach their ends.
Inputs may be any that keep to these rules, and one draw needn't show every extreme that they name: `lengths`: each block of 8 utterances holds one utterance of exactly 1000 frames. Utterance u occupies frames offsets[u] to offsets[u] + lengths[u] - 1 of block u // 8; in a block the utterances come in order, and the runs of empty frames before, between and after them have 2 frames or more. `owners`: each device of dp owns exactly one row block. mix has a positive diagonal larger than the sum of the magnitudes of the rest of its row. Each conv_basis[l], viewed as a 384 x 2 * 192 matrix, is orthogonal.
All inputs are finite; a program needn't handle non-finite values.
Results may differ from the reference program's by a relative error of at most 0.022.
Values may be sent and summed in bfloat16 or wider, within the bound.
No kernel may reach another device: no remote copies, remote signals or barrier semaphores. Data moves between devices by JAX's collectives and lax.ppermute only.
A program may use at most 448 MiB of HBM per device.

```python
import math
import jax
import jax.numpy as jnp
from jax import lax

C = 160
HALF = 80
HID = 192
KER = 5
LAYERS = 4
STEP = 5
FRAMES_DEV = 8192
LMIN = 200
LMAX = 1000
UTT_DEV = 8
UTTS = 64
FRAMES = 65536
N_DP = 8


def packing(key):
    blocks = UTTS // UTT_DEV
    key_length, key_pick, key_spare = jax.random.split(jax.random.fold_in(key, 17), 3)
    length_all = jax.random.randint(key_length, (blocks, UTT_DEV), LMIN, LMAX + 1)
    picked_slot = jax.random.randint(key_pick, (blocks, 1), 0, UTT_DEV)
    slot_index = jnp.arange(UTT_DEV, dtype=jnp.int32)[None, :]
    length_all = jnp.where(slot_index == picked_slot, LMAX, length_all)
    spare_frames = FRAMES_DEV - jnp.sum(length_all, axis=1, keepdims=True) - 2 * (UTT_DEV + 1)
    weights_int = jax.random.randint(key_spare, (blocks, UTT_DEV + 1), 0, 1000)
    gap_sizes = 2 + spare_frames * weights_int // (jnp.sum(weights_int, axis=1, keepdims=True) + 1)
    start_frames = jnp.cumsum(gap_sizes[:, :UTT_DEV], axis=1) + jnp.cumsum(length_all, axis=1) - length_all
    return (length_all.reshape(UTTS).astype(jnp.int32), start_frames.reshape(UTTS).astype(jnp.int32))


def draw_lengths(key, part):
    return packing(key)[0]


def draw_offsets(key, part):
    return packing(key)[1]


def draw_mix(key, part):
    key_diag, key_other = jax.random.split(jax.random.fold_in(key, 23))
    diagonal = jax.random.uniform(key_diag, (4,), jnp.float32, 0.8, 1.2)
    others = jax.random.uniform(key_other, (4, 4), jnp.float32, -0.25, 0.25)
    identity = jnp.eye(4, dtype=jnp.float32)
    return others * (1.0 - identity) + identity * diagonal[None, :]


def draw_conv_basis(key, part):
    size_total = 2 * HID

    def rotation_for(layer_key):
        matrix = jnp.eye(size_total, dtype=jnp.float32)
        for round_idx in range(8):
            key_perm, key_angle = jax.random.split(jax.random.fold_in(layer_key, round_idx))
            row_order = jax.random.permutation(key_perm, size_total)
            first_rows = row_order[0::2]
            second_rows = row_order[1::2]
            angles = jax.random.uniform(key_angle, (size_total // 2,), jnp.float32, -3.14159, 3.14159)
            partner = jnp.zeros((size_total,), jnp.int32).at[first_rows].set(second_rows).at[second_rows].set(first_rows)
            cosine = jnp.zeros((size_total,), jnp.float32).at[first_rows].set(jnp.cos(angles)).at[second_rows].set(jnp.cos(angles))
            signed = jnp.zeros((size_total,), jnp.float32).at[first_rows].set(-jnp.sin(angles)).at[second_rows].set(jnp.sin(angles))
            matrix = cosine[:, None] * matrix + signed[:, None] * matrix[partner]
        return matrix
    layer_keys = jax.random.split(jax.random.fold_in(key, 29), LAYERS)
    return jax.vmap(rotation_for)(layer_keys).reshape(LAYERS, 2, HID, size_total)


def levels(own_key, dims, cuts, least, top_value):
    loudness = 1.0
    for dim, parts in cuts:
        draws = jax.random.uniform(jax.random.fold_in(jax.random.fold_in(own_key, 6), dim), (parts,), jnp.float32, least / len(cuts), top_value / len(cuts))
        loudness = loudness * jnp.repeat(jnp.exp(draws), dims[dim] // parts).reshape((-1,) + (1,) * (len(dims) - 1 - dim))
    return loudness


def noise(rng, shape, scale, bound, cuts=(), kind=jnp.bfloat16):
    loudness = levels(rng, shape, cuts, -0.22, 0.18) if cuts else 1.0
    drawn = jax.random.normal(rng, shape, jnp.float32) * scale * loudness
    return jnp.minimum(jnp.maximum(drawn, -bound), bound).astype(kind)


def setup_inputs(seed: int = 0) -> dict:
    key_list = jax.random.split(jax.random.key(seed), 29)
    return {
        "frames_in": noise(key_list[0], (FRAMES, C), 1.0, 6.0, ((0, 8),)),
        "out_grad": noise(key_list[1], (FRAMES, C), 1.0, 6.0, ((0, 8),)),
        "logdet_grad": noise(key_list[2], (UTTS,), 1.0, 6.0, ((0, 8),), jnp.float32),
        "lengths": draw_lengths(jax.random.fold_in(key_list[28], 71), 0),
        "offsets": draw_offsets(jax.random.fold_in(key_list[28], 71), 0),
        "owners": jax.random.permutation(key_list[5], N_DP).astype(jnp.int32),
        "small_params": jnp.clip(jax.random.uniform(key_list[6], (3, C), jnp.float32, -0.3, 0.3), -0.3, 0.3),
        "small_moment": noise(key_list[7], (3, C), (0.8 * (FRAMES_DEV * N_DP) ** 0.5), 1280.0, (), jnp.float32),
        "small_square": jnp.clip(jnp.exp(jax.random.uniform(key_list[8], (3, C), jnp.float32, math.log(41943.04), math.log(167772.16))), 41943.04, 167772.16),
        "mix": draw_mix(jax.random.fold_in(key_list[28], 71), 0),
        "mix_moment": noise(key_list[10], (4, 4), ((C * FRAMES_DEV * N_DP // 4) ** 0.5), 10240.0, (), jnp.float32),
        "mix_square": jnp.clip(jnp.exp(jax.random.uniform(key_list[11], (4, 4), jnp.float32, math.log(2621440), math.log(10485760))), 2621440, 10485760),
        "pre_weight": noise(key_list[12], (HALF, HID), HALF ** -0.5, 0.625, (), jnp.float32),
        "pre_moment": noise(key_list[13], (HALF, HID), (0.17 * (FRAMES_DEV * N_DP) ** 0.5), 256.0, (), jnp.float32),
        "pre_square": jnp.clip(jnp.exp(jax.random.uniform(key_list[14], (HALF, HID), jnp.float32, math.log(1966.08), math.log(7864.32))), 1966.08, 7864.32),
        "conv_weight": noise(key_list[15], (LAYERS, KER * HID, 2, HID), (KER * HID) ** -0.5, 0.1875, ((1, 8), (3, 4)), jnp.float32),
        "conv_moment": noise(key_list[16], (LAYERS, KER * HID, 2 * HID), (0.1 * (FRAMES_DEV * N_DP) ** 0.5), 160.0, ((1, 8), (2, 4)), jnp.float32),
        "conv_square": jnp.clip(jnp.exp(math.log(2621.44) - 1.3862944 * jax.random.uniform(key_list[17], (LAYERS, KER * HID, 2 * HID), jnp.float32) ** levels(key_list[17], (LAYERS, KER * HID, 2 * HID), ((1, 8), (2, 4)), -0.2, 0.2)), 655.36, 2621.44),
        "conv_basis": draw_conv_basis(jax.random.fold_in(key_list[28], 71), 0),
        "conv_bias": noise(key_list[19], (LAYERS, 2, HID), 0.5, 3.0, ((2, 4),), jnp.float32),
        "conv_bias_moment": noise(key_list[20], (LAYERS, 2, HID), (0.1 * (FRAMES_DEV * N_DP) ** 0.5), 160.0, ((2, 4),), jnp.float32),
        "conv_bias_square": jnp.clip(jnp.exp(math.log(2621.44) - 1.3862944 * jax.random.uniform(key_list[21], (LAYERS, 2, HID), jnp.float32) ** levels(key_list[21], (LAYERS, 2, HID), ((2, 4),), -0.2, 0.2)), 655.36, 2621.44),
        "res_skip": noise(key_list[22], (2 * LAYERS - 1, HID, HID), HID ** -0.5, 0.4375, ((1, 4),), jnp.float32),
        "res_skip_moment": noise(key_list[23], (2 * LAYERS - 1, HID, HID), (0.1 * (FRAMES_DEV * N_DP) ** 0.5), 160.0, ((1, 4),), jnp.float32),
        "res_skip_square": jnp.clip(jnp.exp(math.log(2621.44) - 1.3862944 * jax.random.uniform(key_list[24], (2 * LAYERS - 1, HID, HID), jnp.float32) ** levels(key_list[24], (2 * LAYERS - 1, HID, HID), ((1, 4),), -0.2, 0.2)), 655.36, 2621.44),
        "end_weight": noise(key_list[25], (HID, C), (4 * HID) ** -0.5, 0.21875, ((0, 4),), jnp.float32),
        "end_moment": noise(key_list[26], (HID, C), (0.5 * (FRAMES_DEV * N_DP) ** 0.5), 768.0, ((0, 4),), jnp.float32),
        "end_square": jnp.clip(jnp.exp(math.log(65536.0) - 1.3862944 * jax.random.uniform(key_list[27], (HID, C), jnp.float32) ** levels(key_list[27], (HID, C), ((0, 4),), -0.2, 0.2)), 16384.0, 65536.0),
    }


BETA = 0.5
EPSILON = 1e-08
DECAY = 0.01
RATE_SMALL = 0.1
RATE_MIX = 0.3
RATE_PRE = 0.1
RATE_CONV = 0.03
RATE_BIAS = 0.3
RATE_RESSKIP = 0.07
RATE_END = 0.04
PRECISE = lax.Precision.HIGHEST

@jax.custom_vjp
def low(v):
    return lax.optimization_barrier(v.astype(jnp.bfloat16)).astype(jnp.float32)

@jax.custom_vjp
def low_back(v):
    return v

def low_keep(v):
    return (low(v), None)

def low_pass(kept, grad):
    return (grad,)

def back_keep(v):
    return (v, None)

def back_low(kept, grad):
    return (low(grad),)
low.defvjp(low_keep, low_pass)
low_back.defvjp(back_keep, back_low)

def matmul_high(left_op, right_op):
    return jnp.dot(left_op, right_op, precision=PRECISE, preferred_element_type=jnp.float32)

def minor_det(pair_rows, column_left, column_right):
    return pair_rows[0, column_left] * pair_rows[1, column_right] - pair_rows[1, column_left] * pair_rows[0, column_right]

def determinant(matrix):
    upper_rows = matrix[:2]
    lower_rows = matrix[2:]
    return minor_det(upper_rows, 0, 1) * minor_det(lower_rows, 2, 3) - minor_det(upper_rows, 0, 2) * minor_det(lower_rows, 1, 3) + minor_det(upper_rows, 0, 3) * minor_det(lower_rows, 1, 2) + minor_det(upper_rows, 1, 2) * minor_det(lower_rows, 0, 3) - minor_det(upper_rows, 1, 3) * minor_det(lower_rows, 0, 2) + minor_det(upper_rows, 2, 3) * minor_det(lower_rows, 0, 1)

def channel_mix(values, matrix):
    frame_count = values.shape[0]
    width = values.shape[1]
    folded = values.reshape(frame_count, 2, width // 4, 2)
    mixed = jnp.einsum('fajk,xyak->fxjy', folded, matrix.reshape(2, 2, 2, 2), precision=PRECISE)
    return mixed.reshape(frame_count, width)

def block_forward(parameters, frames, offset_block, length_block):
    small_params, mix, pre_weight, conv_nat, conv_bias, res_skip, end_weight = parameters
    position = jnp.arange(FRAMES_DEV, dtype=jnp.int32)
    member = ((position[None, :] >= offset_block[:, None]) & (position[None, :] < (offset_block + length_block)[:, None])).astype(jnp.float32)
    frame_mask = lax.optimization_barrier(jnp.sum(member, axis=0))[:, None]
    normed = (small_params[1] + jnp.exp(small_params[0]) * frames) * frame_mask
    mixed = channel_mix(normed, mix)
    first_half = mixed[:, :HALF]
    second_half = mixed[:, HALF:]
    hidden = low_back(matmul_high(low(first_half), low(pre_weight))) * frame_mask
    skip_total = jnp.zeros((FRAMES_DEV, HID), jnp.float32)
    half_taps = KER // 2
    for layer_idx in range(LAYERS):
        padded = jnp.pad(low(hidden), ((half_taps, half_taps), (0, 0)))
        shifted = jnp.concatenate([padded[tap_idx:tap_idx + FRAMES_DEV] for tap_idx in range(KER)], axis=1)
        gate_values = low_back(matmul_high(shifted, low(conv_nat[layer_idx]).reshape(KER * HID, 2 * HID)) + conv_bias[layer_idx].reshape(2 * HID))
        activated = low(jnp.tanh(gate_values[:, :HID]) * jax.nn.sigmoid(gate_values[:, HID:]))
        skip_total = skip_total + matmul_high(activated, low(res_skip[LAYERS - 1 + layer_idx]))
        if layer_idx < LAYERS - 1:
            hidden = (hidden + low_back(matmul_high(activated, low(res_skip[layer_idx])))) * frame_mask
    skip_low = low(low_back(skip_total) * frame_mask)
    projected = low_back(matmul_high(skip_low, low(end_weight)) + small_params[2])
    shift_part = projected[:, :HALF]
    log_scale = projected[:, HALF:]
    coupled = (shift_part + jnp.exp(log_scale) * second_half) * frame_mask
    out_block = jnp.concatenate([first_half, coupled], axis=1)
    per_frame = lax.optimization_barrier(jnp.sum(log_scale * frame_mask, axis=1))
    logdet_block = jnp.sum(small_params[0]) + C // 4 * jnp.log(determinant(mix)) + matmul_high(member, per_frame) / length_block.astype(jnp.float32)
    return (out_block, logdet_block)

def moments(moment, square, grad):
    new_moment = BETA * moment + (1.0 - BETA) * grad
    new_square = BETA * square + (1.0 - BETA) * grad * grad
    correction = 1.0 - BETA ** STEP
    direction = new_moment / correction / (jnp.sqrt(new_square / correction) + EPSILON)
    return (new_moment, new_square, direction)

def adam_update(weight, moment, square, grad, rate):
    new_moment, new_square, direction = moments(moment, square, grad)
    return (weight - rate * (direction + DECAY * weight), new_moment, new_square)

def reference(frames_in, out_grad, logdet_grad, lengths, offsets, owners, small_params, small_moment, small_square, mix, mix_moment, mix_square, pre_weight, pre_moment, pre_square, conv_weight, conv_moment, conv_square, conv_basis, conv_bias, conv_bias_moment, conv_bias_square, res_skip, res_skip_moment, res_skip_square, end_weight, end_moment, end_square):
    rows_own = KER * HID // N_DP
    conv_nat = conv_weight.reshape(LAYERS, N_DP, rows_own, 2, HID)[:, owners].reshape(LAYERS, KER * HID, 2, HID)
    frame_blocks = frames_in.astype(jnp.float32).reshape(N_DP, FRAMES_DEV, C)
    offset_blocks = offsets.reshape(N_DP, UTT_DEV)
    length_blocks = lengths.reshape(N_DP, UTT_DEV)

    def whole(parameters, frames_all):

        def scan_body(running, block_items):
            frames, offset_block, length_block = block_items
            out_block, logdet_block = jax.checkpoint(block_forward)(parameters, frames, offset_block, length_block)
            return (running, (out_block, logdet_block))
        unused, (outputs, logdets) = lax.scan(scan_body, jnp.zeros((), jnp.float32), (frames_all, offset_blocks, length_blocks))
        return (outputs.reshape(FRAMES, C), logdets.reshape(UTTS))
    parameters = (small_params, mix, pre_weight, conv_nat, conv_bias, res_skip, end_weight)
    (frames_out, logdet), pullback = jax.vjp(whole, parameters, frame_blocks)
    gradients, frames_grad = pullback((out_grad.astype(jnp.float32), logdet_grad))
    grad_small, grad_mix, grad_pre, grad_conv, grad_bias, grad_resskip, grad_end = gradients
    small_new, small_moment_new, small_square_new = adam_update(small_params, small_moment, small_square, grad_small, RATE_SMALL)
    mix_new, mix_moment_new, mix_square_new = adam_update(mix, mix_moment, mix_square, grad_mix, RATE_MIX)
    pre_new, pre_moment_new, pre_square_new = adam_update(pre_weight, pre_moment, pre_square, grad_pre, RATE_PRE)
    bias_new, bias_moment_new, bias_square_new = adam_update(conv_bias, conv_bias_moment, conv_bias_square, grad_bias, RATE_BIAS)
    resskip_new, resskip_moment_new, resskip_square_new = adam_update(res_skip, res_skip_moment, res_skip_square, grad_resskip, RATE_RESSKIP)
    end_new, end_moment_new, end_square_new = adam_update(end_weight, end_moment, end_square, grad_end, RATE_END)
    inverse = jnp.argsort(owners).astype(jnp.int32)
    grad_stored = grad_conv.reshape(LAYERS, N_DP, rows_own, 2, HID)[:, inverse].reshape(LAYERS, KER * HID, 2 * HID)
    basis = conv_basis.reshape(LAYERS, 2 * HID, 2 * HID)
    rotated = jnp.einsum('lrn,lnk->lrk', grad_stored, basis, precision=PRECISE)
    conv_moment_new, conv_square_new, direction = moments(conv_moment, conv_square, rotated)
    back_rotated = jnp.einsum('lrk,lnk->lrn', direction, basis, precision=PRECISE).reshape(conv_weight.shape)
    conv_new = conv_weight - RATE_CONV * (back_rotated + DECAY * conv_weight)
    return (frames_out, logdet, frames_grad.reshape(FRAMES, C), small_new, small_moment_new, small_square_new, mix_new, mix_moment_new, mix_square_new, pre_new, pre_moment_new, pre_square_new, conv_new, conv_moment_new, conv_square_new, bias_new, bias_moment_new, bias_square_new, resskip_new, resskip_moment_new, resskip_square_new, end_new, end_moment_new, end_square_new)
```

```python
import functools
import jax
import jax.numpy as jnp
import numpy as np
from jax import lax
from jax.experimental import pallas as pl
from jax.experimental.pallas import tpu as pltpu
from jax.sharding import PartitionSpec as P

C = 160
HALF = 80
HID = 192
KER = 5
LAYERS = 4
STEP = 5
HALO = 128
TILE = 768
MAX_PACKED = 1024

BETA = 0.5
EPSILON = 1e-08
DECAY = 0.01
RATE_SMALL = 0.1
RATE_MIX = 0.3
RATE_PRE = 0.1
RATE_CONV = 0.03
RATE_BIAS = 0.3
RATE_RESSKIP = 0.07
RATE_END = 0.04
PRECISE = lax.Precision.HIGHEST
BF = jnp.bfloat16
F32 = jnp.float32

CH = np.arange(C)
PAIR = 2 * (CH // HALF) + CH % 2
GROUP = (CH % HALF) // 2
ONE_HOT = (PAIR[:, None] == np.arange(4)[None, :]).astype(np.float32)
SAME = (GROUP[:, None] == GROUP[None, :]).astype(np.float32)


def nn(a, b, precision=None):
    return lax.dot_general(a, b, (((1,), (0,)), ((), ())), precision=precision, preferred_element_type=F32)


def nt(a, b, precision=None):
    return lax.dot_general(a, b, (((1,), (1,)), ((), ())), precision=precision, preferred_element_type=F32)


def tn(a, b, precision=None):
    return lax.dot_general(a, b, (((0,), (0,)), ((), ())), precision=precision, preferred_element_type=F32)


def sigmoid(x):
    return 0.5 * jnp.tanh(0.5 * x) + 0.5


def vm():
    return pl.BlockSpec(memory_space=pltpu.VMEM)


def sm():
    return pl.BlockSpec(memory_space=pltpu.SMEM)


def hb():
    return pl.BlockSpec(memory_space=pl.ANY)


def bit_reverse(value, bits):
    out = value * 0
    for i in range(bits):
        out = out | (((value >> i) & 1) << (bits - 1 - i))
    return out


def prep_kernel(dp, tp, rows, meta, *refs):
    packed = dp * 128 <= MAX_PACKED
    npiece = dp if packed else 1
    pieces = refs[:npiece]
    res_pieces = refs[npiece : npiece + tp]
    end_pieces = refs[npiece + tp : npiece + 2 * tp]
    wt, wd, rsf, rsb, end, end_t, scratch, sem = refs[npiece + 2 * tp :]
    units = HID // tp
    me_tp = meta[0]
    me_dp = meta[1]
    copies = [pltpu.make_async_copy(pieces[m], scratch.at[m], sem.at[m]) for m in range(npiece)]
    for c in copies:
        c.start()
    for kk in range(tp):
        src = lax.rem(me_tp - kk + tp, tp)
        row = pl.ds(pl.multiple_of(src * units, 16), units)
        for layer in range(LAYERS):
            rsb[layer, row, 0:HID] = res_pieces[kk][LAYERS - 1 + layer]
            if layer < LAYERS - 1:
                rsb[layer, row, HID : 2 * HID] = res_pieces[kk][layer]
            else:
                rsb[layer, row, HID : 2 * HID] = jnp.zeros((units, HID), BF)
        end[row, :] = end_pieces[kk][...]
    for layer in range(LAYERS):
        both = rsb[layer].astype(F32)
        rsf[layer, 0:HID, :] = both[:, HID : 2 * HID].T.astype(BF)
        rsf[layer, HID : 2 * HID, :] = both[:, 0:HID].T.astype(BF)
    end_t[...] = end[...].astype(F32).T.astype(BF)
    for c in copies:
        c.wait()

    def layer_body(layer, carry):
        if not packed:
            wt[layer] = scratch[0, layer]
        for b in range(dp if packed else 0):
            m = jnp.bitwise_xor(me_dp, meta[2 + b])
            for kk in range(tp):
                src = lax.rem(me_tp - kk + tp, tp)
                for h in range(2):
                    row = pl.ds(pl.multiple_of(src * units + h * HID, 16), units)
                    wt[layer, row, b * rows : (b + 1) * rows] = scratch[
                        m, kk, layer, h * units : (h + 1) * units, 0:rows
                    ]
        for k in range(KER):
            wd[layer, :, k * 2 * HID : (k + 1) * 2 * HID] = (
                wt[layer, :, k * HID : (k + 1) * HID].astype(F32).T.astype(BF)
            )
        return carry

    lax.fori_loop(0, LAYERS, layer_body, 0)


def build_taps(read, x_ref, t, groups, reverse):
    half = KER // 2

    def body(i, carry):
        value = read(pl.ds(pl.multiple_of(i * 16, 16), 16))
        for k in range(KER):
            shift = (half - k) if not reverse else (k - half)
            shift %= t
            moved = value if shift == 0 else pltpu.roll(value, shift, 1)
            x_ref[pl.ds(pl.multiple_of(k * groups * 16 + i * 16, 16), 16), :] = moved.astype(BF)
        return carry

    lax.fori_loop(0, groups, body, 0)


def window_forward(own, t, w, s, w0):
    pos = lax.broadcasted_iota(jnp.int32, (8, t), 1) + w0
    member = jnp.logical_and(pos >= w["off"][...], pos < w["end_frame"][...]).astype(F32)
    s["member"][...] = member
    s["mask"][...] = jnp.broadcast_to(jnp.sum(member, axis=0, keepdims=True), (8, t))
    tiles = t // TILE

    def cols_of(j):
        return pl.ds(pl.multiple_of(j * TILE, TILE), TILE)

    def head(j, carry):
        cols = cols_of(j)
        mask = s["mask"][0:1, cols]
        fr = s["fr"][:, cols]
        mixed = (nn(w["a_hi"][...], fr) + nn(w["a_lo"][...], fr) + w["cvec"][...]) * mask
        s["mixed"][:, cols] = mixed
        s["h"][:, cols] = nn(w["pre_t"][...], mixed[0:HALF].astype(BF)) * mask
        s["skip"][:, cols] = jnp.zeros((HID, TILE), F32)
        return carry

    lax.fori_loop(0, tiles, head, 0)

    def layer_body(layer, carry):
        build_taps(lambda rows: s["h"][rows, :], s["x"], t, HID // 16, False)

        def tile(j, carry):
            cols = cols_of(j)
            mask = s["mask"][0:1, cols]
            g = nn(w["wt"][layer], s["x"][0 : KER * HID, cols]) + w["bias"][layer]
            tt = jnp.tanh(g[0:HID])
            ss = sigmoid(g[HID : 2 * HID])
            act = (tt * ss).astype(BF)
            y = nn(w["rsf"][layer], act)
            s["skip"][:, cols] += y[HID : 2 * HID]
            hv = s["h"][:, cols]
            if own:
                s["hb"][layer, :, cols] = hv.astype(BF)
                s["tt"][layer, :, cols] = tt.astype(BF)
                s["ss"][layer, :, cols] = ss.astype(BF)
            s["h"][:, cols] = (hv + y[0:HID]) * mask
            return carry

        lax.fori_loop(0, tiles, tile, 0)
        return carry

    lax.fori_loop(0, LAYERS, layer_body, 0)


def window_tail(own, t, w, s):
    tiles = t // TILE

    def tail(j, carry):
        cols = pl.ds(pl.multiple_of(j * TILE, TILE), TILE)
        mask = s["mask"][0:1, cols]
        skip_low = (s["skip"][:, cols] * mask).astype(BF)
        proj = nn(w["end_t"][...], skip_low) + w["ebias"][...]
        shift = proj[0:HALF]
        log_scale = proj[HALF:C]
        e = jnp.exp(log_scale)
        x0 = s["mixed"][0:HALF, cols]
        x1 = s["mixed"][HALF:C, cols]
        s["fo"][0:HALF, cols] = x0
        s["fo"][HALF:C, cols] = (shift + e * x1) * mask
        s["pf"][:, cols] = jnp.broadcast_to(jnp.sum(log_scale, axis=0, keepdims=True), (8, TILE))
        og = s["og"][:, cols].astype(F32)
        d_shift = og[HALF:C] * mask
        de = d_shift * e
        dm = jnp.concatenate([og[0:HALF] * mask, de], axis=0).astype(BF)
        s["p1"][:, cols] = nn(w["at_hi"][...], dm)
        if own:
            s["dm"][:, cols] = dm
            s["x0b"][:, cols] = x0.astype(BF)
            fw = jnp.sum(s["member"][:, cols] * w["fw"][...], axis=0, keepdims=True)
            d_log = de * x1 + fw
            d_proj = jnp.concatenate([d_shift, d_log], axis=0).astype(BF)
            s["dproj"][:, cols] = d_proj
            s["skl"][:, cols] = skip_low
            s["dsk"][:, cols] = (nn(w["end"][...], d_proj) * mask).astype(BF)
        return carry

    lax.fori_loop(0, tiles, tail, 0)


def logdet_part(s, own_cols):
    part = jnp.sum(s["member"][:, own_cols] * s["pf"][:, own_cols], axis=1, keepdims=True)
    return jnp.broadcast_to(part, (8, 128))


FW = ["wt", "rsf", "bias", "a_hi", "a_lo", "at_hi", "cvec", "pre_t", "end_t", "ebias", "off", "end_frame", "fw"]
OW = ["wd", "rsb", "end", "pre", "mixfull", "consts", "onehot", "same", "extra"]


def fwd_scratch(t):
    return {
        "member": pltpu.VMEM((8, t), F32),
        "mask": pltpu.VMEM((8, t), F32),
        "pf": pltpu.VMEM((8, t), F32),
        "fr": pltpu.VMEM((C, t), BF),
        "og": pltpu.VMEM((C, t), BF),
        "mixed": pltpu.VMEM((C, t), F32),
        "h": pltpu.VMEM((HID, t), F32),
        "skip": pltpu.VMEM((HID, t), F32),
        "fo": pltpu.VMEM((C, t), F32),
        "p1": pltpu.VMEM((C, t), F32),
    }


def own_scratch(t):
    return {
        "hb": pltpu.VMEM((LAYERS, HID, t), BF),
        "tt": pltpu.VMEM((LAYERS, HID, t), BF),
        "ss": pltpu.VMEM((LAYERS, HID, t), BF),
        "dm": pltpu.VMEM((C, t), BF),
        "x0b": pltpu.VMEM((HALF, t), BF),
        "dproj": pltpu.VMEM((C, t), BF),
        "skl": pltpu.VMEM((HID, t), BF),
        "dsk": pltpu.VMEM((HID, t), BF),
        "d": pltpu.VMEM((2 * HID, t), BF),
        "dg": pltpu.VMEM((2 * HID, t), BF),
        "dw": pltpu.VMEM((2 * HID, 1024), F32),
        "smallg": pltpu.VMEM((16, 2 * HID), F32),
    }


def own_kernel(dp, tp, rows, own_len, t, names, snames, meta, *refs):
    n = len(names)
    w = dict(zip(names, refs[: n]))
    fr_any, og_any = refs[n : n + 2]
    fo_any, p1_any, ld, gsend, osend, dpp = refs[n + 2 : n + 8]
    s = dict(zip(snames, refs[n + 8 : -1]))
    smallg = s["smallg"]
    sem = refs[-1]
    w0 = pl.multiple_of(meta[0], 128)
    off = pl.multiple_of(meta[1], 128)
    start = pl.multiple_of(meta[2], 128)
    me_dp = meta[3]
    me_tp = meta[4]
    core = jnp.bitwise_and(me_dp, 1)
    low_half = core
    high_half = 1 - core
    bits = (dp - 1).bit_length()
    units = HID // tp
    slots = [lax.rem(q - me_tp + tp, tp) for q in range(tp)]
    c0 = pltpu.make_async_copy(fr_any.at[:, pl.ds(w0, t)], s["fr"], sem.at[0])
    c1 = pltpu.make_async_copy(og_any.at[:, pl.ds(w0, t)], s["og"], sem.at[1])
    c0.start()
    c1.start()
    c0.wait()
    c1.wait()
    window_forward(True, t, w, s, w0)
    window_tail(True, t, w, s)
    own = pl.ds(off, own_len)
    o0 = pltpu.make_async_copy(s["fo"].at[:, own], fo_any.at[:, pl.ds(start, own_len)], sem.at[2])
    o1 = pltpu.make_async_copy(s["p1"].at[:, own], p1_any.at[:, pl.ds(start, own_len)], sem.at[3])
    o0.start()
    o1.start()
    ld[...] = logdet_part(s, own)
    tiles = t // TILE
    d_end = nt(s["skl"][:, own], s["dproj"][:, own])
    ones = jnp.ones((8, own_len), BF)
    ebias_row = nt(ones, s["dproj"][:, own])
    for q in range(tp):
        osend[high_half, slots[q], units : 2 * units, 0:C] = d_end[q * units : (q + 1) * units].astype(BF)
    s["h"][...] = jnp.zeros((HID, t), F32)

    def layer_body(i, carry):
        layer = LAYERS - 1 - i

        def tile(j, carry):
            cols = pl.ds(pl.multiple_of(j * TILE, TILE), TILE)
            mask = s["mask"][0:1, cols]
            carried = s["h"][:, cols] * mask
            s["h"][:, cols] = carried
            d_all = jnp.concatenate([s["dsk"][:, cols], carried.astype(BF)], axis=0)
            s["d"][:, cols] = d_all
            da = nn(w["rsb"][layer], d_all)
            tt = s["tt"][layer, :, cols].astype(F32)
            ss = s["ss"][layer, :, cols].astype(F32)
            das = da * ss
            s["dg"][0:HID, cols] = (das * (1.0 - tt * tt)).astype(BF)
            s["dg"][HID : 2 * HID, cols] = (das * tt * (1.0 - ss)).astype(BF)
            return carry

        lax.fori_loop(0, tiles, tile, 0)
        act = (s["tt"][layer, :, own].astype(F32) * s["ss"][layer, :, own].astype(F32)).astype(BF)
        d_rs = nt(act, s["d"][:, own])
        for q in range(tp):
            half = jnp.where(layer == LAYERS - 1, high_half, low_half)
            row = pl.multiple_of(lax.rem(layer, LAYERS - 1) * units, 16)
            osend[half, slots[q], pl.ds(row, units), :] = d_rs[q * units : (q + 1) * units].astype(BF)
        bias_row = nt(ones, s["dg"][:, own])
        smallg[pl.ds(layer, 1), 0 : 2 * HID] = bias_row[0:1]
        build_taps(lambda r: s["hb"][layer, r, :].astype(F32), s["x"], t, HID // 16, False)
        for lo in range(0, KER * HID, 256):
            hi = min(lo + 256, KER * HID)
            s["dw"][:, lo:hi] = nt(s["dg"][:, own], s["x"][lo:hi, own])
        if dp * 128 <= MAX_PACKED:
            for b in range(dp):
                p = bit_reverse(jnp.bitwise_xor(me_dp, meta[8 + b]), bits)
                gsend[p, layer, :, 0:rows] = s["dw"][:, b * rows : (b + 1) * rows].astype(BF)
        else:
            gsend[layer] = s["dw"][:, 0 : KER * HID].astype(BF)
        build_taps(lambda r: s["dg"][r, :].astype(F32), s["x"], t, 2 * HID // 16, True)

        def back(j, carry):
            cols = pl.ds(pl.multiple_of(j * TILE, TILE), TILE)
            s["h"][:, cols] += nn(w["wd"][layer], s["x"][:, cols])
            return carry

        lax.fori_loop(0, tiles, back, 0)
        return carry

    lax.fori_loop(0, LAYERS, layer_body, 0)
    d_pre = (s["h"][:, own] * s["mask"][0:1, own]).astype(BF)
    dpp_v = nn(w["pre"][...], d_pre).astype(BF)
    dpp[...] = dpp_v
    d_prew = nt(s["x0b"][:, own], d_pre)
    for q in range(tp):
        osend[high_half, slots[q], units : units + HALF, HID : 2 * HID] = d_prew.astype(BF)
    dm = s["dm"][:, own]
    dpp_f = dpp_v.astype(F32)
    fr = s["fr"][:, own]
    qd = nt(dm, fr)
    q0 = nt(dpp_v, fr)
    qd = jnp.concatenate([qd[0:HALF] + q0, qd[HALF:C]], axis=0)
    v = jnp.sum(dm.astype(F32), axis=1, keepdims=True)
    v0 = jnp.sum(dpp_f, axis=1, keepdims=True)
    v = jnp.concatenate([v[0:HALF] + v0, v[HALF:C]], axis=0)
    mixfull = w["mixfull"][...]
    es = w["consts"][0:1, :]
    bb = w["consts"][1:2, :]
    smallg[4:5, 0:C] = es * jnp.sum(mixfull * qd, axis=0, keepdims=True) + w["consts"][2:3, :]
    smallg[5:6, 0:C] = jnp.sum(mixfull * v, axis=0, keepdims=True)
    smallg[6:7, 0:C] = ebias_row[0:1]
    smallg[7:8, 0:C] = jnp.zeros((1, C), F32)
    d2 = (v * bb + es * qd) * w["same"][...]
    part = tn(w["onehot"][...], d2, PRECISE)
    smallg[8:16, 0:128] = nn(part, w["onehot"][...], PRECISE)[0:8] + w["extra"][...]
    small = smallg[...]
    for q in range(tp):
        for h in range(2):
            osend[high_half, slots[q], 3 * units - 16 : 3 * units, h * units : (h + 1) * units] = small[
                :, h * HID + q * units : h * HID + (q + 1) * units
            ].astype(BF)
        osend[high_half, slots[q], 3 * units - 12 : 3 * units, 0:C] = small[4:16, 0:C].astype(BF)
    o0.wait()
    o1.wait()


def fwd_kernel(own_len, t, names, snames, meta, *refs):
    n = len(names)
    w = dict(zip(names, refs[:n]))
    fr_any, og_any = refs[n : n + 2]
    fo_any, p1_any, ld = refs[n + 4 : n + 7]
    s = dict(zip(snames, refs[n + 7 : -1]))
    sem = refs[-1]
    w0 = pl.multiple_of(meta[0], 128)
    off = pl.multiple_of(meta[1], 128)
    start = pl.multiple_of(meta[2], 128)
    c0 = pltpu.make_async_copy(fr_any.at[:, pl.ds(w0, t)], s["fr"], sem.at[0])
    c1 = pltpu.make_async_copy(og_any.at[:, pl.ds(w0, t)], s["og"], sem.at[1])
    c0.start()
    c1.start()
    c0.wait()
    c1.wait()
    window_forward(False, t, w, s, w0)
    window_tail(False, t, w, s)
    own = pl.ds(off, own_len)
    o0 = pltpu.make_async_copy(s["fo"].at[:, own], fo_any.at[:, pl.ds(start, own_len)], sem.at[2])
    o1 = pltpu.make_async_copy(s["p1"].at[:, own], p1_any.at[:, pl.ds(start, own_len)], sem.at[3])
    o0.start()
    o1.start()
    ld[...] = logdet_part(s, own)
    o0.wait()
    o1.wait()


def fwd_weights_call(w):
    return [w[k] for k in FW]


def call_own(dp, tp, rows, frames, own_len, w, meta, fr, og):
    t = min(own_len + 2 * HALO, frames)
    names = FW + OW
    sc = fwd_scratch(t)
    sc.update(own_scratch(t))
    sc["x"] = pltpu.VMEM((2 * KER * HID, t), BF)
    snames = list(sc)
    units = HID // tp
    out_shape = (
        jax.ShapeDtypeStruct((C, frames), F32),
        jax.ShapeDtypeStruct((C, frames), F32),
        jax.ShapeDtypeStruct((8, 128), F32),
        jax.ShapeDtypeStruct((dp, LAYERS, 2 * HID, 128) if dp * 128 <= MAX_PACKED else (LAYERS, 2 * HID, KER * HID), BF),
        jax.ShapeDtypeStruct((2, tp, 3 * units, 2 * HID), BF),
        jax.ShapeDtypeStruct((HALF, own_len), BF),
    )
    return pl.pallas_call(
        functools.partial(own_kernel, dp, tp, rows, own_len, t, names, snames),
        out_shape=out_shape,
        in_specs=[sm()] + [vm()] * len(names) + [hb(), hb()],
        out_specs=(hb(), hb(), vm(), vm(), vm(), vm()),
        scratch_shapes=list(sc.values()) + [pltpu.SemaphoreType.DMA((4,))],
        compiler_params=pltpu.CompilerParams(vmem_limit_bytes=62 * 1024 * 1024),
        cost_estimate=pl.CostEstimate(flops=30 * 10**9, bytes_accessed=20 * 10**6, transcendentals=0),
        name="own",
    )(meta, *[w[k] for k in names], fr, og)


def call_fwd(frames, own_len, w, meta, fr, og, fo, p1):
    t = min(own_len + 2 * HALO, frames)
    sc = fwd_scratch(t)
    sc["x"] = pltpu.VMEM((KER * HID, t), BF)
    snames = list(sc)
    n = len(FW)
    return pl.pallas_call(
        functools.partial(fwd_kernel, own_len, t, FW, snames),
        out_shape=(
            jax.ShapeDtypeStruct((C, frames), F32),
            jax.ShapeDtypeStruct((C, frames), F32),
            jax.ShapeDtypeStruct((8, 128), F32),
        ),
        in_specs=[sm()] + [vm()] * n + [hb()] * 4,
        out_specs=(hb(), hb(), vm()),
        input_output_aliases={n + 3: 0, n + 4: 1},
        scratch_shapes=list(sc.values()) + [pltpu.SemaphoreType.DMA((4,))],
        compiler_params=pltpu.CompilerParams(vmem_limit_bytes=40 * 1024 * 1024),
        cost_estimate=pl.CostEstimate(flops=8 * 10**9, bytes_accessed=10 * 10**6, transcendentals=0),
        name="fwd",
    )(meta, *[w[k] for k in FW], fr, og, fo, p1)


def moments(moment, square, grad):
    new_moment = BETA * moment + (1.0 - BETA) * grad
    new_square = BETA * square + (1.0 - BETA) * grad * grad
    correction = 1.0 - BETA**STEP
    direction = new_moment / correction / (jnp.sqrt(new_square / correction) + EPSILON)
    return (new_moment, new_square, direction)


def adam_update(weight, moment, square, grad, rate):
    new_moment, new_square, direction = moments(moment, square, grad)
    return (weight - rate * (direction + DECAY * weight), new_moment, new_square)


def rotate_kernel(tp, *refs):
    basis = refs[:tp]
    part = refs[tp]
    outs = refs[tp + 1 :]
    for kk in range(tp):
        for layer in range(LAYERS):
            outs[kk][layer] = nn(basis[kk][layer], part[layer]).astype(BF)


def call_rotate(tp, basis, part):
    cols = basis[0].shape[1]
    return pl.pallas_call(
        functools.partial(rotate_kernel, tp),
        out_shape=[jax.ShapeDtypeStruct((LAYERS, cols, 128), BF)] * tp,
        in_specs=[vm()] * (tp + 1),
        out_specs=[vm()] * tp,
        cost_estimate=pl.CostEstimate(flops=3 * 10**8, bytes_accessed=10**6, transcendentals=0),
        name="rotate",
    )(*basis, part)


def moment_kernel(tp, rows, *refs):
    parts = refs[:tp]
    moment, square, new_moment, new_square, direction = refs[tp:]
    total = parts[0][...].astype(F32)
    for kk in range(1, tp):
        total = total + parts[kk][...].astype(F32)
    grad = total[:, :, 0:rows]
    m, v, d = moments(moment[...], square[...], grad)
    new_moment[...] = m
    new_square[...] = v
    direction[:, :, 0:rows] = d.astype(BF)
    if rows < 128:
        direction[:, :, rows:128] = jnp.zeros(d.shape[:2] + (128 - rows,), BF)


def call_moments(tp, rows, parts, moment, square):
    shape = moment.shape
    return pl.pallas_call(
        functools.partial(moment_kernel, tp, rows),
        out_shape=[
            jax.ShapeDtypeStruct(shape, F32),
            jax.ShapeDtypeStruct(shape, F32),
            jax.ShapeDtypeStruct(shape[:2] + (128,), BF),
        ],
        in_specs=[vm()] * (tp + 2),
        out_specs=[vm()] * 3,
        name="moments",
    )(*parts, moment, square)


def back_kernel(tp, rows, meta, *refs):
    basis = refs[:tp]
    directions = refs[tp : 2 * tp]
    weight, out, scratch = refs[2 * tp :]
    units = HID // tp
    me_tp = meta[4]
    for layer in range(LAYERS):
        total = tn(basis[0][layer], directions[0][layer])
        for kk in range(1, tp):
            total = total + tn(basis[kk][layer], directions[kk][layer])
        scratch[layer] = total
    for layer in range(LAYERS):
        for h in range(2):
            row = pl.ds(pl.multiple_of(h * HID + me_tp * units, 16), units)
            back = scratch[layer, row, 0:rows]
            here = slice(h * units, (h + 1) * units)
            value = weight[layer, here, :]
            out[layer, here, :] = value - RATE_CONV * (back + DECAY * value)


def call_back(tp, rows, meta, basis, directions, weight):
    return pl.pallas_call(
        functools.partial(back_kernel, tp, rows),
        out_shape=jax.ShapeDtypeStruct(weight.shape, F32),
        in_specs=[sm()] + [vm()] * (2 * tp + 1),
        out_specs=vm(),
        scratch_shapes=[pltpu.VMEM((LAYERS, 2 * HID, 128), F32)],
        cost_estimate=pl.CostEstimate(flops=3 * 10**8, bytes_accessed=10**6, transcendentals=0),
        name="back",
    )(meta, *basis, *directions, weight)


def small_kernel(tp, meta, *refs):
    lows, highs = refs[0], refs[1]
    ins = refs[2:20]
    outs = refs[20:]
    units = HID // tp
    core = jnp.bitwise_and(meta[3], 1)

    def put(i, grad, rate, index=None):
        if index is None:
            new = adam_update(ins[3 * i][...], ins[3 * i + 1][...], ins[3 * i + 2][...], grad, rate)
            for k in range(3):
                outs[3 * i + k][...] = new[k]
        else:
            new = adam_update(ins[3 * i][index], ins[3 * i + 1][index], ins[3 * i + 2][index], grad, rate)
            for k in range(3):
                outs[3 * i + k][index] = new[k]

    def rows(half, lo, size, c0, c1):
        a = lows[lo : lo + size, c0:c1].astype(F32)
        b = highs[lo : lo + size, c0:c1].astype(F32)
        return jnp.where(core == half, a, b)

    tail = rows(1, 3 * units - 16, 16, 0, 2 * HID)
    put(0, tail[4:7, 0:C], RATE_SMALL)
    put(1, tail[8:12, 0:4], RATE_MIX)
    put(2, rows(1, units, HALF, HID, 2 * HID), RATE_PRE)
    for h in range(2):
        put(3, tail[0:LAYERS, h * units : (h + 1) * units], RATE_BIAS, (slice(None), h, slice(None)))
    for layer in range(LAYERS):
        half = 1 if layer == LAYERS - 1 else 0
        lo = 0 if layer == LAYERS - 1 else layer * units
        put(4, rows(half, lo, units, 0, HID), RATE_RESSKIP, LAYERS - 1 + layer)
        if layer < LAYERS - 1:
            put(4, rows(half, lo, units, HID, 2 * HID), RATE_RESSKIP, layer)
    put(5, rows(1, units, units, 0, C), RATE_END)


def call_small(tp, meta, low, high, ins):
    return pl.pallas_call(
        functools.partial(small_kernel, tp),
        out_shape=[jax.ShapeDtypeStruct(x.shape, F32) for x in ins],
        in_specs=[sm()] + [vm()] * (2 + len(ins)),
        out_specs=[vm()] * len(ins),
        name="smallupd",
    )(meta, low, high, *ins)


def grad_kernel(meta, a_half, dpp, p1, out):
    out[...] = p1[...] + nn(a_half[...], dpp[...])


def call_grad(own_len, frames, quarter, a_half, dpp, p1):
    return pl.pallas_call(
        grad_kernel,
        out_shape=jax.ShapeDtypeStruct(p1.shape, F32),
        grid_spec=pltpu.PrefetchScalarGridSpec(
            num_scalar_prefetch=1,
            grid=(1,),
            in_specs=[
                pl.BlockSpec(a_half.shape, lambda i, q: (0, 0)),
                pl.BlockSpec(dpp.shape, lambda i, q: (0, 0)),
                pl.BlockSpec((C, own_len), lambda i, q: (0, q[0])),
            ],
            out_specs=pl.BlockSpec((C, own_len), lambda i, q: (0, q[0])),
        ),
        input_output_aliases={3: 0},
        cost_estimate=pl.CostEstimate(flops=10**8, bytes_accessed=3 * 10**6, transcendentals=0),
        name="fgrad",
    )(quarter, a_half, dpp, p1)


def call_prep(dp, tp, rows, meta, pieces, res_pieces, end_pieces):
    return pl.pallas_call(
        functools.partial(prep_kernel, dp, tp, rows),
        out_shape=[
            jax.ShapeDtypeStruct((LAYERS, 2 * HID, KER * HID), BF),
            jax.ShapeDtypeStruct((LAYERS, HID, 2 * KER * HID), BF),
            jax.ShapeDtypeStruct((LAYERS, 2 * HID, HID), BF),
            jax.ShapeDtypeStruct((LAYERS, HID, 2 * HID), BF),
            jax.ShapeDtypeStruct((HID, C), BF),
            jax.ShapeDtypeStruct((C, HID), BF),
        ],
        in_specs=[sm()] + [hb()] * len(pieces) + [vm()] * (2 * tp),
        out_specs=[vm()] * 6,
        scratch_shapes=[
            pltpu.VMEM((len(pieces),) + pieces[0].shape, BF),
            pltpu.SemaphoreType.DMA((len(pieces),)),
        ],
        compiler_params=pltpu.CompilerParams(vmem_limit_bytes=50 * 1024 * 1024),
        cost_estimate=pl.CostEstimate(flops=10**8, bytes_accessed=12 * 10**6, transcendentals=0),
        name="prep",
    )(meta, *pieces, *res_pieces, *end_pieces)


def minor_det(pair_rows, column_left, column_right):
    return (
        pair_rows[0, column_left] * pair_rows[1, column_right]
        - pair_rows[1, column_left] * pair_rows[0, column_right]
    )


def determinant(matrix):
    upper_rows = matrix[:2]
    lower_rows = matrix[2:]
    return (
        minor_det(upper_rows, 0, 1) * minor_det(lower_rows, 2, 3)
        - minor_det(upper_rows, 0, 2) * minor_det(lower_rows, 1, 3)
        + minor_det(upper_rows, 0, 3) * minor_det(lower_rows, 1, 2)
        + minor_det(upper_rows, 1, 2) * minor_det(lower_rows, 0, 3)
        - minor_det(upper_rows, 1, 3) * minor_det(lower_rows, 0, 2)
        + minor_det(upper_rows, 2, 3) * minor_det(lower_rows, 0, 1)
    )


def local(
    frames_in,
    out_grad,
    logdet_grad,
    lengths,
    offsets,
    owners,
    small_params,
    small_moment,
    small_square,
    mix,
    mix_moment,
    mix_square,
    pre_weight,
    pre_moment,
    pre_square,
    conv_weight,
    conv_moment,
    conv_square,
    conv_basis,
    conv_bias,
    conv_bias_moment,
    conv_bias_square,
    res_skip,
    res_skip_moment,
    res_skip_square,
    end_weight,
    end_moment,
    end_square,
):
    dp = lax.axis_size("dp")
    tp = lax.axis_size("tp")
    me_dp = lax.axis_index("dp")
    me_tp = lax.axis_index("tp")
    frames = frames_in.shape[0]
    rows = conv_weight.shape[1]
    units = conv_weight.shape[3]
    own_len = frames // tp
    t = min(own_len + 2 * HALO, frames)

    def shift_tp(x, kk):
        return lax.ppermute(x, "tp", [(i, (i + kk) % tp) for i in range(tp)])

    def swap_dp(x, mask):
        return lax.ppermute(x, "dp", [(i, i ^ mask) for i in range(dp)])

    def gather_tp(x):
        return [x] + [shift_tp(x, kk) for kk in range(1, tp)]

    shard = jnp.transpose(conv_weight, (0, 2, 3, 1)).reshape(LAYERS, 2 * units, rows).astype(BF)
    shard = jnp.pad(shard, ((0, 0), (0, 0), (0, 128 - rows)))
    column = jnp.stack(gather_tp(shard))
    pieces = {0: column}
    for m in range(2, dp, 2):
        pieces[m] = swap_dp(column, m)
    for m in range(0, dp, 2):
        pieces[m + 1] = swap_dp(pieces[m], 1)
    res_pieces = gather_tp(res_skip.astype(BF))
    end_pieces = gather_tp(end_weight.astype(BF))
    basis_t = jnp.transpose(conv_basis.reshape(LAYERS, 2 * HID, -1), (0, 2, 1)).astype(BF)
    basis_pieces = gather_tp(basis_t)
    prep_meta = jnp.concatenate([jnp.stack([me_tp, me_dp]).astype(jnp.int32), owners])
    pieces = [pieces[m] for m in range(dp)]
    packed = dp * 128 <= MAX_PACKED
    if not packed:
        slot = jnp.bitwise_xor(me_dp, owners)
        column_of = lax.rem(me_tp - jnp.arange(tp) + tp, tp)
        stacked = jnp.stack(pieces)[slot][:, column_of]
        stacked = stacked.reshape(dp, tp, LAYERS, 2, units, 128)[..., :rows]
        pieces = [jnp.transpose(stacked, (2, 3, 1, 4, 0, 5)).reshape(LAYERS, 2 * HID, KER * HID)]
    wt, wd, rsf, rsb, end, end_t = call_prep(dp, tp, rows, prep_meta, pieces, res_pieces, end_pieces)
    bias_all = jnp.stack(gather_tp(conv_bias))
    order = lax.rem(me_tp - jnp.arange(tp) + tp, tp)
    bias_all = jnp.transpose(bias_all[order], (1, 2, 0, 3)).reshape(LAYERS, 2 * HID, 1)

    one_hot = jnp.asarray(ONE_HOT)
    same = jnp.asarray(SAME)
    es = jnp.exp(small_params[0])
    mixfull = jnp.dot(jnp.dot(one_hot, mix, precision=PRECISE), one_hot.T, precision=PRECISE) * same
    at = mixfull * es[None, :]
    a_hi = at.astype(BF)
    a_lo = (at - a_hi.astype(F32)).astype(BF)
    cvec = jnp.sum(mixfull * small_params[1][None, :], axis=1, keepdims=True)
    first = (me_tp == 0).astype(F32)
    lg_sum = jnp.sum(logdet_grad)
    constant_ld, mix_pull = jax.value_and_grad(lambda m: jnp.log(determinant(m)))(mix)
    constant_ld = jnp.sum(small_params[0]) + C // 4 * constant_ld
    extra = jnp.pad(first * lg_sum * (C // 4) * mix_pull, ((0, 4), (0, 124)))
    consts = jnp.concatenate(
        [es[None], small_params[1:2], jnp.broadcast_to(first * lg_sum, (1, C)), jnp.zeros((5, C), F32)]
    )
    at_b = at.T.astype(BF)
    w = {
        "wt": wt,
        "rsf": rsf,
        "bias": bias_all,
        "a_hi": a_hi,
        "a_lo": a_lo,
        "at_hi": at_b,
        "cvec": cvec,
        "pre_t": pre_weight.T.astype(BF),
        "end_t": end_t,
        "ebias": small_params[2][:, None],
        "off": offsets[:, None],
        "end_frame": (offsets + lengths)[:, None],
        "fw": (logdet_grad / lengths.astype(F32))[:, None],
        "wd": wd,
        "rsb": rsb,
        "end": end,
        "pre": pre_weight.astype(BF),
        "mixfull": mixfull,
        "consts": consts,
        "onehot": jnp.pad(one_hot, ((0, 0), (0, 124))),
        "same": same,
        "extra": extra,
    }
    fr = frames_in.T
    og = out_grad.T

    def meta_of(q):
        start = q * own_len
        w0 = jnp.clip(start - HALO, 0, frames - t)
        head = jnp.stack([w0, start - w0, start, me_dp, me_tp, q, q, q]).astype(jnp.int32)
        return jnp.concatenate([head, owners])

    meta = meta_of(me_tp)
    fo, p1, ld, gsend, osend, dpp = call_own(dp, tp, rows, frames, own_len, w, meta, fr, og)
    lds = [ld]

    if not packed:
        place = jnp.bitwise_xor(me_dp, bit_reverse(jnp.arange(dp), (dp - 1).bit_length()))
        block = jnp.argsort(owners)[place]
        gsend = jnp.transpose(gsend.reshape(LAYERS, 2 * HID, dp, rows), (2, 0, 1, 3))[block]
        gsend = jnp.pad(gsend, ((0, 0), (0, 0), (0, 0), (0, 128 - rows)))
    buf = gsend
    bit = 0
    while buf.shape[0] > 1:
        half = buf.shape[0] // 2
        got = swap_dp(buf[half:], 1 << bit)
        buf = (buf[:half].astype(F32) + got.astype(F32)).astype(BF)
        bit += 1
    turned = call_rotate(tp, basis_pieces, buf[0])
    parts = [turned[0]] + [
        lax.ppermute(turned[kk], "tp", [(i, (i - kk) % tp) for i in range(tp)]) for kk in range(1, tp)
    ]
    conv_m, conv_v, direction = call_moments(
        tp,
        rows,
        parts,
        jnp.transpose(conv_moment, (0, 2, 1)),
        jnp.transpose(conv_square, (0, 2, 1)),
    )
    directions = gather_tp(direction)
    cw = jnp.transpose(conv_weight, (0, 2, 3, 1)).reshape(LAYERS, 2 * units, rows)
    conv_new = call_back(tp, rows, meta, basis_pieces, directions, cw)

    got = swap_dp(osend[1], 1)
    obuf = (osend[0].astype(F32) + got.astype(F32)).astype(BF)
    arrived = [obuf[0]] + [
        lax.ppermute(obuf[kk], "tp", [(i, (i + kk) % tp) for i in range(tp)]) for kk in range(1, tp)
    ]
    arrived = [x.astype(F32) for x in arrived]
    while len(arrived) > 1:
        mid = len(arrived) // 2
        arrived = [arrived[i] + arrived[i + mid] for i in range(mid)]
    total = arrived[0].astype(BF)
    for bit in range(1, (dp - 1).bit_length()):
        total = (total.astype(F32) + swap_dp(total, 1 << bit).astype(F32)).astype(BF)
    other = swap_dp(total, 1)
    updated = call_small(
        tp,
        meta,
        total,
        other,
        [
            small_params, small_moment, small_square,
            mix, mix_moment, mix_square,
            pre_weight, pre_moment, pre_square,
            conv_bias, conv_bias_moment, conv_bias_square,
            res_skip, res_skip_moment, res_skip_square,
            end_weight, end_moment, end_square,
        ],
    )

    for kk in range(1, tp):
        q = lax.rem(me_tp + tp - kk, tp)
        fo, p1, ld = call_fwd(frames, own_len, w, meta_of(q), fr, og, fo, p1)
        lds.append(ld)
    dpps = gather_tp(dpp)
    a_half = at_b[:, :HALF]
    for kk in range(tp):
        q = lax.rem(me_tp + tp - kk, tp)
        p1 = call_grad(own_len, frames, q[None].astype(jnp.int32), a_half, dpps[kk], p1)
    frame_sums = sum(x[:, 0] for x in lds)
    logdet = constant_ld + frame_sums / lengths.astype(F32)

    def conv_out(x):
        return jnp.transpose(x.reshape(LAYERS, 2, units, rows), (0, 3, 1, 2))

    (small_new, small_m, small_v, mix_new, mix_m, mix_v, pre_new, pre_m, pre_v, bias_new, bias_m, bias_v,
     rs_new, rs_m, rs_v, end_new, end_m, end_v) = updated
    return (
        fo.T,
        logdet,
        p1.T,
        small_new,
        small_m,
        small_v,
        mix_new,
        mix_m,
        mix_v,
        pre_new,
        pre_m,
        pre_v,
        conv_out(conv_new),
        jnp.transpose(conv_m, (0, 2, 1)),
        jnp.transpose(conv_v, (0, 2, 1)),
        bias_new,
        bias_m,
        bias_v,
        rs_new,
        rs_m,
        rs_v,
        end_new,
        end_m,
        end_v,
    )


def solution(mesh):
    return jax.shard_map(
        local,
        mesh=mesh,
        in_specs=(
            P("dp", None),
            P("dp", None),
            P("dp"),
            P("dp"),
            P("dp"),
            P(),
            P(),
            P(),
            P(),
            P(),
            P(),
            P(),
            P(),
            P(),
            P(),
            P(None, "dp", None, "tp"),
            P(None, "dp", "tp"),
            P(None, "dp", "tp"),
            P(None, None, None, "tp"),
            P(None, None, "tp"),
            P(None, None, "tp"),
            P(None, None, "tp"),
            P(None, "tp", None),
            P(None, "tp", None),
            P(None, "tp", None),
            P("tp", None),
            P("tp", None),
            P("tp", None),
        ),
        out_specs=(
            P("dp", None),
            P("dp"),
            P("dp", None),
            P(),
            P(),
            P(),
            P(),
            P(),
            P(),
            P(),
            P(),
            P(),
            P(None, "dp", None, "tp"),
            P(None, "dp", "tp"),
            P(None, "dp", "tp"),
            P(None, None, "tp"),
            P(None, None, "tp"),
            P(None, None, "tp"),
            P(None, "tp", None),
            P(None, "tp", None),
            P(None, "tp", None),
            P("tp", None),
            P("tp", None),
            P("tp", None),
        ),
        check_vma=False,
    )
```

```python
import functools
import jax
import jax.numpy as jnp
import numpy as np
from jax import lax
from jax.experimental import pallas as pl
from jax.experimental.pallas import tpu as pltpu
from jax.sharding import PartitionSpec as P

C = 160
HALF = 80
HID = 192
KER = 5
LAYERS = 4
STEP = 5
HALO = 128
MAX_PACKED = 1024
VMEM_BYTES = 62 * 1024 * 1024

BETA = 0.5
EPSILON = 1e-08
DECAY = 0.01
RATE_SMALL = 0.1
RATE_MIX = 0.3
RATE_PRE = 0.1
RATE_CONV = 0.03
RATE_BIAS = 0.3
RATE_RESSKIP = 0.07
RATE_END = 0.04
PRECISE = lax.Precision.HIGHEST
BF = jnp.bfloat16
F32 = jnp.float32

CH = np.arange(C)
PAIR = 2 * (CH // HALF) + CH % 2
GROUP = (CH % HALF) // 2
ONE_HOT = (PAIR[:, None] == np.arange(4)[None, :]).astype(np.float32)
SAME = (GROUP[:, None] == GROUP[None, :]).astype(np.float32)


def nn(a, b, precision=None):
    return lax.dot_general(a, b, (((1,), (0,)), ((), ())), precision=precision, preferred_element_type=F32)


def nt(a, b, precision=None):
    return lax.dot_general(a, b, (((1,), (1,)), ((), ())), precision=precision, preferred_element_type=F32)


def tn(a, b, precision=None):
    return lax.dot_general(a, b, (((0,), (0,)), ((), ())), precision=precision, preferred_element_type=F32)


def sigmoid(x):
    return 0.5 * jnp.tanh(0.5 * x) + 0.5


def vm():
    return pl.BlockSpec(memory_space=pltpu.VMEM)


def sm():
    return pl.BlockSpec(memory_space=pltpu.SMEM)


def hb():
    return pl.BlockSpec(memory_space=pl.ANY)


def bit_reverse(value, bits):
    out = value * 0
    for i in range(bits):
        out = out | (((value >> i) & 1) << (bits - 1 - i))
    return out


def axis(name):
    return lax.axis_index(name)


def from_left(me, kk, n):
    return lax.rem(me - kk + n, n)


def column(scalars, dtype, rows=8):
    index = lax.broadcasted_iota(jnp.int32, (rows, 1), 0)
    out = jnp.zeros((rows, 1), dtype)
    for u in range(rows):
        out = jnp.where(index == u, scalars[u], out)
    return out


def to_column(row):
    n = row.shape[1]
    eye = lax.broadcasted_iota(jnp.int32, (n, n), 0) == lax.broadcasted_iota(jnp.int32, (n, n), 1)
    return jnp.sum(jnp.where(eye, jnp.broadcast_to(row, (n, n)), 0.0), axis=1, keepdims=True)


def pack_kernel(rows, units, conv, res, end, bias, basis, conv_a, conv_b, res_out, basis_out, full):
    zero = jnp.zeros((2 * units, 128 - rows), BF)
    for layer in range(LAYERS):
        dst = conv_a if layer < 2 else conv_b
        dst[layer % 2, :, 0:rows] = conv[layer].astype(BF)
        dst[layer % 2, :, rows:128] = zero
    core = jnp.bitwise_and(axis("dp"), 1)
    for layer in range(LAYERS):
        full[layer, :, 0:HID] = res[LAYERS - 1 + layer].astype(BF)
        if layer < LAYERS - 1:
            full[layer, :, HID : 2 * HID] = res[layer].astype(BF)
    full[LAYERS - 1, :, HID : HID + C] = end[...].astype(BF)
    flat = jnp.concatenate([bias[layer] for layer in range(LAYERS)], axis=0).T
    hi = flat.astype(BF)
    lo = (flat - hi.astype(F32)).astype(BF)
    full[LAYERS - 1, :, HID + C : 2 * HID] = jnp.concatenate(
        [hi, lo, jnp.zeros((units, HID - C - 16), BF)], axis=1
    )
    res_out[...] = full[pl.ds(2 * core, 2)]
    for layer in range(LAYERS):
        basis_out[layer] = basis[layer].T.astype(BF)


def call_pack(rows, units, conv, res, end, bias, basis):
    return pl.pallas_call(
        functools.partial(pack_kernel, rows, units),
        out_shape=[
            jax.ShapeDtypeStruct((2, 2 * units, 128), BF),
            jax.ShapeDtypeStruct((2, 2 * units, 128), BF),
            jax.ShapeDtypeStruct((2, units, 2 * HID), BF),
            jax.ShapeDtypeStruct((LAYERS, basis.shape[2], 2 * HID), BF),
        ],
        in_specs=[vm()] * 5,
        out_specs=[vm()] * 4,
        scratch_shapes=[pltpu.VMEM((LAYERS, units, 2 * HID), BF)],
        name="pack",
    )(conv, res, end, bias, basis)


def minor_det(m, r, left, right):
    return m[r, left] * m[r + 1, right] - m[r + 1, left] * m[r, right]


def consts_kernel(mix, lg, small, pre, a_hi, a_lo, at_b, cvec, pre_t, pre_b, ebias, mixfull, rows_out, extra):
    m = [[mix[i, j] for j in range(4)] for i in range(4)]
    ch_r = lax.broadcasted_iota(jnp.int32, (C, 1), 0)
    ch_c = lax.broadcasted_iota(jnp.int32, (1, C), 1)

    def pair(ch):
        return 2 * (ch >= HALF).astype(jnp.int32) + jnp.bitwise_and(ch, 1)

    def group(ch):
        return lax.shift_right_logical(ch - jnp.where(ch >= HALF, HALF, 0), 1)

    same = group(ch_r) == group(ch_c)
    pr, pc = pair(ch_r), pair(ch_c)
    full = jnp.zeros((C, C), F32)
    turned = jnp.zeros((C, C), F32)
    for p in range(4):
        row = jnp.zeros((1, C), F32)
        row_t = jnp.zeros((1, C), F32)
        for q in range(4):
            row = jnp.where(pc == q, m[p][q], row)
            row_t = jnp.where(pc == q, m[q][p], row_t)
        full = jnp.where(pr == p, row, full)
        turned = jnp.where(pr == p, row_t, turned)
    full = jnp.where(same, full, 0.0)
    turned = jnp.where(same, turned, 0.0)
    es = jnp.exp(small[0:1, :])
    at = full * es
    hi = at.astype(BF)
    a_hi[...] = hi
    a_lo[...] = (at - hi.astype(F32)).astype(BF)
    at_b[...] = (turned * to_column(es)).astype(BF)
    cvec[...] = jnp.sum(full * small[1:2, :], axis=1, keepdims=True)
    mixfull[...] = full
    pre_t[...] = pre[...].T.astype(BF)
    pre_b[...] = pre[...].astype(BF)
    ebias[...] = to_column(small[2:3, :])
    pairs = [(0, 1), (0, 2), (0, 3), (1, 2), (1, 3), (2, 3)]
    up = {ab: m[0][ab[0]] * m[1][ab[1]] - m[1][ab[0]] * m[0][ab[1]] for ab in pairs}
    dn = {ab: m[2][ab[0]] * m[3][ab[1]] - m[3][ab[0]] * m[2][ab[1]] for ab in pairs}
    det = (
        up[0, 1] * dn[2, 3]
        - up[0, 2] * dn[1, 3]
        + up[0, 3] * dn[1, 2]
        + up[1, 2] * dn[0, 3]
        - up[1, 3] * dn[0, 2]
        + up[2, 3] * dn[0, 1]
    )

    def minor3(i, j):
        cols = [c for c in range(4) if c != j]
        two = dn if i < 2 else up
        other = m[1 - i] if i < 2 else m[5 - i]
        return (
            other[cols[0]] * two[cols[1], cols[2]]
            - other[cols[1]] * two[cols[0], cols[2]]
            + other[cols[2]] * two[cols[0], cols[1]]
        )

    total = lg[0]
    for u in range(1, lg.shape[0]):
        total = total + lg[u]
    first = jnp.where(axis("tp") == 0, total, 0.0)
    det_v = jnp.full((8, 128), det, F32)
    r = lax.broadcasted_iota(jnp.int32, (8, 128), 0)
    c = lax.broadcasted_iota(jnp.int32, (8, 128), 1)
    cof = jnp.zeros((8, 128), F32)
    for i in range(4):
        for j in range(4):
            sign = 1.0 if (i + j) % 2 == 0 else -1.0
            cof = jnp.where(jnp.logical_and(r == i, c == j), sign * minor3(i, j), cof)
    extra[0:8, :] = first * (C // 4) * cof / det_v
    gain = jnp.sum(small[0:1, :], axis=1, keepdims=True)
    extra[8:16, :] = gain + (C // 4) * jnp.log(det_v)
    rows_out[...] = jnp.concatenate(
        [es, small[1:2, :], jnp.full((1, C), first, F32), jnp.zeros((5, C), F32)], axis=0
    )


def call_consts(mix, lg, small, pre):
    return pl.pallas_call(
        consts_kernel,
        out_shape=[
            jax.ShapeDtypeStruct((C, C), BF),
            jax.ShapeDtypeStruct((C, C), BF),
            jax.ShapeDtypeStruct((C, C), BF),
            jax.ShapeDtypeStruct((C, 1), F32),
            jax.ShapeDtypeStruct((HID, HALF), BF),
            jax.ShapeDtypeStruct((HALF, HID), BF),
            jax.ShapeDtypeStruct((C, 1), F32),
            jax.ShapeDtypeStruct((C, C), F32),
            jax.ShapeDtypeStruct((8, C), F32),
            jax.ShapeDtypeStruct((16, 128), F32),
        ],
        in_specs=[sm(), sm(), vm(), vm()],
        out_specs=[vm()] * 10,
        name="consts",
    )(mix, lg, small, pre)


def tap_stack(wide, size, reverse):
    half = KER // 2
    parts = []
    for k in range(KER):
        shift = half - k if not reverse else k - half
        moved = wide if shift == 0 else pltpu.roll(wide, shift % wide.shape[1], 1)
        parts.append(moved[:, 128 : 128 + size])
    return jnp.concatenate(parts, axis=0)


def make_masks(s, scal, t, w0):
    off, length, lg = scal
    o = column(off, jnp.int32)
    n = column(length, jnp.int32)
    pos = lax.broadcasted_iota(jnp.int32, (8, t), 1) + w0
    member = jnp.logical_and(pos >= o, pos < o + n).astype(F32)
    s["member"][...] = member
    s["mask"][...] = jnp.broadcast_to(jnp.sum(member, axis=0, keepdims=True), (8, t))
    return column(lg, F32) / n.astype(F32)


def zero_edges(ref, lead, t):
    for slot in lead:
        at = ref if slot is None else ref.at[slot]
        z = jnp.zeros((at.shape[0], 128), BF)
        at[:, 0:128] = z
        at[:, t + 128 : t + 256] = z


def mixed_of(w, fr, mask):
    return (nn(w["a_hi"][...], fr) + nn(w["a_lo"][...], fr) + w["cvec"][...]) * mask


def unpack_conv(tp, rows, owners, dp, scratch, wt):
    me_tp, me_dp = axis("tp"), axis("dp")
    units = HID // tp

    def layer_body(layer, carry):
        for b in range(dp):
            m = jnp.bitwise_xor(me_dp, owners[b])
            for kk in range(tp):
                src = from_left(me_tp, kk, tp)
                for h in range(2):
                    row = pl.ds(pl.multiple_of(src * units + h * HID, 16), units)
                    wt[layer, row, b * rows : (b + 1) * rows] = scratch[
                        m, kk, layer, h * units : (h + 1) * units, 0:rows
                    ]
        return carry

    lax.fori_loop(0, 2, layer_body, 0)


def unpack_res(tp, res_pieces, rsb, rsf, end, end_t, bias, scr):
    me_tp = axis("tp")
    core = jnp.bitwise_and(axis("dp"), 1)
    units = HID // tp
    for kk in range(tp):
        for i in range(2):
            scr[kk, 2 * core + i] = res_pieces[kk][i]
            scr[kk, 2 * (1 - core) + i] = res_pieces[tp][kk, i]
    res_pieces = [scr.at[kk] for kk in range(tp)]
    for kk in range(tp):
        src = from_left(me_tp, kk, tp)
        row = pl.ds(pl.multiple_of(src * units, 16), units)
        for layer in range(LAYERS - 1):
            rsb[layer, row, :] = res_pieces[kk][layer]
        last = res_pieces[kk][LAYERS - 1]
        rsb[LAYERS - 1, row, 0:HID] = last[:, 0:HID]
        rsb[LAYERS - 1, row, HID : 2 * HID] = jnp.zeros((units, HID), BF)
        end[row, :] = last[:, HID : HID + C]
        tail = last[:, HID + C : 2 * HID].astype(F32)
        for layer in range(LAYERS):
            for h in range(2):
                i = layer * 2 + h
                at = pl.ds(pl.multiple_of(src * units + h * HID, 16), units)
                bias[layer, at, :] = tail[:, i : i + 1] + tail[:, 8 + i : 9 + i]
    for layer in range(LAYERS):
        rsf[layer, 0:HID, :] = rsb[layer, :, HID : 2 * HID].astype(F32).T.astype(BF)
        rsf[layer, HID : 2 * HID, :] = rsb[layer, :, 0:HID].astype(F32).T.astype(BF)
    end_t[...] = end[...].astype(F32).T.astype(BF)


def forward_layer(s, t, wt, rsf, bias, mask, here, after, save):
    g = nn(wt, tap_stack(s["hb"][here], t, False)) + bias
    tt = jnp.tanh(g[0:HID])
    ss = sigmoid(g[HID : 2 * HID])
    act = (tt * ss).astype(BF)
    y = nn(rsf, act)
    s["skip"][...] += y[HID : 2 * HID]
    hv = (s["h"][...] + y[0:HID]) * mask
    s["h"][...] = hv
    if save is not None:
        s["tt"][save] = tt.astype(BF)
        s["ss"][save] = ss.astype(BF)
    s["hb"][after, :, 128 : t + 128] = hv.astype(BF)


def start_hidden(s, t, w, mixed, mask):
    hv = nn(w["pre_t"][...], mixed[0:HALF].astype(BF)) * mask
    s["h"][...] = hv
    s["hb"][0, :, 128 : t + 128] = hv.astype(BF)
    s["skip"][...] = jnp.zeros((HID, t), F32)


def window_tail(own, t, w, s, mixed, mask, weight, dpp=None):
    skip_low = (s["skip"][...] * mask).astype(BF)
    proj = nn(w["end_t"][...], skip_low) + w["ebias"][...]
    shift = proj[0:HALF]
    log_scale = proj[HALF:C]
    e = jnp.exp(log_scale)
    x0 = mixed[0:HALF]
    x1 = mixed[HALF:C]
    s["fo"][0:HALF, :] = x0
    s["fo"][HALF:C, :] = (shift + e * x1) * mask
    s["pf"][...] = jnp.broadcast_to(jnp.sum(log_scale, axis=0, keepdims=True), (8, t))
    og = s["og"][...].astype(F32)
    d_shift = og[HALF:C] * mask
    de = d_shift * e
    first = og[0:HALF] * mask
    if not own and dpp is not None:
        first = first + dpp
    dm = jnp.concatenate([first, de], axis=0).astype(BF)
    if not own:
        s["p1"][...] = nn(w["at_b"][...], dm)
    if own:
        s["dm"][...] = dm
        s["x0b"][...] = x0.astype(BF)
        fw = jnp.sum(s["member"][...] * weight, axis=0, keepdims=True)
        d_log = de * x1 + fw
        d_proj = jnp.concatenate([d_shift, d_log], axis=0).astype(BF)
        s["dproj"][...] = d_proj
        s["skl"][...] = skip_low
        s["dsk"][...] = (nn(w["end"][...], d_proj) * mask).astype(BF)


def logdet_part(s, own):
    part = jnp.sum(s["member"][:, own] * s["pf"][:, own], axis=1, keepdims=True)
    return jnp.broadcast_to(part, (8, 128))


def backward_layer(s, t, layer, slot, own, own_in, own_len, wt, rsb, mask, ones, put_rs, put_conv):
    carried = s["h"][...] * mask
    s["h"][...] = carried
    s["d"][0:HID, :] = s["dsk"][...]
    s["d"][HID : 2 * HID, :] = carried.astype(BF)
    da = nn(rsb[layer], s["d"][...])
    tt = s["tt"][slot].astype(F32)
    ss = s["ss"][slot].astype(F32)
    das = da * ss
    s["dg"][0:HID, 128 : t + 128] = (das * (1.0 - tt * tt)).astype(BF)
    s["dg"][HID : 2 * HID, 128 : t + 128] = (das * tt * (1.0 - ss)).astype(BF)
    act = (s["tt"][slot, :, own].astype(F32) * s["ss"][slot, :, own].astype(F32)).astype(BF)
    put_rs(layer, nt(act, s["d"][:, own]))
    s["smallg"][pl.ds(layer, 1), :] = nt(ones, s["dg"][:, own_in])[0:1]
    wide = s["hb"][slot, :, pl.ds(pl.multiple_of(own_in.start - 128, 128), own_len + 256)]
    s["dw"][:, 0 : KER * HID] = nt(s["dg"][:, own_in], tap_stack(wide, own_len, False))
    put_conv(slot)
    for k in range(KER):
        s["wd"][:, k * 2 * HID : (k + 1) * 2 * HID] = (
            wt[slot, :, k * HID : (k + 1) * HID].astype(F32).T.astype(BF)
        )
    s["h"][...] += nn(s["wd"][...], tap_stack(s["dg"][...], t, True))


def rs_writer(tp, osend, units):
    me_tp, me_dp = axis("tp"), axis("dp")
    core = jnp.bitwise_and(me_dp, 1)
    slots = [from_left(q, 0, tp) if False else lax.rem(q - me_tp + tp, tp) for q in range(tp)]

    def put(layer, value):
        half = jnp.where(layer == LAYERS - 1, 1 - core, core)
        row = pl.multiple_of(lax.rem(layer, LAYERS - 1) * units, 16)
        for q in range(tp):
            osend[half, slots[q], pl.ds(row, units), :] = value[q * units : (q + 1) * units].astype(BF)

    return put, slots, 1 - core


def conv_writer(dp, rows, owners, gsend, dw):
    me_dp = axis("dp")
    bits = (dp - 1).bit_length()

    def put(slot):
        if dp * 128 <= MAX_PACKED:
            for b in range(dp):
                p = bit_reverse(jnp.bitwise_xor(me_dp, owners[b]), bits)
                gsend[p, slot, :, 0:rows] = dw[:, b * rows : (b + 1) * rows].astype(BF)
        else:
            gsend[slot] = dw[:, 0 : KER * HID].astype(BF)

    return put


def place(own_len, t, frames, q):
    start = q * own_len
    w0 = jnp.clip(start - HALO, 0, frames - t)
    return pl.multiple_of(w0, 128), pl.multiple_of(start - w0, 128), pl.multiple_of(start, 128)


BASE_W = ["a_hi", "a_lo", "cvec", "pre_t"]
TAIL_W = ["a_hi", "a_lo", "cvec", "end_t", "ebias", "at_b"]


def own_forward_kernel(dp, tp, rows, own_len, t, frames, npiece, snames, owners, off, length, lg, *refs):
    w = dict(zip(BASE_W, refs))
    refs = refs[len(BASE_W) :]
    fr_any = refs[0]
    pieces = refs[1 : 1 + npiece]
    res_pieces = refs[1 + npiece : 2 + npiece + tp]
    outs = refs[2 + npiece + tp :]
    wt, rsb, rsf, end, end_t, bias, h_any, skip_any, hb_any, tt_any, ss_any = outs[:11]
    s = dict(zip(snames, outs[11:-2]))
    piece_sem, sem = outs[-2:]
    w0, _, _ = place(own_len, t, frames, axis("tp"))
    copies = [pltpu.make_async_copy(pieces[m], s["pieces"].at[m], piece_sem.at[m]) for m in range(npiece)]
    load = pltpu.make_async_copy(fr_any.at[:, pl.ds(w0, t)], s["fr"], sem.at[0])
    load.start()
    for c in copies:
        c.start()
    make_masks(s, (off, length, lg), t, w0)
    zero_edges(s["hb"], range(3), t)
    unpack_res(tp, res_pieces, rsb, rsf, end, end_t, bias, s["res"])
    load.wait()
    mask = s["mask"][0:1, :]
    start_hidden(s, t, w, mixed_of(w, s["fr"][...], mask), mask)
    for c in copies:
        c.wait()
    if npiece > 1:
        unpack_conv(tp, rows, owners, dp, s["pieces"], wt)
    else:
        wt[...] = s["pieces"][0]

    def layer_body(layer, carry):
        forward_layer(s, t, wt[layer], rsf[layer], bias[layer], s["mask"][0:1, :], layer, layer + 1, layer)
        return carry

    lax.fori_loop(0, 2, layer_body, 0)
    stores = [
        pltpu.make_async_copy(s["h"], h_any, sem.at[1]),
        pltpu.make_async_copy(s["skip"], skip_any, sem.at[2]),
        pltpu.make_async_copy(s["hb"].at[pl.ds(0, 2)], hb_any, sem.at[3]),
        pltpu.make_async_copy(s["tt"], tt_any, sem.at[4]),
        pltpu.make_async_copy(s["ss"], ss_any, sem.at[5]),
    ]
    for c in stores:
        c.start()
    for c in stores:
        c.wait()


def call_own_forward(dp, tp, rows, own_len, frames, scal, w, fr, pieces, res_pieces):
    t = min(own_len + 2 * HALO, frames)
    sc = {
        "member": pltpu.VMEM((8, t), F32),
        "mask": pltpu.VMEM((8, t), F32),
        "fr": pltpu.VMEM((C, t), BF),
        "h": pltpu.VMEM((HID, t), F32),
        "skip": pltpu.VMEM((HID, t), F32),
        "hb": pltpu.VMEM((3, HID, t + 256), BF),
        "tt": pltpu.VMEM((2, HID, t), BF),
        "ss": pltpu.VMEM((2, HID, t), BF),
        "pieces": pltpu.VMEM((len(pieces),) + pieces[0].shape, BF),
        "res": pltpu.VMEM((tp, LAYERS, HID // tp, 2 * HID), BF),
    }
    sds = jax.ShapeDtypeStruct
    return pl.pallas_call(
        functools.partial(own_forward_kernel, dp, tp, rows, own_len, t, frames, len(pieces), list(sc)),
        out_shape=[
            sds((2, 2 * HID, KER * HID), BF),
            sds((LAYERS, HID, 2 * HID), BF),
            sds((LAYERS, 2 * HID, HID), BF),
            sds((HID, C), BF),
            sds((C, HID), BF),
            sds((LAYERS, 2 * HID, 1), F32),
            sds((HID, t), F32),
            sds((HID, t), F32),
            sds((2, HID, t + 256), BF),
            sds((2, HID, t), BF),
            sds((2, HID, t), BF),
        ],
        in_specs=[sm()] * 4 + [vm()] * len(BASE_W) + [hb()] * (1 + len(pieces)) + [vm()] * (tp + 1),
        out_specs=[vm()] * 6 + [hb()] * 5,
        scratch_shapes=list(sc.values())
        + [pltpu.SemaphoreType.DMA((len(pieces),)), pltpu.SemaphoreType.DMA((6,))],
        compiler_params=pltpu.CompilerParams(vmem_limit_bytes=VMEM_BYTES),
        cost_estimate=pl.CostEstimate(flops=1000, bytes_accessed=1000, transcendentals=0),
        name="ownfwd",
    )(*scal, *[w[k] for k in BASE_W], fr, *pieces, *res_pieces)


def conv_shape(dp):
    return (dp, 2, 2 * HID, 128) if dp * 128 <= MAX_PACKED else (2, 2 * HID, KER * HID)


MID_W = ["a_hi", "a_lo", "cvec", "end_t", "ebias", "at_b", "end", "rsf", "bias"]
MID_STATE = ["hb", "tt", "ss", "dsk", "dm", "x0b"]


def own_middle_kernel(dp, tp, rows, own_len, t, frames, npiece, snames, owners, off, length, lg, *refs):
    w = dict(zip(MID_W, refs))
    refs = refs[len(MID_W) :]
    fr_any, og_any, h_in, skip_in = refs[:4]
    pieces = refs[4 : 4 + npiece]
    refs = refs[4 + npiece :]
    wt, fo_any, result, d_end_out, ebias_out = refs[:5]
    state = dict(zip(MID_STATE, refs[5:11]))
    s = dict(zip(snames, refs[11:-2]))
    piece_sem, sem = refs[-2:]
    w0, off_own, start = place(own_len, t, frames, axis("tp"))
    copies = [pltpu.make_async_copy(pieces[m], s["pieces"].at[m], piece_sem.at[m]) for m in range(npiece)]
    loads = [
        pltpu.make_async_copy(h_in, s["h"], sem.at[0]),
        pltpu.make_async_copy(skip_in, s["skip"], sem.at[1]),
        pltpu.make_async_copy(fr_any.at[:, pl.ds(w0, t)], s["fr"], sem.at[2]),
        pltpu.make_async_copy(og_any.at[:, pl.ds(w0, t)], s["og"], sem.at[3]),
    ]
    for c in copies + loads:
        c.start()
    weight = make_masks(s, (off, length, lg), t, w0)
    zero_edges(s["hb"], range(3), t)
    for c in copies:
        c.wait()
    if npiece > 1:
        unpack_conv(tp, rows, owners, dp, s["pieces"], wt)
    else:
        wt[...] = s["pieces"][0]
    for c in loads:
        c.wait()
    s["hb"][0, :, 128 : t + 128] = s["h"][...].astype(BF)

    def layer_body(i, carry):
        forward_layer(
            s, t, wt[i], w["rsf"][i + 2], w["bias"][i + 2], s["mask"][0:1, :], i, i + 1, i
        )
        return carry

    lax.fori_loop(0, 2, layer_body, 0)
    stores = [
        pltpu.make_async_copy(s["hb"].at[pl.ds(0, 2)], state["hb"], sem.at[5]),
        pltpu.make_async_copy(s["tt"], state["tt"], sem.at[6]),
        pltpu.make_async_copy(s["ss"], state["ss"], sem.at[7]),
    ]
    for c in stores:
        c.start()
    mask = s["mask"][0:1, :]
    window_tail(True, t, w, s, mixed_of(w, s["fr"][...], mask), mask, weight)
    own = pl.ds(off_own, own_len)
    more = [
        pltpu.make_async_copy(s["fo"].at[:, own], fo_any.at[:, pl.ds(start, own_len)], sem.at[4]),
        pltpu.make_async_copy(s["dsk"], state["dsk"], sem.at[8]),
        pltpu.make_async_copy(s["dm"], state["dm"], sem.at[9]),
        pltpu.make_async_copy(s["x0b"], state["x0b"], sem.at[10]),
    ]
    for c in more:
        c.start()
    result[0:HALF, :] = s["fo"][HALF:C, own].astype(BF)
    result[HALF:C, :] = s["dm"][HALF:C, own]
    ld = logdet_part(s, own)
    hi = ld.astype(BF)
    lo = (ld - hi.astype(F32)).astype(BF)
    result[C : C + 16, 0:128] = jnp.concatenate([hi, lo], axis=0)
    ones = jnp.ones((8, own_len), BF)
    d_end_out[...] = nt(s["skl"][:, own], s["dproj"][:, own])
    ebias_out[...] = nt(ones, s["dproj"][:, own])
    for c in stores + more:
        c.wait()


def call_own_middle(dp, tp, rows, own_len, frames, scal, w, fr, og, h, skip, pieces):
    t = min(own_len + 2 * HALO, frames)
    sc = {
        "member": pltpu.VMEM((8, t), F32),
        "mask": pltpu.VMEM((8, t), F32),
        "pf": pltpu.VMEM((8, t), F32),
        "fr": pltpu.VMEM((C, t), BF),
        "og": pltpu.VMEM((C, t), BF),
        "h": pltpu.VMEM((HID, t), F32),
        "skip": pltpu.VMEM((HID, t), F32),
        "fo": pltpu.VMEM((C, t), F32),
        "hb": pltpu.VMEM((3, HID, t + 256), BF),
        "tt": pltpu.VMEM((2, HID, t), BF),
        "ss": pltpu.VMEM((2, HID, t), BF),
        "pieces": pltpu.VMEM((len(pieces),) + pieces[0].shape, BF),
        "dm": pltpu.VMEM((C, t), BF),
        "x0b": pltpu.VMEM((HALF, t), BF),
        "dproj": pltpu.VMEM((C, t), BF),
        "skl": pltpu.VMEM((HID, t), BF),
        "dsk": pltpu.VMEM((HID, t), BF),
    }
    sds = jax.ShapeDtypeStruct
    return pl.pallas_call(
        functools.partial(own_middle_kernel, dp, tp, rows, own_len, t, frames, len(pieces), list(sc)),
        out_shape=[
            sds((2, 2 * HID, KER * HID), BF),
            sds((C, frames), F32),
            sds((C + 16, own_len), BF),
            sds((HID, C), F32),
            sds((8, C), F32),
            sds((2, HID, t + 256), BF),
            sds((2, HID, t), BF),
            sds((2, HID, t), BF),
            sds((HID, t), BF),
            sds((C, t), BF),
            sds((HALF, t), BF),
        ],
        in_specs=[sm()] * 4 + [vm()] * len(MID_W) + [hb()] * (4 + len(pieces)),
        out_specs=[vm(), hb(), vm(), vm(), vm()] + [hb()] * 6,
        scratch_shapes=list(sc.values())
        + [pltpu.SemaphoreType.DMA((len(pieces),)), pltpu.SemaphoreType.DMA((11,))],
        compiler_params=pltpu.CompilerParams(vmem_limit_bytes=VMEM_BYTES),
        cost_estimate=pl.CostEstimate(flops=1000, bytes_accessed=1000, transcendentals=0),
        name="ownmid",
    )(*scal, *[w[k] for k in MID_W], fr, og, h, skip, *pieces)


def own_back_kernel(dp, tp, rows, own_len, t, frames, snames, owners, off, length, lg, *refs):
    wt, rsb, d_end, ebias = refs[:4]
    dsk_in, tt_in, ss_in, hb_in = refs[4:8]
    gkeep, gsend, osend, smallg, dh_any = refs[8:13]
    s = dict(zip(snames, refs[13:-1]))
    s["smallg"] = smallg
    sem = refs[-1]
    units = HID // tp
    w0, off_own, start = place(own_len, t, frames, axis("tp"))
    loads = [
        pltpu.make_async_copy(dsk_in, s["dsk"], sem.at[0]),
        pltpu.make_async_copy(tt_in, s["tt"], sem.at[1]),
        pltpu.make_async_copy(ss_in, s["ss"], sem.at[2]),
        pltpu.make_async_copy(hb_in, s["hb"], sem.at[3]),
    ]
    for c in loads:
        c.start()
    make_masks(s, (off, length, lg), t, w0)
    zero_edges(s["dg"], [None], t)
    own = pl.ds(off_own, own_len)
    own_in = pl.ds(pl.multiple_of(off_own + 128, 128), own_len)
    smallg[...] = jnp.zeros((16, 2 * HID), F32)
    ones = jnp.ones((8, own_len), BF)
    put_rs, slots, high = rs_writer(tp, osend, units)
    for q in range(tp):
        osend[high, slots[q], units : 2 * units, 0:C] = d_end[q * units : (q + 1) * units].astype(BF)
    smallg[6:7, 0:C] = ebias[0:1]
    s["h"][...] = jnp.zeros((HID, t), F32)
    put_conv = conv_writer(dp, rows, owners, s["g"], s["dw"])
    for c in loads:
        c.wait()

    def back_body(i, carry):
        slot = 1 - i
        backward_layer(
            s, t, slot + 2, slot, own, own_in, own_len, wt, rsb, s["mask"][0:1, :], ones, put_rs, put_conv
        )
        return carry

    lax.fori_loop(0, 2, back_body, 0)
    stores = [pltpu.make_async_copy(s["h"], dh_any, sem.at[4])]
    half = s["g"].shape[0] // 2
    for ref, lo, i in ((gkeep, 0, 5), (gsend, half, 6)):
        stores += [pltpu.make_async_copy(s["g"].at[pl.ds(lo, half)], ref, sem.at[i])]
    for c in stores:
        c.start()
    for c in stores:
        c.wait()


def call_own_back(dp, tp, rows, own_len, frames, scal, w, d_end, ebias, dsk, tt, ss, hbs):
    shape = conv_shape(dp)
    t = min(own_len + 2 * HALO, frames)
    units = HID // tp
    sc = {
        "member": pltpu.VMEM((8, t), F32),
        "mask": pltpu.VMEM((8, t), F32),
        "h": pltpu.VMEM((HID, t), F32),
        "g": pltpu.VMEM(shape, BF),
        "hb": pltpu.VMEM((2, HID, t + 256), BF),
        "tt": pltpu.VMEM((2, HID, t), BF),
        "ss": pltpu.VMEM((2, HID, t), BF),
        "dsk": pltpu.VMEM((HID, t), BF),
        "d": pltpu.VMEM((2 * HID, t), BF),
        "dg": pltpu.VMEM((2 * HID, t + 256), BF),
        "dw": pltpu.VMEM((2 * HID, 1024), F32),
        "wd": pltpu.VMEM((HID, 2 * KER * HID), BF),
    }
    sds = jax.ShapeDtypeStruct
    return pl.pallas_call(
        functools.partial(own_back_kernel, dp, tp, rows, own_len, t, frames, list(sc)),
        out_shape=[
            sds((shape[0] // 2,) + shape[1:], BF),
            sds((shape[0] // 2,) + shape[1:], BF),
            sds((2, tp, 3 * units, 2 * HID), BF),
            sds((16, 2 * HID), F32),
            sds((HID, t), F32),
        ],
        in_specs=[sm()] * 4 + [vm()] * 4 + [hb()] * 4,
        out_specs=[hb(), hb(), vm(), vm(), hb()],
        scratch_shapes=list(sc.values()) + [pltpu.SemaphoreType.DMA((7,))],
        compiler_params=pltpu.CompilerParams(vmem_limit_bytes=VMEM_BYTES),
        cost_estimate=pl.CostEstimate(flops=1000, bytes_accessed=1000, transcendentals=0),
        name="ownback",
    )(*scal, w["wt_b"], w["rsb"], d_end, ebias, dsk, tt, ss, hbs)


ASM_W = ["a_hi", "a_lo", "cvec", "at_b"]


def assemble_kernel(tp, kk, own_len, snames, off, length, lg, *refs):
    w = dict(zip(ASM_W, refs))
    dpp, result_any, fr_any, og_any = refs[len(ASM_W) : len(ASM_W) + 4]
    fo_any, fg_any = refs[len(ASM_W) + 6 : len(ASM_W) + 8]
    s = dict(zip(snames, refs[len(ASM_W) + 8 : -1]))
    sem = refs[-1]
    start = pl.multiple_of(from_left(axis("tp"), kk, tp) * own_len, 128)
    where = pl.ds(start, own_len)
    c0 = pltpu.make_async_copy(fr_any.at[:, where], s["fr"], sem.at[0])
    c1 = pltpu.make_async_copy(og_any.at[pl.ds(0, HALF), where], s["og"], sem.at[1])
    c2 = pltpu.make_async_copy(result_any.at[pl.ds(0, C)], s["result"], sem.at[4])
    result = s["result"]
    c0.start()
    c1.start()
    c2.start()
    make_masks(s, (off, length, lg), own_len, start)
    c0.wait()
    c1.wait()
    c2.wait()
    mask = s["mask"][0:1, :]
    fr = s["fr"][...]
    half = slice(0, HALF)
    s["fo"][0:HALF, :] = (nn(w["a_hi"][half, :], fr) + nn(w["a_lo"][half, :], fr) + w["cvec"][half, :]) * mask
    s["fo"][HALF:C, :] = result[0:HALF, :].astype(F32)
    o0 = pltpu.make_async_copy(s["fo"], fo_any.at[:, where], sem.at[2])
    o0.start()
    first = s["og"][...].astype(F32) * mask + dpp[...].astype(F32)
    dm = jnp.concatenate([first.astype(BF), result[HALF:C, :]], axis=0)
    s["fg"][...] = nn(w["at_b"][...], dm)
    o1 = pltpu.make_async_copy(s["fg"], fg_any.at[:, where], sem.at[3])
    o1.start()
    o0.wait()
    o1.wait()


def call_assemble(tp, kk, own_len, scal, w, result, dpp, fr, og, fo, fg):
    sc = {
        "member": pltpu.VMEM((8, own_len), F32),
        "mask": pltpu.VMEM((8, own_len), F32),
        "fr": pltpu.VMEM((C, own_len), BF),
        "og": pltpu.VMEM((HALF, own_len), BF),
        "result": pltpu.VMEM((C, own_len), BF),
        "fo": pltpu.VMEM((C, own_len), F32),
        "fg": pltpu.VMEM((C, own_len), F32),
    }
    n = len(ASM_W)
    return pl.pallas_call(
        functools.partial(assemble_kernel, tp, kk, own_len, list(sc)),
        out_shape=[jax.ShapeDtypeStruct(fo.shape, F32), jax.ShapeDtypeStruct(fg.shape, F32)],
        in_specs=[sm()] * 3 + [vm()] * (n + 1) + [hb()] * 5,
        out_specs=[hb(), hb()],
        input_output_aliases={n + 7: 0, n + 8: 1},
        scratch_shapes=list(sc.values()) + [pltpu.SemaphoreType.DMA((5,))],
        compiler_params=pltpu.CompilerParams(vmem_limit_bytes=32 * 1024 * 1024),
        cost_estimate=pl.CostEstimate(flops=1000, bytes_accessed=1000, transcendentals=0),
        name="assemble",
    )(*scal[1:], *[w[k] for k in ASM_W], dpp, result, fr, og, fo, fg)


LAST_W = ["wt_a", "rsb", "pre_b", "mixfull", "rows", "extra", "at_b"]


def own_last_kernel(dp, tp, rows, own_len, t, frames, snames, owners, off, length, lg, *refs):
    w = dict(zip(LAST_W, refs))
    refs = refs[len(LAST_W) :]
    osend_in, smallg_in, fr_any, hb_in, tt_in, ss_in, dh_in, dsk_in, dm_in, x0_in = refs[:10]
    gkeep, gsend, okeep, osend_out, dpp, fg_any = refs[10:16]
    s = dict(zip(snames, refs[16:-1]))
    osend = s["o"]
    sem = refs[-1]
    units = HID // tp
    w0, off_own, start = place(own_len, t, frames, axis("tp"))
    loads = [
        pltpu.make_async_copy(dh_in, s["h"], sem.at[0]),
        pltpu.make_async_copy(dsk_in, s["dsk"], sem.at[1]),
        pltpu.make_async_copy(tt_in, s["tt"], sem.at[2]),
        pltpu.make_async_copy(ss_in, s["ss"], sem.at[3]),
        pltpu.make_async_copy(hb_in, s["hb"], sem.at[4]),
        pltpu.make_async_copy(fr_any.at[:, pl.ds(start, own_len)], s["fr"], sem.at[5]),
        pltpu.make_async_copy(dm_in, s["dm"], sem.at[6]),
        pltpu.make_async_copy(x0_in, s["x0b"], sem.at[7]),
    ]
    for c in loads:
        c.start()
    make_masks(s, (off, length, lg), t, w0)
    zero_edges(s["dg"], [None], t)
    osend[...] = osend_in[...]
    s["smallg"][...] = smallg_in[...]
    own = pl.ds(off_own, own_len)
    own_in = pl.ds(pl.multiple_of(off_own + 128, 128), own_len)
    ones = jnp.ones((8, own_len), BF)
    put_rs, slots, high = rs_writer(tp, osend, units)
    put_conv = conv_writer(dp, rows, owners, s["g"], s["dw"])
    for c in loads:
        c.wait()

    def back_body(i, carry):
        slot = 1 - i
        backward_layer(
            s, t, slot, slot, own, own_in, own_len, w["wt_a"], w["rsb"], s["mask"][0:1, :], ones, put_rs, put_conv
        )
        return carry

    lax.fori_loop(0, 2, back_body, 0)
    stores = []
    half = s["g"].shape[0] // 2
    for ref, lo, i in ((gkeep, 0, 8), (gsend, half, 9)):
        stores += [pltpu.make_async_copy(s["g"].at[pl.ds(lo, half)], ref, sem.at[i])]
        stores[-1].start()
    smallg = s["smallg"]
    d_pre = (s["h"][:, own] * s["mask"][0:1, own]).astype(BF)
    dpp_v = nn(w["pre_b"][...], d_pre).astype(BF)
    dpp[...] = dpp_v
    d_prew = nt(s["x0b"][:, own], d_pre)
    dm = s["dm"][:, own]
    total = jnp.concatenate([dm[0:HALF].astype(F32) + dpp_v.astype(F32), dm[HALF:C].astype(F32)], axis=0)
    s["fg"][...] = nn(w["at_b"][...], total.astype(BF))
    stores += [pltpu.make_async_copy(s["fg"], fg_any.at[:, pl.ds(start, own_len)], sem.at[10])]
    stores[-1].start()
    fr = s["fr"][...]
    qd = nt(dm, fr)
    q0 = nt(dpp_v, fr)
    qd = jnp.concatenate([qd[0:HALF] + q0, qd[HALF:C]], axis=0)
    v = jnp.sum(dm.astype(F32), axis=1, keepdims=True)
    v0 = jnp.sum(dpp_v.astype(F32), axis=1, keepdims=True)
    v = jnp.concatenate([v[0:HALF] + v0, v[HALF:C]], axis=0)
    mixfull = w["mixfull"][...]
    es = w["rows"][0:1, :]
    bb = w["rows"][1:2, :]
    smallg[4:5, 0:C] = es * jnp.sum(mixfull * qd, axis=0, keepdims=True) + w["rows"][2:3, :]
    smallg[5:6, 0:C] = jnp.sum(mixfull * v, axis=0, keepdims=True)
    ch_r = lax.broadcasted_iota(jnp.int32, (C, 1), 0)
    ch_c = lax.broadcasted_iota(jnp.int32, (1, C), 1)

    def group(ch):
        return lax.shift_right_logical(ch - jnp.where(ch >= HALF, HALF, 0), 1)

    d2 = jnp.where(group(ch_r) == group(ch_c), v * bb + es * qd, 0.0)
    wide = lax.broadcasted_iota(jnp.int32, (C, 128), 1)
    chan = lax.broadcasted_iota(jnp.int32, (C, 128), 0)
    pair = 2 * (chan >= HALF).astype(jnp.int32) + jnp.bitwise_and(chan, 1)
    one_hot = (pair == wide).astype(F32)
    part = tn(one_hot, d2, PRECISE)
    smallg[8:16, 0:128] = nn(part, one_hot, PRECISE)[0:8] + w["extra"][0:8, :]
    small = smallg[...]
    for q in range(tp):
        osend[high, slots[q], units : units + HALF, HID : 2 * HID] = d_prew.astype(BF)
        for h in range(2):
            osend[high, slots[q], 3 * units - 16 : 3 * units, h * units : (h + 1) * units] = small[
                :, h * HID + q * units : h * HID + (q + 1) * units
            ].astype(BF)
        osend[high, slots[q], 3 * units - 12 : 3 * units, 0:C] = small[4:16, 0:C].astype(BF)
    for ref, i in ((okeep, 11), (osend_out, 12)):
        stores += [pltpu.make_async_copy(osend.at[i - 11], ref, sem.at[i])]
        stores[-1].start()
    for c in stores:
        c.wait()


def call_own_last(dp, tp, rows, own_len, frames, scal, w, osend, smallg, fr, hbs, tt, ss, dh, dsk, dm, x0):
    shape = conv_shape(dp)
    t = min(own_len + 2 * HALO, frames)
    sc = {
        "member": pltpu.VMEM((8, t), F32),
        "mask": pltpu.VMEM((8, t), F32),
        "fr": pltpu.VMEM((C, own_len), BF),
        "h": pltpu.VMEM((HID, t), F32),
        "hb": pltpu.VMEM((2, HID, t + 256), BF),
        "tt": pltpu.VMEM((2, HID, t), BF),
        "ss": pltpu.VMEM((2, HID, t), BF),
        "dm": pltpu.VMEM((C, t), BF),
        "x0b": pltpu.VMEM((HALF, t), BF),
        "dsk": pltpu.VMEM((HID, t), BF),
        "d": pltpu.VMEM((2 * HID, t), BF),
        "dg": pltpu.VMEM((2 * HID, t + 256), BF),
        "dw": pltpu.VMEM((2 * HID, 1024), F32),
        "wd": pltpu.VMEM((HID, 2 * KER * HID), BF),
        "smallg": pltpu.VMEM((16, 2 * HID), F32),
        "g": pltpu.VMEM(shape, BF),
        "o": pltpu.VMEM(osend.shape, BF),
        "fg": pltpu.VMEM((C, own_len), F32),
    }
    sds = jax.ShapeDtypeStruct
    return pl.pallas_call(
        functools.partial(own_last_kernel, dp, tp, rows, own_len, t, frames, list(sc)),
        out_shape=[
            sds((shape[0] // 2,) + shape[1:], BF),
            sds((shape[0] // 2,) + shape[1:], BF),
            sds(osend.shape[1:], BF),
            sds(osend.shape[1:], BF),
            sds((HALF, own_len), BF),
            sds((C, frames), F32),
        ],
        in_specs=[sm()] * 4 + [vm()] * (len(LAST_W) + 2) + [hb()] * 8,
        out_specs=[hb(), hb(), hb(), hb(), vm(), hb()],
        scratch_shapes=list(sc.values()) + [pltpu.SemaphoreType.DMA((13,))],
        compiler_params=pltpu.CompilerParams(vmem_limit_bytes=VMEM_BYTES),
        cost_estimate=pl.CostEstimate(flops=1000, bytes_accessed=1000, transcendentals=0),
        name="ownlast",
    )(*scal, *[w[k] for k in LAST_W], osend, smallg, fr, hbs, tt, ss, dh, dsk, dm, x0)


FWD_W = ["a_hi", "a_lo", "cvec", "pre_t", "end_t", "ebias", "at_b", "wt_a", "wt_b", "rsf", "bias"]


def fwd_kernel(tp, kk, own_len, t, frames, has_dpp, snames, off, length, lg, *refs):
    w = dict(zip(FWD_W, refs))
    refs = refs[len(FWD_W) :]
    fr_any, og_any = refs[:2]
    nd = 1 if has_dpp else 0
    fo_any, p1_any, ld = refs[4 + nd : 7 + nd]
    s = dict(zip(snames, refs[7 + nd : -1]))
    sem = refs[-1]
    w0, off_own, start = place(own_len, t, frames, from_left(axis("tp"), kk, tp))
    dpp = None
    if has_dpp:
        s["dpp"][...] = jnp.zeros((HALF, t), BF)
        s["dpp"][:, pl.ds(off_own, own_len)] = refs[4][...]
        dpp = s["dpp"]
    c0 = pltpu.make_async_copy(fr_any.at[:, pl.ds(w0, t)], s["fr"], sem.at[0])
    c1 = pltpu.make_async_copy(og_any.at[:, pl.ds(w0, t)], s["og"], sem.at[1])
    c0.start()
    c1.start()
    make_masks(s, (off, length, lg), t, w0)
    zero_edges(s["hb"], range(2), t)
    c0.wait()
    mask = s["mask"][0:1, :]
    mixed = mixed_of(w, s["fr"][...], mask)
    s["mixed"][...] = mixed
    start_hidden(s, t, w, mixed, mask)
    for half in range(2):
        wt = w["wt_a"] if half == 0 else w["wt_b"]

        def layer_body(i, carry):
            layer = 2 * half + i
            forward_layer(
                s, t, wt[i], w["rsf"][layer], w["bias"][layer], s["mask"][0:1, :], i, 1 - i, None
            )
            return carry

        lax.fori_loop(0, 2, layer_body, 0)
    c1.wait()
    dpp = None if dpp is None else dpp[...].astype(F32)
    window_tail(False, t, w, s, s["mixed"][...], s["mask"][0:1, :], None, dpp)
    own = pl.ds(off_own, own_len)
    o0 = pltpu.make_async_copy(s["fo"].at[:, own], fo_any.at[:, pl.ds(start, own_len)], sem.at[2])
    o1 = pltpu.make_async_copy(s["p1"].at[:, own], p1_any.at[:, pl.ds(start, own_len)], sem.at[3])
    o0.start()
    o1.start()
    ld[...] = logdet_part(s, own)
    o0.wait()
    o1.wait()


def call_fwd(tp, kk, own_len, frames, scal, w, fr, og, fo, p1, dpp=None):
    t = min(own_len + 2 * HALO, frames)
    sc = {
        "member": pltpu.VMEM((8, t), F32),
        "mask": pltpu.VMEM((8, t), F32),
        "pf": pltpu.VMEM((8, t), F32),
        "fr": pltpu.VMEM((C, t), BF),
        "og": pltpu.VMEM((C, t), BF),
        "mixed": pltpu.VMEM((C, t), F32),
        "h": pltpu.VMEM((HID, t), F32),
        "skip": pltpu.VMEM((HID, t), F32),
        "fo": pltpu.VMEM((C, t), F32),
        "p1": pltpu.VMEM((C, t), F32),
        "hb": pltpu.VMEM((2, HID, t + 256), BF),
    }
    n = len(FWD_W)
    more = [] if dpp is None else [dpp]
    if more:
        sc["dpp"] = pltpu.VMEM((HALF, t), BF)
    return pl.pallas_call(
        functools.partial(fwd_kernel, tp, kk, own_len, t, frames, dpp is not None, list(sc)),
        out_shape=(
            jax.ShapeDtypeStruct((C, frames), F32),
            jax.ShapeDtypeStruct((C, frames), F32),
            jax.ShapeDtypeStruct((8, 128), F32),
        ),
        in_specs=[sm()] * 3 + [vm()] * n + [hb()] * 4 + [vm()] * len(more),
        out_specs=(hb(), hb(), vm()),
        input_output_aliases={n + 5: 0, n + 6: 1},
        scratch_shapes=list(sc.values()) + [pltpu.SemaphoreType.DMA((4,))],
        compiler_params=pltpu.CompilerParams(vmem_limit_bytes=VMEM_BYTES),
        cost_estimate=pl.CostEstimate(flops=1000, bytes_accessed=1000, transcendentals=0),
        name="fwd",
    )(*scal[1:], *[w[k] for k in FWD_W], fr, og, fo, p1, *more)


def moments(moment, square, grad):
    new_moment = BETA * moment + (1.0 - BETA) * grad
    new_square = BETA * square + (1.0 - BETA) * grad * grad
    correction = 1.0 - BETA**STEP
    direction = new_moment / correction / (jnp.sqrt(new_square / correction) + EPSILON)
    return (new_moment, new_square, direction)


def adam_update(weight, moment, square, grad, rate):
    new_moment, new_square, direction = moments(moment, square, grad)
    return (weight - rate * (direction + DECAY * weight), new_moment, new_square)


def fold_kernel(n, tp, *refs):
    keep_a, got_a, keep_b, got_b, keep_o, got_o = refs[:6]
    outs = refs[6:]
    for m in range(n):
        outs[m][0:2] = (keep_a[m].astype(F32) + got_a[m].astype(F32)).astype(BF)
        outs[m][2:4] = (keep_b[m].astype(F32) + got_b[m].astype(F32)).astype(BF)
    for q in range(tp):
        outs[n + q][...] = (keep_o[q].astype(F32) + got_o[q].astype(F32)).astype(BF)


def call_fold(keep_a, got_a, keep_b, got_b, keep_o, got_o):
    n, tp = keep_a.shape[0], keep_o.shape[0]
    return pl.pallas_call(
        functools.partial(fold_kernel, n, tp),
        out_shape=[jax.ShapeDtypeStruct((LAYERS,) + keep_a.shape[2:], BF)] * n
        + [jax.ShapeDtypeStruct(keep_o.shape[1:], BF)] * tp,
        in_specs=[vm()] * 6,
        out_specs=[vm()] * (n + tp),
        compiler_params=pltpu.CompilerParams(vmem_limit_bytes=VMEM_BYTES),
        name="fold",
    )(keep_a, got_a, keep_b, got_b, keep_o, got_o)


def rotate_kernel(n, tp, *refs):
    basis = refs[:tp]
    parts = refs[tp : tp + n]
    outs = refs[tp + n :]
    for layer in range(LAYERS):
        total = parts[0][layer].astype(F32)
        for m in range(1, n):
            total = total + parts[m][layer].astype(F32)
        total = total.astype(BF)
        for kk in range(tp):
            outs[kk][layer] = nn(basis[kk][layer], total).astype(BF)


def call_rotate(tp, basis, parts):
    cols = basis[0].shape[1]
    n = len(parts)
    return pl.pallas_call(
        functools.partial(rotate_kernel, n, tp),
        out_shape=[jax.ShapeDtypeStruct((LAYERS, cols, 128), BF)] * tp,
        in_specs=[vm()] * (tp + n),
        out_specs=[vm()] * tp,
        compiler_params=pltpu.CompilerParams(vmem_limit_bytes=VMEM_BYTES),
        cost_estimate=pl.CostEstimate(flops=1000, bytes_accessed=1000, transcendentals=0),
        name="rotate",
    )(*basis, *parts)


def moment_kernel(tp, rows, *refs):
    parts = refs[:tp]
    moment, square, new_moment, new_square, direction = refs[tp:]
    total = parts[0][...].astype(F32)
    for kk in range(1, tp):
        total = total + parts[kk][...].astype(F32)
    grad = total[:, :, 0:rows]
    m, v, d = moments(moment[...], square[...], grad)
    new_moment[...] = m
    new_square[...] = v
    direction[:, :, 0:rows] = d.astype(BF)
    if rows < 128:
        direction[:, :, rows:128] = jnp.zeros(d.shape[:2] + (128 - rows,), BF)


def call_moments(tp, rows, parts, moment, square):
    shape = moment.shape
    return pl.pallas_call(
        functools.partial(moment_kernel, tp, rows),
        out_shape=[
            jax.ShapeDtypeStruct(shape, F32),
            jax.ShapeDtypeStruct(shape, F32),
            jax.ShapeDtypeStruct(shape[:2] + (128,), BF),
        ],
        in_specs=[vm()] * (tp + 2),
        out_specs=[vm()] * 3,
        name="moments",
    )(*parts, moment, square)


def back_kernel(tp, rows, *refs):
    basis = refs[:tp]
    directions = refs[tp : 2 * tp]
    weight, out, scratch = refs[2 * tp :]
    units = HID // tp
    me_tp = axis("tp")
    for layer in range(LAYERS):
        total = tn(basis[0][layer], directions[0][layer])
        for kk in range(1, tp):
            total = total + tn(basis[kk][layer], directions[kk][layer])
        scratch[layer] = total
    for layer in range(LAYERS):
        for h in range(2):
            row = pl.ds(pl.multiple_of(h * HID + me_tp * units, 16), units)
            back = scratch[layer, row, 0:rows]
            here = slice(h * units, (h + 1) * units)
            value = weight[layer, here, :]
            out[layer, here, :] = value - RATE_CONV * (back + DECAY * value)


def call_back(tp, rows, basis, directions, weight):
    return pl.pallas_call(
        functools.partial(back_kernel, tp, rows),
        out_shape=jax.ShapeDtypeStruct(weight.shape, F32),
        in_specs=[vm()] * (2 * tp + 1),
        out_specs=vm(),
        scratch_shapes=[pltpu.VMEM((LAYERS, 2 * HID, 128), F32)],
        cost_estimate=pl.CostEstimate(flops=1000, bytes_accessed=1000, transcendentals=0),
        name="back",
    )(*basis, *directions, weight)


def small_kernel(tp, *refs):
    lows, highs = refs[0], refs[1]
    ins = refs[2:20]
    outs = refs[20:]
    units = HID // tp
    core = jnp.bitwise_and(axis("dp"), 1)

    def put(i, grad, rate, index=None):
        if index is None:
            new = adam_update(ins[3 * i][...], ins[3 * i + 1][...], ins[3 * i + 2][...], grad, rate)
            for k in range(3):
                outs[3 * i + k][...] = new[k]
        else:
            new = adam_update(ins[3 * i][index], ins[3 * i + 1][index], ins[3 * i + 2][index], grad, rate)
            for k in range(3):
                outs[3 * i + k][index] = new[k]

    def rows(half, lo, size, c0, c1):
        a = lows[lo : lo + size, c0:c1].astype(F32)
        b = highs[lo : lo + size, c0:c1].astype(F32)
        return jnp.where(core == half, a, b)

    tail = rows(1, 3 * units - 16, 16, 0, 2 * HID)
    put(0, tail[4:7, 0:C], RATE_SMALL)
    put(1, tail[8:12, 0:4], RATE_MIX)
    put(2, rows(1, units, HALF, HID, 2 * HID), RATE_PRE)
    for h in range(2):
        put(3, tail[0:LAYERS, h * units : (h + 1) * units], RATE_BIAS, (slice(None), h, slice(None)))
    for layer in range(LAYERS):
        half = 1 if layer == LAYERS - 1 else 0
        lo = 0 if layer == LAYERS - 1 else layer * units
        put(4, rows(half, lo, units, 0, HID), RATE_RESSKIP, LAYERS - 1 + layer)
        if layer < LAYERS - 1:
            put(4, rows(half, lo, units, HID, 2 * HID), RATE_RESSKIP, layer)
    put(5, rows(1, units, units, 0, C), RATE_END)


def call_small(tp, low, high, ins):
    return pl.pallas_call(
        functools.partial(small_kernel, tp),
        out_shape=[jax.ShapeDtypeStruct(x.shape, F32) for x in ins],
        in_specs=[vm()] * (2 + len(ins)),
        out_specs=[vm()] * len(ins),
        name="smallupd",
    )(low, high, *ins)


def grad_kernel(tp, kk, own_len, at_b, dpp, p1_any, out_any, scratch, sem):
    _, _, start = place(own_len, own_len, own_len * tp, from_left(axis("tp"), kk, tp))
    where = pl.ds(start, own_len)
    load = pltpu.make_async_copy(p1_any.at[:, where], scratch, sem.at[0])
    load.start()
    more = nn(at_b[:, 0:HALF], dpp[...])
    load.wait()
    scratch[...] += more
    store = pltpu.make_async_copy(scratch, out_any.at[:, where], sem.at[1])
    store.start()
    store.wait()


def call_grad(tp, kk, own_len, at_b, dpp, p1):
    return pl.pallas_call(
        functools.partial(grad_kernel, tp, kk, own_len),
        out_shape=jax.ShapeDtypeStruct(p1.shape, F32),
        in_specs=[vm(), vm(), hb()],
        out_specs=hb(),
        input_output_aliases={2: 0},
        scratch_shapes=[pltpu.VMEM((C, own_len), F32), pltpu.SemaphoreType.DMA((2,))],
        cost_estimate=pl.CostEstimate(flops=1000, bytes_accessed=1000, transcendentals=0),
        name="fgrad",
    )(at_b, dpp, p1)


def local(
    frames_in,
    out_grad,
    logdet_grad,
    lengths,
    offsets,
    owners,
    small_params,
    small_moment,
    small_square,
    mix,
    mix_moment,
    mix_square,
    pre_weight,
    pre_moment,
    pre_square,
    conv_weight,
    conv_moment,
    conv_square,
    conv_basis,
    conv_bias,
    conv_bias_moment,
    conv_bias_square,
    res_skip,
    res_skip_moment,
    res_skip_square,
    end_weight,
    end_moment,
    end_square,
):
    dp = lax.axis_size("dp")
    tp = lax.axis_size("tp")
    frames = frames_in.shape[0]
    rows = conv_weight.shape[1]
    units = conv_weight.shape[3]
    own_len = frames // tp
    packed = dp * 128 <= MAX_PACKED

    def shift_tp(x, kk):
        return lax.ppermute(x, "tp", [(i, (i + kk) % tp) for i in range(tp)])

    def swap_dp(x, mask):
        return lax.ppermute(x, "dp", [(i, i ^ mask) for i in range(dp)])

    def gather_tp(x):
        return [x] + [shift_tp(x, kk) for kk in range(1, tp)]

    def after(value, *deps):
        return lax.optimization_barrier((value, *deps))[0]

    cw = jnp.transpose(conv_weight, (0, 2, 3, 1)).reshape(LAYERS, 2 * units, rows)
    conv_a, conv_b, res_s, basis_t = call_pack(
        rows, units, cw, res_skip, end_weight, conv_bias, conv_basis.reshape(LAYERS, 2 * HID, -1)
    )
    names = ["a_hi", "a_lo", "at_b", "cvec", "pre_t", "pre_b", "ebias", "mixfull", "rows", "extra"]
    w = dict(zip(names, call_consts(mix, logdet_grad, small_params, pre_weight)))

    def chips(col):
        return {m: (col if m == 0 else swap_dp(col, m)) for m in range(0, dp, 2)}

    def cores(pieces):
        pieces = dict(pieces)
        for m in range(0, dp, 2):
            pieces[m + 1] = swap_dp(pieces[m], 1)
        pieces = [pieces[m] for m in range(dp)]
        if not packed:
            slot = jnp.bitwise_xor(lax.axis_index("dp"), owners)
            column_of = lax.rem(lax.axis_index("tp") - jnp.arange(tp) + tp, tp)
            stacked = jnp.stack(pieces)[slot][:, column_of]
            stacked = stacked.reshape(dp, tp, 2, 2, units, 128)[..., :rows]
            pieces = [jnp.transpose(stacked, (2, 3, 1, 4, 0, 5)).reshape(2, 2 * HID, KER * HID)]
        return pieces

    col_a = gather_tp(conv_a)
    conv_b, res_s, *col_a = lax.optimization_barrier((conv_b, res_s, *col_a))
    half_a = chips(after(jnp.stack(col_a), w["rows"]))
    res_col = gather_tp(res_s)
    col_b = gather_tp(conv_b)
    pieces_a = cores(half_a)
    res_pieces = res_col + [swap_dp(jnp.stack(res_col), 1)]
    basis_t, *col_b = lax.optimization_barrier((basis_t, *col_b))
    half_b = chips(jnp.stack(col_b))
    basis_pieces = gather_tp(basis_t)
    scal = [owners, offsets, lengths, logdet_grad]
    fr = frames_in.T
    og = out_grad.T

    (wt_a, rsb, rsf, end, end_t, bias, h, skip, hbs, tt, ss) = call_own_forward(
        dp, tp, rows, own_len, frames, scal, w, fr, pieces_a, res_pieces
    )
    w.update(wt_a=wt_a, rsb=rsb, rsf=rsf, end=end, end_t=end_t, bias=bias)
    pieces_b = cores(after(half_b, h))
    h, *basis_pieces = lax.optimization_barrier((h, *basis_pieces))
    (wt_b, fo, result, d_end, d_ebias, hbs_b, tt_b, ss_b, dsk, dm, x0) = call_own_middle(
        dp, tp, rows, own_len, frames, scal, w, fr, og, h, skip, pieces_b
    )
    w["wt_b"] = wt_b
    turn = tp // 2
    rest = [kk for kk in range(1, tp) if kk != turn]
    results = {kk: shift_tp(result, kk) for kk in rest}
    keep_b, send_b, osend, smallg, dh = call_own_back(
        dp, tp, rows, own_len, frames, scal, w, d_end, d_ebias, dsk, tt_b, ss_b, hbs_b
    )
    (keep_a, send_a, keep_o, send_o, dpp, fg) = call_own_last(
        dp, tp, rows, own_len, frames, scal, w, osend, smallg, fr, hbs, tt, ss, dh, dsk, dm, x0
    )

    def order(keep, send):
        if packed:
            return keep, send
        gsend = jnp.concatenate([keep, send])
        where = jnp.bitwise_xor(lax.axis_index("dp"), bit_reverse(jnp.arange(dp), (dp - 1).bit_length()))
        block = jnp.argsort(owners)[where]
        gsend = jnp.transpose(gsend.reshape(2, 2 * HID, dp, rows), (2, 0, 1, 3))[block]
        gsend = jnp.pad(gsend, ((0, 0), (0, 0), (0, 0), (0, 128 - rows)))
        return gsend[: dp // 2], gsend[dp // 2 :]

    send_a, send_o, *gone = lax.optimization_barrier((send_a, send_o, *results.values()))
    results = dict(zip(results, gone))
    keep_a, send_a = order(keep_a, send_a)
    keep_b, send_b = order(keep_b, send_b)
    got_b = swap_dp(send_b, 1)
    got_a = swap_dp(send_a, 1)
    got_o = swap_dp(send_o, 1)
    folded = call_fold(keep_a, got_a, keep_b, got_b, keep_o, got_o)
    n = dp // 2
    bits = (dp - 1).bit_length()
    masks = [2 * bit_reverse(p, bits - 1) for p in range(n)]
    parts = [folded[0]] + [swap_dp(folded[p], masks[p]) for p in range(1, n)]
    others = folded[n:]
    dpps = {kk: shift_tp(dpp, kk) for kk in rest + [turn]}
    arrived = [others[0]] + [
        lax.ppermute(others[kk], "tp", [(i, (i + kk) % tp) for i in range(tp)]) for kk in range(1, tp)
    ]

    fr1 = after(fr, folded[0])
    fo, fg, ld = call_fwd(tp, turn, own_len, frames, scal, w, fr1, og, fo, fg)
    lds = [ld[:, 0]] + [
        jnp.sum(x[C : C + 16, 0].astype(F32).reshape(2, 8), axis=0) for x in [result, *results.values()]
    ]

    ready, *near = lax.optimization_barrier((parts[0], ld, *parts[1:], *[dpps[kk] for kk in rest]))
    parts = [ready] + near[1:n]
    dpps.update(zip(rest, near[n:]))
    turned = call_rotate(tp, basis_pieces, parts)
    rotated = [turned[0]] + [
        lax.ppermute(turned[kk], "tp", [(i, (i - kk) % tp) for i in range(tp)]) for kk in range(1, tp)
    ]
    arrived = [x.astype(F32) for x in arrived]
    while len(arrived) > 1:
        mid = len(arrived) // 2
        arrived = [arrived[i] + arrived[i + mid] for i in range(mid)]
    total = after(arrived[0].astype(BF), ld)
    sums = [total] + [swap_dp(total, m) for m in range(2, dp, 2)]

    fr2 = after(fr, turned[0], total)
    for kk in rest:
        fo, fg = call_assemble(tp, kk, own_len, scal, w, results[kk], dpps[kk], fr2, og, fo, fg)

    conv_m, conv_v, direction = call_moments(
        tp,
        rows,
        [rotated[0]] + [after(x, fg) for x in rotated[1:]],
        jnp.transpose(conv_moment, (0, 2, 1)),
        jnp.transpose(conv_square, (0, 2, 1)),
    )
    directions = gather_tp(direction)
    sums = [x.astype(F32) for x in sums]
    while len(sums) > 1:
        sums = [sums[i] + sums[i + 1] for i in range(0, len(sums), 2)]
    total = after(sums[0].astype(BF), fg)
    other = swap_dp(total, 1)

    p1 = call_grad(tp, turn, own_len, w["at_b"], dpps[turn], after(fg, direction))
    updated = call_small(
        tp,
        total,
        other,
        [
            small_params, small_moment, small_square,
            mix, mix_moment, mix_square,
            pre_weight, pre_moment, pre_square,
            conv_bias, conv_bias_moment, conv_bias_square,
            res_skip, res_skip_moment, res_skip_square,
            end_weight, end_moment, end_square,
        ],
    )
    conv_new = call_back(
        tp, rows, basis_pieces, [direction] + [after(x, p1, updated[0]) for x in directions[1:]], cw
    )
    logdet = w["extra"][8:, 0] + sum(lds) / lengths.astype(F32)

    def conv_out(x):
        return jnp.transpose(x.reshape(LAYERS, 2, units, rows), (0, 3, 1, 2))

    (small_new, small_m, small_v, mix_new, mix_m, mix_v, pre_new, pre_m, pre_v, bias_new, bias_m, bias_v,
     rs_new, rs_m, rs_v, end_new, end_m, end_v) = updated
    return (
        fo.T,
        logdet,
        p1.T,
        small_new,
        small_m,
        small_v,
        mix_new,
        mix_m,
        mix_v,
        pre_new,
        pre_m,
        pre_v,
        conv_out(conv_new),
        jnp.transpose(conv_m, (0, 2, 1)),
        jnp.transpose(conv_v, (0, 2, 1)),
        bias_new,
        bias_m,
        bias_v,
        rs_new,
        rs_m,
        rs_v,
        end_new,
        end_m,
        end_v,
    )


def solution(mesh):
    return jax.shard_map(
        local,
        mesh=mesh,
        in_specs=(
            P("dp", None),
            P("dp", None),
            P("dp"),
            P("dp"),
            P("dp"),
            P(),
            P(),
            P(),
            P(),
            P(),
            P(),
            P(),
            P(),
            P(),
            P(),
            P(None, "dp", None, "tp"),
            P(None, "dp", "tp"),
            P(None, "dp", "tp"),
            P(None, None, None, "tp"),
            P(None, None, "tp"),
            P(None, None, "tp"),
            P(None, None, "tp"),
            P(None, "tp", None),
            P(None, "tp", None),
            P(None, "tp", None),
            P("tp", None),
            P("tp", None),
            P("tp", None),
        ),
        out_specs=(
            P("dp", None),
            P("dp"),
            P("dp", None),
            P(),
            P(),
            P(),
            P(),
            P(),
            P(),
            P(),
            P(),
            P(),
            P(None, "dp", None, "tp"),
            P(None, "dp", "tp"),
            P(None, "dp", "tp"),
            P(None, None, "tp"),
            P(None, None, "tp"),
            P(None, None, "tp"),
            P(None, "tp", None),
            P(None, "tp", None),
            P(None, "tp", None),
            P("tp", None),
            P("tp", None),
            P("tp", None),
        ),
        check_vma=False,
    )
```

```python
import functools
import types
import jax
import jax.numpy as jnp
from jax import lax
from jax.experimental import pallas as pl
from jax.experimental.pallas import tpu as pltpu
from jax.sharding import PartitionSpec as P

C = 160
HALF = 80
HID = 192
KER = 5
LAYERS = 4
STEP = 5
HALO = 128
MAX_PACKED = 1024
VMEM_BYTES = 62 * 1024 * 1024

BETA = 0.5
EPSILON = 1e-08
DECAY = 0.01
RATE_SMALL = 0.1
RATE_MIX = 0.3
RATE_PRE = 0.1
RATE_CONV = 0.03
RATE_BIAS = 0.3
RATE_RESSKIP = 0.07
RATE_END = 0.04
PRECISE = lax.Precision.HIGHEST
BF = jnp.bfloat16
TP = "tp"
DP = "dp"
F32 = jnp.float32


class Names:
    def __init__(self):
        self.found = []

    def __getattr__(self, name):
        self.found.append(name)


def names_of(select):
    got = Names()
    select(got)
    return got.found


def space(names, values):
    return types.SimpleNamespace(**dict(zip(names, values)))


CONST_W = names_of(
    lambda w: (w.a_hi, w.a_lo, w.at_b, w.cvec, w.pre_t, w.pre_b, w.ebias, w.mixfull, w.rows, w.extra)
)


def nn(a, b, precision=None):
    return lax.dot_general(a, b, (((1,), (0,)), ((), ())), precision=precision, preferred_element_type=F32)


def nt(a, b, precision=None):
    return lax.dot_general(a, b, (((1,), (1,)), ((), ())), precision=precision, preferred_element_type=F32)


def tn(a, b, precision=None):
    return lax.dot_general(a, b, (((0,), (0,)), ((), ())), precision=precision, preferred_element_type=F32)


def sigmoid(x):
    return 0.5 * jnp.tanh(0.5 * x) + 0.5


def vm():
    return pl.BlockSpec(memory_space=pltpu.VMEM)


def sm():
    return pl.BlockSpec(memory_space=pltpu.SMEM)


def hb():
    return pl.BlockSpec(memory_space=pl.ANY)


def bit_reverse(value, bits):
    out = value * 0
    for i in range(bits):
        out = out | (((value >> i) & 1) << (bits - 1 - i))
    return out


def axis(name):
    return lax.axis_index(name)


def from_left(me, kk, n):
    return lax.rem(me - kk + n, n)


def column(scalars, dtype, rows=8):
    index = lax.broadcasted_iota(jnp.int32, (rows, 1), 0)
    out = jnp.zeros((rows, 1), dtype)
    for u in range(rows):
        out = jnp.where(index == u, scalars[u], out)
    return out


def to_column(row):
    n = row.shape[1]
    eye = lax.broadcasted_iota(jnp.int32, (n, n), 0) == lax.broadcasted_iota(jnp.int32, (n, n), 1)
    return jnp.sum(jnp.where(eye, jnp.broadcast_to(row, (n, n)), 0.0), axis=1, keepdims=True)


def pack_kernel(rows, units, conv, res, end, bias, basis, packed, later, basis_out, full):
    zero = jnp.zeros((2 * units, 128 - rows), BF)
    for layer in range(LAYERS):
        dst = packed if layer < 2 else later
        here = slice((layer % 2) * 2 * units, (layer % 2 + 1) * 2 * units)
        dst[here, 0:rows] = conv[layer].astype(BF)
        dst[here, rows:128] = zero
    core = jnp.bitwise_and(axis(DP), 1)
    for layer in range(LAYERS):
        full[layer, :, 0:HID] = res[LAYERS - 1 + layer].astype(BF)
        if layer < LAYERS - 1:
            full[layer, :, HID : 2 * HID] = res[layer].astype(BF)
    full[LAYERS - 1, :, HID : HID + C] = end[...].astype(BF)
    flat = jnp.concatenate([bias[layer] for layer in range(LAYERS)], axis=0).T
    hi = flat.astype(BF)
    lo = (flat - hi.astype(F32)).astype(BF)
    full[LAYERS - 1, :, HID + C : 2 * HID] = jnp.concatenate(
        [hi, lo, jnp.zeros((units, HID - C - 16), BF)], axis=1
    )
    for i in range(2):
        for c in range(3):
            lo = 4 * units + (3 * i + c) * units
            packed[lo : lo + units, :] = full[2 * core + i, :, c * 128 : (c + 1) * 128]
    for i in range(2):
        basis_out[i] = basis[2 * core + i].T.astype(BF)


def call_pack(rows, units, conv, res, end, bias, basis):
    return pl.pallas_call(
        functools.partial(pack_kernel, rows, units),
        out_shape=[
            jax.ShapeDtypeStruct((10 * units, 128), BF),
            jax.ShapeDtypeStruct((4 * units, 128), BF),
            jax.ShapeDtypeStruct((2, basis.shape[2], 2 * HID), BF),
        ],
        in_specs=[vm()] * 5,
        out_specs=[vm()] * 3,
        scratch_shapes=[pltpu.VMEM((LAYERS, units, 2 * HID), BF)],
        name="pack",
    )(conv, res, end, bias, basis)


def minor_det(m, r, left, right):
    return m[r, left] * m[r + 1, right] - m[r + 1, left] * m[r, right]


def consts_kernel(mix, lg, small, pre, a_hi, a_lo, at_b, cvec, pre_t, pre_b, ebias, mixfull, rows_out, extra):
    m = [[mix[i, j] for j in range(4)] for i in range(4)]
    ch_r = lax.broadcasted_iota(jnp.int32, (C, 1), 0)
    ch_c = lax.broadcasted_iota(jnp.int32, (1, C), 1)

    def pair(ch):
        return 2 * (ch >= HALF).astype(jnp.int32) + jnp.bitwise_and(ch, 1)

    def group(ch):
        return lax.shift_right_logical(ch - jnp.where(ch >= HALF, HALF, 0), 1)

    same = group(ch_r) == group(ch_c)
    pr, pc = pair(ch_r), pair(ch_c)
    full = jnp.zeros((C, C), F32)
    turned = jnp.zeros((C, C), F32)
    for p in range(4):
        row = jnp.zeros((1, C), F32)
        row_t = jnp.zeros((1, C), F32)
        for q in range(4):
            row = jnp.where(pc == q, m[p][q], row)
            row_t = jnp.where(pc == q, m[q][p], row_t)
        full = jnp.where(pr == p, row, full)
        turned = jnp.where(pr == p, row_t, turned)
    full = jnp.where(same, full, 0.0)
    turned = jnp.where(same, turned, 0.0)
    es = jnp.exp(small[0:1, :])
    at = full * es
    hi = at.astype(BF)
    a_hi[...] = hi
    a_lo[...] = (at - hi.astype(F32)).astype(BF)
    at_b[...] = (turned * to_column(es)).astype(BF)
    cvec[...] = jnp.sum(full * small[1:2, :], axis=1, keepdims=True)
    mixfull[...] = full
    pre_t[...] = pre[...].T.astype(BF)
    pre_b[...] = pre[...].astype(BF)
    ebias[...] = to_column(small[2:3, :])
    pairs = [(0, 1), (0, 2), (0, 3), (1, 2), (1, 3), (2, 3)]
    up = {ab: m[0][ab[0]] * m[1][ab[1]] - m[1][ab[0]] * m[0][ab[1]] for ab in pairs}
    dn = {ab: m[2][ab[0]] * m[3][ab[1]] - m[3][ab[0]] * m[2][ab[1]] for ab in pairs}
    det = (
        up[0, 1] * dn[2, 3]
        - up[0, 2] * dn[1, 3]
        + up[0, 3] * dn[1, 2]
        + up[1, 2] * dn[0, 3]
        - up[1, 3] * dn[0, 2]
        + up[2, 3] * dn[0, 1]
    )

    def minor3(i, j):
        cols = [c for c in range(4) if c != j]
        two = dn if i < 2 else up
        other = m[1 - i] if i < 2 else m[5 - i]
        return (
            other[cols[0]] * two[cols[1], cols[2]]
            - other[cols[1]] * two[cols[0], cols[2]]
            + other[cols[2]] * two[cols[0], cols[1]]
        )

    total = lg[0]
    for u in range(1, lg.shape[0]):
        total = total + lg[u]
    first = jnp.where(axis(TP) == 0, total, 0.0)
    det_v = jnp.full((8, 128), det, F32)
    r = lax.broadcasted_iota(jnp.int32, (8, 128), 0)
    c = lax.broadcasted_iota(jnp.int32, (8, 128), 1)
    cof = jnp.zeros((8, 128), F32)
    for i in range(4):
        for j in range(4):
            sign = 1.0 if (i + j) % 2 == 0 else -1.0
            cof = jnp.where(jnp.logical_and(r == i, c == j), sign * minor3(i, j), cof)
    extra[0:8, :] = first * (C // 4) * cof / det_v
    gain = jnp.sum(small[0:1, :], axis=1, keepdims=True)
    extra[8:16, :] = gain + (C // 4) * jnp.log(det_v)
    rows_out[...] = jnp.concatenate(
        [es, small[1:2, :], jnp.full((1, C), first, F32), jnp.zeros((5, C), F32)], axis=0
    )


def call_consts(mix, lg, small, pre):
    return pl.pallas_call(
        consts_kernel,
        out_shape=[
            jax.ShapeDtypeStruct((C, C), BF),
            jax.ShapeDtypeStruct((C, C), BF),
            jax.ShapeDtypeStruct((C, C), BF),
            jax.ShapeDtypeStruct((C, 1), F32),
            jax.ShapeDtypeStruct((HID, HALF), BF),
            jax.ShapeDtypeStruct((HALF, HID), BF),
            jax.ShapeDtypeStruct((C, 1), F32),
            jax.ShapeDtypeStruct((C, C), F32),
            jax.ShapeDtypeStruct((8, C), F32),
            jax.ShapeDtypeStruct((16, 128), F32),
        ],
        in_specs=[sm(), sm(), vm(), vm()],
        out_specs=[vm()] * 10,
        name="consts",
    )(mix, lg, small, pre)


def tap_stack(wide, size, reverse):
    half = KER // 2
    parts = []
    for k in range(KER):
        shift = half - k if not reverse else k - half
        moved = wide if shift == 0 else pltpu.roll(wide, shift % wide.shape[1], 1)
        parts.append(moved[:, 128 : 128 + size])
    return jnp.concatenate(parts, axis=0)


def make_masks(s, scal, t, w0):
    off, length, lg = scal
    o = column(off, jnp.int32)
    n = column(length, jnp.int32)
    pos = lax.broadcasted_iota(jnp.int32, (8, t), 1) + w0
    member = jnp.logical_and(pos >= o, pos < o + n).astype(F32)
    s.member[...] = member
    s.mask[...] = jnp.broadcast_to(jnp.sum(member, axis=0, keepdims=True), (8, t))
    return column(lg, F32) / n.astype(F32)


def zero_edges(ref, lead, t):
    for slot in lead:
        at = ref if slot is None else ref.at[slot]
        z = jnp.zeros((at.shape[0], 128), BF)
        at[:, 0:128] = z
        at[:, t + 128 : t + 256] = z


def mixed_of(w, fr, mask):
    return (nn(w.a_hi[...], fr) + nn(w.a_lo[...], fr) + w.cvec[...]) * mask


def unpack_conv(tp, rows, owners, dp, scratch, wt):
    me_tp, me_dp = axis(TP), axis(DP)
    units = HID // tp

    def layer_body(layer, carry):
        for b in range(dp):
            m = jnp.bitwise_xor(me_dp, owners[b])
            for kk in range(tp):
                src = from_left(me_tp, kk, tp)
                for h in range(2):
                    row = pl.ds(pl.multiple_of(src * units + h * HID, 16), units)
                    lo = pl.multiple_of(layer * 2 * units + h * units, 16)
                    wt[layer, row, b * rows : (b + 1) * rows] = scratch[m, kk, pl.ds(lo, units), 0:rows]
        return carry

    lax.fori_loop(0, 2, layer_body, 0)


def unpack_res(tp, res_pieces, rsb, rsf, end, end_t, bias, scr):
    me_tp = axis(TP)
    core = jnp.bitwise_and(axis(DP), 1)
    units = HID // tp
    for kk in range(tp):
        for i in range(2):
            for c in range(3):
                lo = (3 * i + c) * units
                lanes = slice(c * 128, (c + 1) * 128)
                scr[kk, 2 * core + i, :, lanes] = res_pieces[0][kk, lo : lo + units, :]
                scr[kk, 2 * (1 - core) + i, :, lanes] = res_pieces[1][kk, lo : lo + units, :]
    res_pieces = [scr.at[kk] for kk in range(tp)]
    for kk in range(tp):
        src = from_left(me_tp, kk, tp)
        row = pl.ds(pl.multiple_of(src * units, 16), units)
        for layer in range(LAYERS - 1):
            rsb[layer, row, :] = res_pieces[kk][layer]
        last = res_pieces[kk][LAYERS - 1]
        rsb[LAYERS - 1, row, 0:HID] = last[:, 0:HID]
        rsb[LAYERS - 1, row, HID : 2 * HID] = jnp.zeros((units, HID), BF)
        end[row, :] = last[:, HID : HID + C]
        tail = last[:, HID + C : 2 * HID].astype(F32)
        for layer in range(LAYERS):
            for h in range(2):
                i = layer * 2 + h
                at = pl.ds(pl.multiple_of(src * units + h * HID, 16), units)
                bias[layer, at, :] = tail[:, i : i + 1] + tail[:, 8 + i : 9 + i]
    for layer in range(LAYERS):
        rsf[layer, 0:HID, :] = rsb[layer, :, HID : 2 * HID].astype(F32).T.astype(BF)
        rsf[layer, HID : 2 * HID, :] = rsb[layer, :, 0:HID].astype(F32).T.astype(BF)
    end_t[...] = end[...].astype(F32).T.astype(BF)


def forward_layer(s, t, wt, rsf, bias, mask, here, after, save, before_skip=None):
    g = nn(wt, tap_stack(s.hb[here], t, False)) + bias
    tt = jnp.tanh(g[0:HID])
    ss = sigmoid(g[HID : 2 * HID])
    act = (tt * ss).astype(BF)
    y = nn(rsf, act)
    if before_skip is not None:
        before_skip()
    s.skip[...] += y[HID : 2 * HID]
    hv = (s.h[...] + y[0:HID]) * mask
    s.h[...] = hv
    if save is not None:
        s.tt[save] = tt.astype(BF)
        s.ss[save] = ss.astype(BF)
    s.hb[after, :, 128 : t + 128] = hv.astype(BF)


def start_hidden(s, t, w, mixed, mask):
    hv = nn(w.pre_t[...], mixed[0:HALF].astype(BF)) * mask
    s.h[...] = hv
    s.hb[0, :, 128 : t + 128] = hv.astype(BF)
    s.skip[...] = jnp.zeros((HID, t), F32)


def window_tail(own, t, w, s, mixed, mask, weight, dpp=None):
    skip_low = (s.skip[...] * mask).astype(BF)
    proj = nn(w.end_t[...], skip_low) + w.ebias[...]
    shift = proj[0:HALF]
    log_scale = proj[HALF:C]
    e = jnp.exp(log_scale)
    x0 = mixed[0:HALF]
    x1 = mixed[HALF:C]
    s.fo[0:HALF, :] = x0
    s.fo[HALF:C, :] = (shift + e * x1) * mask
    s.pf[...] = jnp.broadcast_to(jnp.sum(log_scale, axis=0, keepdims=True), (8, t))
    og = s.og[...].astype(F32)
    d_shift = og[HALF:C] * mask
    de = d_shift * e
    first = og[0:HALF] * mask
    if not own and dpp is not None:
        first = first + dpp
    dm = jnp.concatenate([first, de], axis=0).astype(BF)
    if not own:
        s.p1[...] = nn(w.at_b[...], dm)
    if own:
        s.dm[...] = dm
        s.x0b[...] = x0.astype(BF)
        fw = jnp.sum(s.member[...] * weight, axis=0, keepdims=True)
        d_log = de * x1 + fw
        d_proj = jnp.concatenate([d_shift, d_log], axis=0).astype(BF)
        s.dproj[...] = d_proj
        s.skl[...] = skip_low
        s.dsk[...] = (nn(w.end[...], d_proj) * mask).astype(BF)


def logdet_part(s, own):
    part = jnp.sum(s.member[:, own] * s.pf[:, own], axis=1, keepdims=True)
    return jnp.broadcast_to(part, (8, 128))


def backward_layer(s, t, layer, slot, own, own_in, own_len, wt, rsb, mask, ones, put_rs, put_conv):
    carried = s.h[...] * mask
    s.h[...] = carried
    s.d[0:HID, :] = s.dsk[...]
    s.d[HID : 2 * HID, :] = carried.astype(BF)
    da = nn(rsb[layer], s.d[...])
    tt = s.tt[slot].astype(F32)
    ss = s.ss[slot].astype(F32)
    das = da * ss
    s.dg[0:HID, 128 : t + 128] = (das * (1.0 - tt * tt)).astype(BF)
    s.dg[HID : 2 * HID, 128 : t + 128] = (das * tt * (1.0 - ss)).astype(BF)
    act = (s.tt[slot, :, own].astype(F32) * s.ss[slot, :, own].astype(F32)).astype(BF)
    put_rs(layer, nt(act, s.d[:, own]))
    s.smallg[pl.ds(layer, 1), :] = nt(ones, s.dg[:, own_in])[0:1]
    wide = s.hb[slot, :, pl.ds(pl.multiple_of(own_in.start - 128, 128), own_len + 256)]
    s.dw[:, 0 : KER * HID] = nt(s.dg[:, own_in], tap_stack(wide, own_len, False))
    put_conv(slot)
    for k in range(KER):
        s.wd[:, k * 2 * HID : (k + 1) * 2 * HID] = (
            wt[slot, :, k * HID : (k + 1) * HID].astype(F32).T.astype(BF)
        )
    s.h[...] += nn(s.wd[...], tap_stack(s.dg[...], t, True))


def rs_writer(tp, osend, units):
    me_tp, me_dp = axis(TP), axis(DP)
    core = jnp.bitwise_and(me_dp, 1)
    slots = [jnp.bitwise_xor(q, me_tp) for q in range(tp)]

    def put(layer, value):
        half = jnp.where(layer == LAYERS - 1, 1 - core, core)
        row = pl.multiple_of(lax.rem(layer, LAYERS - 1) * units, 16)
        for q in range(tp):
            osend[half, slots[q], pl.ds(row, units), :] = value[q * units : (q + 1) * units].astype(BF)

    return put, slots, 1 - core


def conv_writer(dp, rows, owners, gsend, dw):
    me_dp = axis(DP)
    bits = (dp - 1).bit_length()

    def put(slot):
        if dp * 128 <= MAX_PACKED:
            for b in range(dp):
                p = bit_reverse(jnp.bitwise_xor(me_dp, owners[b]), bits)
                gsend[p, slot, :, 0:rows] = dw[:, b * rows : (b + 1) * rows].astype(BF)
        else:
            gsend[slot] = dw[:, 0 : KER * HID].astype(BF)

    return put


def place(own_len, t, frames, q):
    start = q * own_len
    w0 = jnp.clip(start - HALO, 0, frames - t)
    return pl.multiple_of(w0, 128), pl.multiple_of(start - w0, 128), pl.multiple_of(start, 128)


BASE_W = names_of(lambda w: (w.a_hi, w.a_lo, w.cvec, w.pre_t,))
TAIL_W = names_of(lambda w: (w.a_hi, w.a_lo, w.cvec, w.end_t, w.ebias, w.at_b,))


def own_forward_kernel(dp, tp, rows, own_len, t, frames, npiece, snames, owners, off, length, lg, *refs):
    w = space(BASE_W, refs)
    refs = refs[len(BASE_W) :]
    fr_any = refs[0]
    pieces = refs[1 : 1 + npiece]
    res_pieces = refs[1 + npiece : 3 + npiece]
    outs = refs[3 + npiece :]
    wt_any, rsb, rsf, end, end_t, bias, h_any, skip_any, hb_any, tt_any, ss_any = outs[:11]
    s = space(snames, outs[11:-2])
    piece_sem, sem = outs[-2:]
    w0, _, _ = place(own_len, t, frames, axis(TP))
    copies = [pltpu.make_async_copy(pieces[m], s.pieces.at[m], piece_sem.at[m]) for m in range(npiece)]
    load = pltpu.make_async_copy(fr_any.at[:, pl.ds(w0, t)], s.fr, sem.at[0])
    load.start()
    for c in copies:
        c.start()
    make_masks(s, (off, length, lg), t, w0)
    zero_edges(s.hb, range(3), t)
    unpack_res(tp, res_pieces, rsb, rsf, end, end_t, bias, s.res)
    load.wait()
    mask = s.mask[0:1, :]
    start_hidden(s, t, w, mixed_of(w, s.fr[...], mask), mask)
    for c in copies:
        c.wait()
    if npiece > 1:
        unpack_conv(tp, rows, owners, dp, s.pieces, s.wt)
    else:
        s.wt[...] = s.pieces[0]
    stores = [pltpu.make_async_copy(s.wt, wt_any, sem.at[6])]
    stores[0].start()

    def kept(layer):
        return [
            pltpu.make_async_copy(s.hb.at[layer], hb_any.at[layer], sem.at[7 + layer]),
            pltpu.make_async_copy(s.tt.at[layer], tt_any.at[layer], sem.at[9 + layer]),
            pltpu.make_async_copy(s.ss.at[layer], ss_any.at[layer], sem.at[11 + layer]),
        ]

    def layer_body(layer, carry):
        forward_layer(s, t, s.wt[layer], rsf[layer], bias[layer], s.mask[0:1, :], layer, layer + 1, layer)
        for c in kept(layer):
            c.start()
        return carry

    lax.fori_loop(0, 2, layer_body, 0)
    last = [
        pltpu.make_async_copy(s.h, h_any, sem.at[1]),
        pltpu.make_async_copy(s.skip, skip_any, sem.at[2]),
    ]
    for c in last:
        c.start()
    for c in stores + last + kept(0) + kept(1):
        c.wait()


def call_own_forward(dp, tp, rows, own_len, frames, scal, w, fr, pieces, res_pieces):
    t = min(own_len + 2 * HALO, frames)
    sc = dict(
        member=pltpu.VMEM((8, t), F32),
        mask=pltpu.VMEM((8, t), F32),
        fr=pltpu.VMEM((C, t), BF),
        h=pltpu.VMEM((HID, t), F32),
        skip=pltpu.VMEM((HID, t), F32),
        hb=pltpu.VMEM((3, HID, t + 256), BF),
        tt=pltpu.VMEM((2, HID, t), BF),
        ss=pltpu.VMEM((2, HID, t), BF),
        pieces=pltpu.VMEM((len(pieces),) + pieces[0].shape, BF),
        res=pltpu.VMEM((tp, LAYERS, HID // tp, 2 * HID), BF),
        wt=pltpu.VMEM((2, 2 * HID, KER * HID), BF),
    )
    sds = jax.ShapeDtypeStruct
    return pl.pallas_call(
        functools.partial(own_forward_kernel, dp, tp, rows, own_len, t, frames, len(pieces), list(sc)),
        out_shape=[
            sds((2, 2 * HID, KER * HID), BF),
            sds((LAYERS, HID, 2 * HID), BF),
            sds((LAYERS, 2 * HID, HID), BF),
            sds((HID, C), BF),
            sds((C, HID), BF),
            sds((LAYERS, 2 * HID, 1), F32),
            sds((HID, t), F32),
            sds((HID, t), F32),
            sds((2, HID, t + 256), BF),
            sds((2, HID, t), BF),
            sds((2, HID, t), BF),
        ],
        in_specs=[sm()] * 4 + [vm()] * len(BASE_W) + [hb()] * (1 + len(pieces)) + [vm()] * 2,
        out_specs=[hb()] + [vm()] * 5 + [hb()] * 5,
        scratch_shapes=list(sc.values())
        + [pltpu.SemaphoreType.DMA((len(pieces),)), pltpu.SemaphoreType.DMA((13,))],
        compiler_params=pltpu.CompilerParams(vmem_limit_bytes=VMEM_BYTES),
        cost_estimate=pl.CostEstimate(flops=1000, bytes_accessed=1000, transcendentals=0),
        name="ownfwd",
    )(*scal, *[getattr(w, k) for k in BASE_W], fr, *pieces, *res_pieces)


def conv_shape(dp):
    return (dp, LAYERS, 2 * HID, 128) if dp * 128 <= MAX_PACKED else (LAYERS, 2 * HID, KER * HID)


MID_W = names_of(lambda w: (w.a_hi, w.a_lo, w.cvec, w.end_t, w.ebias, w.at_b, w.end, w.rsf, w.bias,))
MID_STATE = names_of(lambda w: (w.hb, w.tt, w.ss, w.dsk, w.dm, w.x0b,))


def own_middle_kernel(dp, tp, rows, own_len, t, frames, npiece, snames, owners, off, length, lg, *refs):
    w = space(MID_W, refs)
    refs = refs[len(MID_W) :]
    fr_any, og_any, h_in, skip_in = refs[:4]
    pieces = refs[4 : 4 + npiece]
    refs = refs[4 + npiece :]
    wt_any, fo_any, result, d_end_out, ebias_out = refs[:5]
    state = space(MID_STATE, refs[5:11])
    s = space(snames, refs[11:-2])
    piece_sem, sem = refs[-2:]
    w0, off_own, start = place(own_len, t, frames, axis(TP))
    copies = [pltpu.make_async_copy(pieces[m], s.pieces.at[m], piece_sem.at[m]) for m in range(npiece)]
    loads = [
        pltpu.make_async_copy(h_in, s.h, sem.at[0]),
        pltpu.make_async_copy(skip_in, s.skip, sem.at[1]),
        pltpu.make_async_copy(fr_any.at[:, pl.ds(w0, t)], s.fr, sem.at[2]),
        pltpu.make_async_copy(og_any.at[:, pl.ds(w0, t)], s.og, sem.at[3]),
    ]
    for c in loads[:1] + copies + loads[1:]:
        c.start()
    weight = make_masks(s, (off, length, lg), t, w0)
    zero_edges(s.hb, range(3), t)
    loads[0].wait()
    s.hb[0, :, 128 : t + 128] = s.h[...].astype(BF)
    for c in copies:
        c.wait()
    if npiece > 1:
        unpack_conv(tp, rows, owners, dp, s.pieces, s.wt)
    else:
        s.wt[...] = s.pieces[0]
    stores = [pltpu.make_async_copy(s.wt, wt_any, sem.at[11])]
    stores[0].start()

    def kept(layer):
        return [
            pltpu.make_async_copy(s.hb.at[layer], state.hb.at[layer], sem.at[12 + layer]),
            pltpu.make_async_copy(s.tt.at[layer], state.tt.at[layer], sem.at[14 + layer]),
            pltpu.make_async_copy(s.ss.at[layer], state.ss.at[layer], sem.at[16 + layer]),
        ]

    def layer_body(i, carry):
        def skip_here():
            @pl.when(i == 0)
            def _():
                loads[1].wait()

        forward_layer(
            s, t, s.wt[i], w.rsf[i + 2], w.bias[i + 2], s.mask[0:1, :], i, i + 1, i, skip_here
        )
        for c in kept(i):
            c.start()
        return carry

    lax.fori_loop(0, 2, layer_body, 0)
    for c in loads[2:]:
        c.wait()
    mask = s.mask[0:1, :]
    window_tail(True, t, w, s, mixed_of(w, s.fr[...], mask), mask, weight)
    own = pl.ds(off_own, own_len)
    more = [
        pltpu.make_async_copy(s.fo.at[:, own], fo_any.at[:, pl.ds(start, own_len)], sem.at[4]),
        pltpu.make_async_copy(s.dsk, state.dsk, sem.at[8]),
        pltpu.make_async_copy(s.dm, state.dm, sem.at[9]),
        pltpu.make_async_copy(s.x0b, state.x0b, sem.at[10]),
    ]
    for c in more:
        c.start()
    result[0:HALF, :] = s.fo[HALF:C, own].astype(BF)
    result[HALF:C, :] = s.dm[HALF:C, own]
    ld = logdet_part(s, own)
    hi = ld.astype(BF)
    lo = (ld - hi.astype(F32)).astype(BF)
    result[C : C + 16, 0:128] = jnp.concatenate([hi, lo], axis=0)
    ones = jnp.ones((8, own_len), BF)
    d_end_out[...] = nt(s.skl[:, own], s.dproj[:, own])
    ebias_out[...] = nt(ones, s.dproj[:, own])
    for c in stores + more + kept(0) + kept(1):
        c.wait()


def call_own_middle(dp, tp, rows, own_len, frames, scal, w, fr, og, h, skip, pieces):
    t = min(own_len + 2 * HALO, frames)
    sc = dict(
        member=pltpu.VMEM((8, t), F32),
        mask=pltpu.VMEM((8, t), F32),
        pf=pltpu.VMEM((8, t), F32),
        fr=pltpu.VMEM((C, t), BF),
        og=pltpu.VMEM((C, t), BF),
        h=pltpu.VMEM((HID, t), F32),
        skip=pltpu.VMEM((HID, t), F32),
        fo=pltpu.VMEM((C, t), F32),
        hb=pltpu.VMEM((3, HID, t + 256), BF),
        tt=pltpu.VMEM((2, HID, t), BF),
        ss=pltpu.VMEM((2, HID, t), BF),
        pieces=pltpu.VMEM((len(pieces),) + pieces[0].shape, BF),
        dm=pltpu.VMEM((C, t), BF),
        x0b=pltpu.VMEM((HALF, t), BF),
        dproj=pltpu.VMEM((C, t), BF),
        skl=pltpu.VMEM((HID, t), BF),
        dsk=pltpu.VMEM((HID, t), BF),
        wt=pltpu.VMEM((2, 2 * HID, KER * HID), BF),
    )
    sds = jax.ShapeDtypeStruct
    return pl.pallas_call(
        functools.partial(own_middle_kernel, dp, tp, rows, own_len, t, frames, len(pieces), list(sc)),
        out_shape=[
            sds((2, 2 * HID, KER * HID), BF),
            sds((C, frames), F32),
            sds((C + 16, own_len), BF),
            sds((HID, C), F32),
            sds((8, C), F32),
            sds((2, HID, t + 256), BF),
            sds((2, HID, t), BF),
            sds((2, HID, t), BF),
            sds((HID, t), BF),
            sds((C, t), BF),
            sds((HALF, t), BF),
        ],
        in_specs=[sm()] * 4 + [vm()] * len(MID_W) + [hb()] * (4 + len(pieces)),
        out_specs=[hb(), hb(), vm(), vm(), vm()] + [hb()] * 6,
        scratch_shapes=list(sc.values())
        + [pltpu.SemaphoreType.DMA((len(pieces),)), pltpu.SemaphoreType.DMA((18,))],
        compiler_params=pltpu.CompilerParams(vmem_limit_bytes=VMEM_BYTES),
        cost_estimate=pl.CostEstimate(flops=1000, bytes_accessed=1000, transcendentals=0),
        name="ownmid",
    )(*scal, *[getattr(w, k) for k in MID_W], fr, og, h, skip, *pieces)


ASM_W = names_of(lambda w: (w.a_hi, w.a_lo, w.cvec, w.at_b,))


def assemble_kernel(tp, kks, turn, own_len, snames, off, length, lg, *refs):
    w = space(ASM_W, refs)
    refs = refs[len(ASM_W) :]
    n = len(kks)
    dpps, results = refs[:n], refs[n : 2 * n]
    fr_any, og_any, merged, _, fg_in = refs[2 * n : 2 * n + 5]
    fo_any, fg_any = refs[2 * n + 5 : 2 * n + 7]
    s = space(snames, refs[2 * n + 7 : -1])
    sem = refs[-1]
    half = slice(0, HALF)
    blocks = own_len // 128
    turned = pl.ds(pl.multiple_of(from_left(axis(TP), turn, tp) * own_len, 128), own_len)
    tail = [
        pltpu.make_async_copy(merged.at[pl.ds(0, blocks * HALF)], s.dpp, sem.at[n, 0]),
        pltpu.make_async_copy(fg_in.at[:, turned], s.part, sem.at[n, 1]),
    ]
    starts = [pl.multiple_of(from_left(axis(TP), kk, tp) * own_len, 128) for kk in kks]
    loads = [
        [
            pltpu.make_async_copy(fr_any.at[:, pl.ds(start, own_len)], s.fr.at[i], sem.at[i, 0]),
            pltpu.make_async_copy(og_any.at[pl.ds(0, HALF), pl.ds(start, own_len)], s.og.at[i], sem.at[i, 1]),
            pltpu.make_async_copy(results[i].at[pl.ds(0, C)], s.result.at[i], sem.at[i, 2]),
        ]
        for i, start in enumerate(starts)
    ]
    for group in loads + [tail]:
        for c in group:
            c.start()
    stores = []
    for i, start in enumerate(starts):
        make_masks(s, (off, length, lg), own_len, start)
        for c in loads[i]:
            c.wait()
        mask = s.mask[0:1, :]
        fr = s.fr[i]
        where = pl.ds(start, own_len)
        s.fo[i, 0:HALF, :] = (nn(w.a_hi[half, :], fr) + nn(w.a_lo[half, :], fr) + w.cvec[half, :]) * mask
        s.fo[i, HALF:C, :] = s.result[i, 0:HALF, :].astype(F32)
        stores += [pltpu.make_async_copy(s.fo.at[i], fo_any.at[:, where], sem.at[i, 3])]
        stores[-1].start()
        first = s.og[i].astype(F32) * mask + dpps[i][...].astype(F32)
        dm = jnp.concatenate([first.astype(BF), s.result[i, HALF:C, :]], axis=0)
        s.fg[i] = nn(w.at_b[...], dm)
        stores += [pltpu.make_async_copy(s.fg.at[i], fg_any.at[:, where], sem.at[i, 4])]
        stores[-1].start()
    for c in tail:
        c.wait()
    dpp = jnp.concatenate([s.dpp[j * HALF : (j + 1) * HALF, :] for j in range(blocks)], axis=1)
    s.part[...] += nn(w.at_b[:, half], dpp)
    stores += [pltpu.make_async_copy(s.part, fg_any.at[:, turned], sem.at[n, 2])]
    stores[-1].start()
    for c in stores:
        c.wait()


def call_assemble(tp, kks, turn, own_len, scal, w, results, dpps, fr, og, merged, fo, fg):
    n = len(kks)
    sc = dict(
        member=pltpu.VMEM((8, own_len), F32),
        mask=pltpu.VMEM((8, own_len), F32),
        fr=pltpu.VMEM((n, C, own_len), BF),
        og=pltpu.VMEM((n, HALF, own_len), BF),
        result=pltpu.VMEM((n, C, own_len), BF),
        fo=pltpu.VMEM((n, C, own_len), F32),
        fg=pltpu.VMEM((n, C, own_len), F32),
        dpp=pltpu.VMEM((own_len // 128 * HALF, 128), BF),
        part=pltpu.VMEM((C, own_len), F32),
    )
    base = 3 + len(ASM_W) + 2 * n + 3
    return pl.pallas_call(
        functools.partial(assemble_kernel, tp, kks, turn, own_len, list(sc)),
        out_shape=[jax.ShapeDtypeStruct(fo.shape, F32), jax.ShapeDtypeStruct(fg.shape, F32)],
        in_specs=[sm()] * 3 + [vm()] * (len(ASM_W) + n) + [hb()] * (n + 5),
        out_specs=[hb(), hb()],
        input_output_aliases={base: 0, base + 1: 1},
        scratch_shapes=list(sc.values()) + [pltpu.SemaphoreType.DMA((n + 1, 5))],
        compiler_params=pltpu.CompilerParams(vmem_limit_bytes=VMEM_BYTES),
        cost_estimate=pl.CostEstimate(flops=1000, bytes_accessed=1000, transcendentals=0),
        name="assemble",
    )(*scal[1:], *[getattr(w, k) for k in ASM_W], *dpps, *results, fr, og, merged, fo, fg)


LAST_W = names_of(lambda w: (w.rsb, w.pre_b, w.mixfull, w.rows, w.extra, w.at_b, w.d_end, w.d_ebias))


def own_last_kernel(dp, tp, rows, own_len, t, frames, snames, owners, off, length, lg, *refs):
    w = space(LAST_W, refs)
    refs = refs[len(LAST_W) :]
    fr_any, dsk_in, dm_in, x0_in = refs[:4]
    by_layer = [refs[4:8], refs[8:12]]
    gkeep, gsend, okeep, osend_out, dpp, fg_any = refs[12:18]
    s = space(snames, refs[18:-2])
    osend = s.o
    layer_sem, sem = refs[-2:]
    units = HID // tp
    w0, off_own, start = place(own_len, t, frames, axis(TP))
    into = [s.wt, s.tt, s.ss, s.hb]
    first = pltpu.make_async_copy(dsk_in, s.dsk, sem.at[0])
    first.start()
    for layer in reversed(range(LAYERS)):
        for i in (1, 2, 3, 0):
            pltpu.make_async_copy(
                by_layer[layer // 2][i].at[layer % 2], into[i].at[layer], layer_sem.at[i, layer]
            ).start()
    loads = [
        pltpu.make_async_copy(fr_any.at[:, pl.ds(start, own_len)], s.fr, sem.at[5]),
        pltpu.make_async_copy(dm_in, s.dm, sem.at[6]),
        pltpu.make_async_copy(x0_in, s.x0b, sem.at[7]),
    ]
    for c in loads:
        c.start()
    make_masks(s, (off, length, lg), t, w0)
    zero_edges(s.dg, [None], t)
    own = pl.ds(off_own, own_len)
    own_in = pl.ds(pl.multiple_of(off_own + 128, 128), own_len)
    ones = jnp.ones((8, own_len), BF)
    s.smallg[...] = jnp.zeros((16, 2 * HID), F32)
    s.smallg[6:7, 0:C] = w.d_ebias[0:1]
    put_rs, slots, high = rs_writer(tp, osend, units)
    for q in range(tp):
        osend[high, slots[q], units : 2 * units, 0:C] = w.d_end[q * units : (q + 1) * units].astype(BF)
    put_conv = conv_writer(dp, rows, owners, s.g, s.dw)
    s.h[...] = jnp.zeros((HID, t), F32)
    first.wait()

    def back_body(i, carry):
        layer = LAYERS - 1 - i
        for kind in range(4):
            pltpu.make_async_copy(
                by_layer[0][kind].at[0], into[kind].at[layer], layer_sem.at[kind, layer]
            ).wait()
        backward_layer(
            s, t, layer, layer, own, own_in, own_len, s.wt, w.rsb, s.mask[0:1, :], ones, put_rs, put_conv
        )
        return carry

    lax.fori_loop(0, LAYERS, back_body, 0)
    for c in loads:
        c.wait()
    stores = []
    half = s.g.shape[0] // 2
    for ref, lo, i in ((gkeep, 0, 8), (gsend, half, 9)):
        stores += [pltpu.make_async_copy(s.g.at[pl.ds(lo, half)], ref, sem.at[i])]
        stores[-1].start()
    smallg = s.smallg
    d_pre = (s.h[:, own] * s.mask[0:1, own]).astype(BF)
    dpp_v = nn(w.pre_b[...], d_pre).astype(BF)
    dpp[...] = dpp_v
    d_prew = nt(s.x0b[:, own], d_pre)
    dm = s.dm[:, own]
    total = jnp.concatenate([dm[0:HALF].astype(F32) + dpp_v.astype(F32), dm[HALF:C].astype(F32)], axis=0)
    s.fg[...] = nn(w.at_b[...], total.astype(BF))
    stores += [pltpu.make_async_copy(s.fg, fg_any.at[:, pl.ds(start, own_len)], sem.at[10])]
    stores[-1].start()
    fr = s.fr[...]
    qd = nt(dm, fr)
    q0 = nt(dpp_v, fr)
    qd = jnp.concatenate([qd[0:HALF] + q0, qd[HALF:C]], axis=0)
    v = jnp.sum(dm.astype(F32), axis=1, keepdims=True)
    v0 = jnp.sum(dpp_v.astype(F32), axis=1, keepdims=True)
    v = jnp.concatenate([v[0:HALF] + v0, v[HALF:C]], axis=0)
    mixfull = w.mixfull[...]
    es = w.rows[0:1, :]
    bb = w.rows[1:2, :]
    smallg[4:5, 0:C] = es * jnp.sum(mixfull * qd, axis=0, keepdims=True) + w.rows[2:3, :]
    smallg[5:6, 0:C] = jnp.sum(mixfull * v, axis=0, keepdims=True)
    ch_r = lax.broadcasted_iota(jnp.int32, (C, 1), 0)
    ch_c = lax.broadcasted_iota(jnp.int32, (1, C), 1)

    def group(ch):
        return lax.shift_right_logical(ch - jnp.where(ch >= HALF, HALF, 0), 1)

    d2 = jnp.where(group(ch_r) == group(ch_c), v * bb + es * qd, 0.0)
    wide = lax.broadcasted_iota(jnp.int32, (C, 128), 1)
    chan = lax.broadcasted_iota(jnp.int32, (C, 128), 0)
    pair = 2 * (chan >= HALF).astype(jnp.int32) + jnp.bitwise_and(chan, 1)
    one_hot = (pair == wide).astype(F32)
    part = tn(one_hot, d2, PRECISE)
    smallg[8:16, 0:128] = nn(part, one_hot, PRECISE)[0:8] + w.extra[0:8, :]
    small = smallg[...]
    for q in range(tp):
        osend[high, slots[q], units : units + HALF, HID : 2 * HID] = d_prew.astype(BF)
        for h in range(2):
            osend[high, slots[q], 3 * units - 16 : 3 * units, h * units : (h + 1) * units] = small[
                :, h * HID + q * units : h * HID + (q + 1) * units
            ].astype(BF)
        osend[high, slots[q], 3 * units - 12 : 3 * units, 0:C] = small[4:16, 0:C].astype(BF)
    for ref, i in ((okeep, 11), (osend_out, 12)):
        stores += [pltpu.make_async_copy(osend.at[i - 11], ref, sem.at[i])]
        stores[-1].start()
    for c in stores:
        c.wait()


def call_own_last(dp, tp, rows, own_len, frames, scal, w, fr, dsk, dm, x0, kept_a, kept_b):
    shape = conv_shape(dp)
    t = min(own_len + 2 * HALO, frames)
    units = HID // tp
    sc = dict(
        member=pltpu.VMEM((8, t), F32),
        mask=pltpu.VMEM((8, t), F32),
        fr=pltpu.VMEM((C, own_len), BF),
        h=pltpu.VMEM((HID, t), F32),
        wt=pltpu.VMEM((LAYERS, 2 * HID, KER * HID), BF),
        hb=pltpu.VMEM((LAYERS, HID, t + 256), BF),
        tt=pltpu.VMEM((LAYERS, HID, t), BF),
        ss=pltpu.VMEM((LAYERS, HID, t), BF),
        dm=pltpu.VMEM((C, t), BF),
        x0b=pltpu.VMEM((HALF, t), BF),
        dsk=pltpu.VMEM((HID, t), BF),
        d=pltpu.VMEM((2 * HID, t), BF),
        dg=pltpu.VMEM((2 * HID, t + 256), BF),
        dw=pltpu.VMEM((2 * HID, 1024), F32),
        wd=pltpu.VMEM((HID, 2 * KER * HID), BF),
        smallg=pltpu.VMEM((16, 2 * HID), F32),
        g=pltpu.VMEM(shape, BF),
        o=pltpu.VMEM((2, tp, 3 * units, 2 * HID), BF),
        fg=pltpu.VMEM((C, own_len), F32),
    )
    sds = jax.ShapeDtypeStruct
    return pl.pallas_call(
        functools.partial(own_last_kernel, dp, tp, rows, own_len, t, frames, list(sc)),
        out_shape=[
            sds((shape[0] // 2,) + shape[1:], BF),
            sds((shape[0] // 2,) + shape[1:], BF),
            sds((tp, 3 * units, 2 * HID), BF),
            sds((tp, 3 * units, 2 * HID), BF),
            sds((HALF, own_len), BF),
            sds((C, frames), F32),
        ],
        in_specs=[sm()] * 4 + [vm()] * len(LAST_W) + [hb()] * 12,
        out_specs=[hb(), hb(), hb(), hb(), vm(), hb()],
        scratch_shapes=list(sc.values()) + [pltpu.SemaphoreType.DMA((4, LAYERS)), pltpu.SemaphoreType.DMA((13,))],
        compiler_params=pltpu.CompilerParams(vmem_limit_bytes=VMEM_BYTES),
        cost_estimate=pl.CostEstimate(flops=1000, bytes_accessed=1000, transcendentals=0),
        name="ownlast",
    )(*scal, *[getattr(w, k) for k in LAST_W], fr, dsk, dm, x0, *kept_a, *kept_b)


FWD_W = names_of(lambda w: (w.a_hi, w.a_lo, w.cvec, w.pre_t, w.end_t, w.ebias, w.at_b, w.wt_a, w.wt_b, w.rsf, w.bias,))


def fwd_kernel(tp, kk, own_len, t, frames, has_dpp, snames, off, length, lg, *refs):
    w = space(FWD_W, refs)
    refs = refs[len(FWD_W) :]
    fr_any, og_any = refs[:2]
    nd = 1 if has_dpp else 0
    fo_any, p1_any, ld = refs[4 + nd : 7 + nd]
    s = space(snames, refs[7 + nd : -1])
    sem = refs[-1]
    w0, off_own, start = place(own_len, t, frames, from_left(axis(TP), kk, tp))
    dpp = None
    if has_dpp:
        s.dpp[...] = jnp.zeros((HALF, t), BF)
        s.dpp[:, pl.ds(off_own, own_len)] = refs[4][...]
        dpp = s.dpp
    c0 = pltpu.make_async_copy(fr_any.at[:, pl.ds(w0, t)], s.fr, sem.at[0])
    c1 = pltpu.make_async_copy(og_any.at[:, pl.ds(w0, t)], s.og, sem.at[1])
    c0.start()
    c1.start()
    make_masks(s, (off, length, lg), t, w0)
    zero_edges(s.hb, range(2), t)
    c0.wait()
    mask = s.mask[0:1, :]
    mixed = mixed_of(w, s.fr[...], mask)
    s.mixed[...] = mixed
    start_hidden(s, t, w, mixed, mask)
    for half in range(2):
        wt = w.wt_a if half == 0 else w.wt_b

        def layer_body(i, carry):
            layer = 2 * half + i
            forward_layer(
                s, t, wt[i], w.rsf[layer], w.bias[layer], s.mask[0:1, :], i, 1 - i, None
            )
            return carry

        lax.fori_loop(0, 2, layer_body, 0)
    c1.wait()
    dpp = None if dpp is None else dpp[...].astype(F32)
    window_tail(False, t, w, s, s.mixed[...], s.mask[0:1, :], None, dpp)
    own = pl.ds(off_own, own_len)
    o0 = pltpu.make_async_copy(s.fo.at[:, own], fo_any.at[:, pl.ds(start, own_len)], sem.at[2])
    o1 = pltpu.make_async_copy(s.p1.at[:, own], p1_any.at[:, pl.ds(start, own_len)], sem.at[3])
    o0.start()
    o1.start()
    ld[...] = logdet_part(s, own)
    o0.wait()
    o1.wait()


def call_fwd(tp, kk, own_len, frames, scal, w, fr, og, fo, p1, dpp=None):
    t = min(own_len + 2 * HALO, frames)
    sc = dict(
        member=pltpu.VMEM((8, t), F32),
        mask=pltpu.VMEM((8, t), F32),
        pf=pltpu.VMEM((8, t), F32),
        fr=pltpu.VMEM((C, t), BF),
        og=pltpu.VMEM((C, t), BF),
        mixed=pltpu.VMEM((C, t), F32),
        h=pltpu.VMEM((HID, t), F32),
        skip=pltpu.VMEM((HID, t), F32),
        fo=pltpu.VMEM((C, t), F32),
        p1=pltpu.VMEM((C, t), F32),
        hb=pltpu.VMEM((2, HID, t + 256), BF),
    )
    n = len(FWD_W)
    more = [] if dpp is None else [dpp]
    if more:
        sc.update(dpp=pltpu.VMEM((HALF, t), BF))
    return pl.pallas_call(
        functools.partial(fwd_kernel, tp, kk, own_len, t, frames, dpp is not None, list(sc)),
        out_shape=(
            jax.ShapeDtypeStruct((C, frames), F32),
            jax.ShapeDtypeStruct((C, frames), F32),
            jax.ShapeDtypeStruct((8, 128), F32),
        ),
        in_specs=[sm()] * 3 + [vm()] * n + [hb()] * 4 + [vm()] * len(more),
        out_specs=(hb(), hb(), vm()),
        input_output_aliases={n + 5: 0, n + 6: 1},
        scratch_shapes=list(sc.values()) + [pltpu.SemaphoreType.DMA((4,))],
        compiler_params=pltpu.CompilerParams(vmem_limit_bytes=VMEM_BYTES),
        cost_estimate=pl.CostEstimate(flops=1000, bytes_accessed=1000, transcendentals=0),
        name="fwd",
    )(*scal[1:], *[getattr(w, k) for k in FWD_W], fr, og, fo, p1, *more)


def moments(moment, square, grad):
    new_moment = BETA * moment + (1.0 - BETA) * grad
    new_square = BETA * square + (1.0 - BETA) * grad * grad
    correction = 1.0 - BETA**STEP
    direction = new_moment / correction / (jnp.sqrt(new_square / correction) + EPSILON)
    return (new_moment, new_square, direction)


def adam_update(weight, moment, square, grad, rate):
    new_moment, new_square, direction = moments(moment, square, grad)
    return (weight - rate * (direction + DECAY * weight), new_moment, new_square)


def fold_kernel(n, tp, *refs):
    keep_a, got_a, keep_o, got_o, dpp = refs[:5]
    outs = refs[5:]
    for m in range(n):
        outs[m][...] = (keep_a[m].astype(F32) + got_a[m].astype(F32)).astype(BF)
    keep, merged = outs[n:]
    blocks = dpp.shape[1] // 128
    for j in range(blocks):
        merged[j * HALF : (j + 1) * HALF, :] = dpp[:, j * 128 : (j + 1) * 128]
    half = tp // 2
    size = keep_o.shape[1]
    for q in range(tp):
        value = (keep_o[q].astype(F32) + got_o[q].astype(F32)).astype(BF)
        for j in range(3):
            lo = ((q % half) * 3 + j) * size
            part = value[:, j * 128 : (j + 1) * 128]
            if q < half:
                keep[lo : lo + size, :] = part
            else:
                merged[blocks * HALF + lo : blocks * HALF + lo + size, :] = part


def call_fold(keep_a, got_a, keep_o, got_o, dpp):
    n, tp, size = keep_a.shape[0], keep_o.shape[0], keep_o.shape[1]
    other = (tp // 2) * 3 * size
    sds = jax.ShapeDtypeStruct
    return pl.pallas_call(
        functools.partial(fold_kernel, n, tp),
        out_shape=[sds((LAYERS,) + keep_a.shape[2:], BF)] * n
        + [sds((other, 128), BF), sds((dpp.shape[1] // 128 * HALF + other, 128), BF)],
        in_specs=[vm()] * 5,
        out_specs=[vm()] * (n + 2),
        compiler_params=pltpu.CompilerParams(vmem_limit_bytes=VMEM_BYTES),
        cost_estimate=pl.CostEstimate(flops=1000, bytes_accessed=1000, transcendentals=0),
        name="fold",
    )(keep_a, got_a, keep_o, got_o, dpp)


def join_basis(own, other, scratch):
    core = jnp.bitwise_and(axis(DP), 1)
    for kk in range(own.shape[0]):
        for i in range(2):
            scratch[kk, 2 * core + i] = own[kk, i]
            scratch[kk, 2 * (1 - core) + i] = other[kk, i]


def rotate_kernel(n, tp, *refs):
    parts = refs[2 : 2 + n]
    outs = refs[2 + n : -1]
    basis = refs[-1]
    join_basis(refs[0], refs[1], basis)
    for layer in range(LAYERS):
        total = parts[0][layer].astype(F32)
        for m in range(1, n):
            total = total + parts[m][layer].astype(F32)
        total = total.astype(BF)
        for kk in range(tp):
            outs[kk][layer] = nn(basis[kk, layer], total).astype(BF)


def call_rotate(tp, basis, parts):
    cols = basis[0].shape[2]
    n = len(parts)
    return pl.pallas_call(
        functools.partial(rotate_kernel, n, tp),
        out_shape=[jax.ShapeDtypeStruct((LAYERS, cols, 128), BF)] * tp,
        in_specs=[vm()] * (2 + n),
        out_specs=[vm()] * tp,
        scratch_shapes=[pltpu.VMEM((tp, LAYERS, cols, 2 * HID), BF)],
        compiler_params=pltpu.CompilerParams(vmem_limit_bytes=VMEM_BYTES),
        cost_estimate=pl.CostEstimate(flops=1000, bytes_accessed=1000, transcendentals=0),
        name="rotate",
    )(*basis, *parts)


def moment_kernel(tp, rows, *refs):
    parts = refs[:tp]
    moment, square, new_moment, new_square, direction = refs[tp:]
    total = parts[0][...].astype(F32)
    for kk in range(1, tp):
        total = total + parts[kk][...].astype(F32)
    grad = total[:, :, 0:rows]
    m, v, d = moments(moment[...], square[...], grad)
    new_moment[...] = m
    new_square[...] = v
    direction[:, :, 0:rows] = d.astype(BF)
    if rows < 128:
        direction[:, :, rows:128] = jnp.zeros(d.shape[:2] + (128 - rows,), BF)


def call_moments(tp, rows, parts, moment, square):
    shape = moment.shape
    return pl.pallas_call(
        functools.partial(moment_kernel, tp, rows),
        out_shape=[
            jax.ShapeDtypeStruct(shape, F32),
            jax.ShapeDtypeStruct(shape, F32),
            jax.ShapeDtypeStruct(shape[:2] + (128,), BF),
        ],
        in_specs=[vm()] * (tp + 2),
        out_specs=[vm()] * 3,
        name="moments",
    )(*parts, moment, square)


def back_kernel(tp, rows, *refs):
    directions = refs[2 : 2 + tp]
    weight, out, scratch, basis = refs[2 + tp :]
    join_basis(refs[0], refs[1], basis)
    units = HID // tp
    me_tp = axis(TP)
    for layer in range(LAYERS):
        total = tn(basis[0, layer], directions[0][layer])
        for kk in range(1, tp):
            total = total + tn(basis[kk, layer], directions[kk][layer])
        scratch[layer] = total
    for layer in range(LAYERS):
        for h in range(2):
            row = pl.ds(pl.multiple_of(h * HID + me_tp * units, 16), units)
            back = scratch[layer, row, 0:rows]
            here = slice(h * units, (h + 1) * units)
            value = weight[layer, here, :]
            out[layer, here, :] = value - RATE_CONV * (back + DECAY * value)


def call_back(tp, rows, basis, directions, weight):
    return pl.pallas_call(
        functools.partial(back_kernel, tp, rows),
        out_shape=jax.ShapeDtypeStruct(weight.shape, F32),
        in_specs=[vm()] * (tp + 3),
        out_specs=vm(),
        scratch_shapes=[
            pltpu.VMEM((LAYERS, 2 * HID, 128), F32),
            pltpu.VMEM((tp, LAYERS, basis[0].shape[2], 2 * HID), BF),
        ],
        cost_estimate=pl.CostEstimate(flops=1000, bytes_accessed=1000, transcendentals=0),
        name="back",
    )(*basis, *directions, weight)


def small_kernel(tp, *refs):
    ins = refs[2:20]
    outs = refs[20:-1]
    scratch = refs[-1]
    size = scratch.shape[1]
    for i in range(2):
        for j in range(3):
            scratch[i, :, j * 128 : (j + 1) * 128] = refs[i][j * size : (j + 1) * size, :]
    lows, highs = scratch.at[0], scratch.at[1]
    units = HID // tp
    core = jnp.bitwise_and(axis(DP), 1)

    def put(i, grad, rate, index=None):
        if index is None:
            new = adam_update(ins[3 * i][...], ins[3 * i + 1][...], ins[3 * i + 2][...], grad, rate)
            for k in range(3):
                outs[3 * i + k][...] = new[k]
        else:
            new = adam_update(ins[3 * i][index], ins[3 * i + 1][index], ins[3 * i + 2][index], grad, rate)
            for k in range(3):
                outs[3 * i + k][index] = new[k]

    def rows(half, lo, size, c0, c1):
        a = lows[lo : lo + size, c0:c1].astype(F32)
        b = highs[lo : lo + size, c0:c1].astype(F32)
        return jnp.where(core == half, a, b)

    tail = rows(1, 3 * units - 16, 16, 0, 2 * HID)
    put(0, tail[4:7, 0:C], RATE_SMALL)
    put(1, tail[8:12, 0:4], RATE_MIX)
    put(2, rows(1, units, HALF, HID, 2 * HID), RATE_PRE)
    for h in range(2):
        put(3, tail[0:LAYERS, h * units : (h + 1) * units], RATE_BIAS, (slice(None), h, slice(None)))
    for layer in range(LAYERS):
        half = 1 if layer == LAYERS - 1 else 0
        lo = 0 if layer == LAYERS - 1 else layer * units
        put(4, rows(half, lo, units, 0, HID), RATE_RESSKIP, LAYERS - 1 + layer)
        if layer < LAYERS - 1:
            put(4, rows(half, lo, units, HID, 2 * HID), RATE_RESSKIP, layer)
    put(5, rows(1, units, units, 0, C), RATE_END)


def call_small(tp, low, high, ins):
    return pl.pallas_call(
        functools.partial(small_kernel, tp),
        out_shape=[jax.ShapeDtypeStruct(x.shape, F32) for x in ins],
        in_specs=[vm()] * (2 + len(ins)),
        out_specs=[vm()] * len(ins),
        scratch_shapes=[pltpu.VMEM((2, low.shape[0] // 3, 2 * HID), BF)],
        name="smallupd",
    )(low, high, *ins)


def local(
    frames_in,
    out_grad,
    logdet_grad,
    lengths,
    offsets,
    owners,
    small_params,
    small_moment,
    small_square,
    mix,
    mix_moment,
    mix_square,
    pre_weight,
    pre_moment,
    pre_square,
    conv_weight,
    conv_moment,
    conv_square,
    conv_basis,
    conv_bias,
    conv_bias_moment,
    conv_bias_square,
    res_skip,
    res_skip_moment,
    res_skip_square,
    end_weight,
    end_moment,
    end_square,
):
    dp = lax.axis_size("dp")
    tp = lax.axis_size("tp")
    frames = frames_in.shape[0]
    rows = conv_weight.shape[1]
    units = conv_weight.shape[3]
    own_len = frames // tp
    packed = dp * 128 <= MAX_PACKED

    def shift_tp(x, kk):
        return lax.ppermute(x, "tp", [(i, (i + kk) % tp) for i in range(tp)])

    def swap_dp(x, mask):
        return lax.ppermute(x, "dp", [(i, i ^ mask) for i in range(dp)])

    def swap_tp(x, mask):
        return lax.ppermute(x, TP, [(i, i ^ mask) for i in range(tp)])

    def plus(x, y):
        return (x.astype(F32) + y.astype(F32)).astype(BF)

    def gather_tp(x):
        return [x] + [shift_tp(x, kk) for kk in range(1, tp)]

    def after(value, *deps):
        return lax.optimization_barrier((value, *deps))[0]

    cw = jnp.transpose(conv_weight, (0, 2, 3, 1)).reshape(LAYERS, 2 * units, rows)
    shard, shard_b, basis_t = call_pack(
        rows, units, cw, res_skip, end_weight, conv_bias, conv_basis.reshape(LAYERS, 2 * HID, -1)
    )
    w = space(CONST_W, call_consts(mix, logdet_grad, small_params, pre_weight))

    def chips(col):
        return {m: (col if m == 0 else swap_dp(col, m)) for m in range(0, dp, 2)}

    def cores(pieces):
        pieces = dict(pieces)
        for m in range(0, dp, 2):
            pieces[m + 1] = swap_dp(pieces[m], 1)
        pieces = [pieces[m] for m in range(dp)]
        if not packed:
            slot = jnp.bitwise_xor(lax.axis_index("dp"), owners)
            column_of = lax.rem(lax.axis_index("tp") - jnp.arange(tp) + tp, tp)
            stacked = jnp.stack(pieces)[slot][:, column_of]
            stacked = stacked.reshape(dp, tp, 2, 2, units, 128)[..., :rows]
            pieces = [jnp.transpose(stacked, (2, 3, 1, 4, 0, 5)).reshape(2, 2 * HID, KER * HID)]
        return pieces

    both = gather_tp(shard)
    col_a = after(jnp.stack([x[: 4 * units] for x in both]), w.rows)
    res_own = jnp.stack([x[4 * units :] for x in both])
    half_a = chips(col_a)
    res_pieces = [res_own, swap_dp(res_own, 1)]
    pieces_a = cores(half_a)
    col_b = jnp.stack(gather_tp(after(shard_b, w.rows)))
    half_b = chips(after(col_b, half_a[dp - 2]))
    basis_t = after(basis_t, *[half_a[m] for m in range(2, dp, 2)])[None]
    basis_near = swap_tp(basis_t, 1)
    scal = [owners, offsets, lengths, logdet_grad]
    fr = frames_in.T
    og = out_grad.T

    (wt_a, rsb, rsf, end, end_t, bias, h, skip, hbs, tt, ss) = call_own_forward(
        dp, tp, rows, own_len, frames, scal, w, fr, pieces_a, res_pieces
    )
    w.wt_a = wt_a
    w.rsb = rsb
    w.rsf = rsf
    w.end = end
    w.end_t = end_t
    w.bias = bias
    pieces_b = cores(after(half_b, h))
    basis_col = jnp.concatenate([basis_t, after(basis_near, h)])
    basis_far = swap_tp(basis_col, 2)
    (wt_b, fo, result, d_end, d_ebias, hbs_b, tt_b, ss_b, dsk, dm, x0) = call_own_middle(
        dp, tp, rows, own_len, frames, scal, w, fr, og, h, skip, pieces_b
    )
    w.wt_b = wt_b
    basis_far, result = lax.optimization_barrier((basis_far, result))
    basis_col = jnp.concatenate([basis_col, basis_far])
    basis_pieces = [basis_col, swap_dp(basis_col, 1)]
    turn = tp // 2
    rest = [kk for kk in range(1, tp) if kk != turn]
    results = {kk: shift_tp(result, kk) for kk in rest}
    w.d_end = d_end
    w.d_ebias = d_ebias
    (keep_a, send_a, keep_o, send_o, dpp, fg) = call_own_last(
        dp, tp, rows, own_len, frames, scal, w, fr, dsk, dm, x0, [wt_a, tt, ss, hbs], [wt_b, tt_b, ss_b, hbs_b]
    )

    def order(keep, send):
        if packed:
            return keep, send
        gsend = jnp.concatenate([keep, send])
        where = jnp.bitwise_xor(lax.axis_index("dp"), bit_reverse(jnp.arange(dp), (dp - 1).bit_length()))
        block = jnp.argsort(owners)[where]
        gsend = jnp.transpose(gsend.reshape(LAYERS, 2 * HID, dp, rows), (2, 0, 1, 3))[block]
        gsend = jnp.pad(gsend, ((0, 0), (0, 0), (0, 0), (0, 128 - rows)))
        return gsend[: dp // 2], gsend[dp // 2 :]

    send_a, send_o, basis_pieces[1], *gone = lax.optimization_barrier(
        (send_a, send_o, basis_pieces[1], *results.values())
    )
    results = dict(zip(results, gone))
    keep_a, send_a = order(keep_a, send_a)
    got_a = swap_dp(send_a, 1)
    got_o = swap_dp(send_o, 1)
    folded = call_fold(keep_a, got_a, keep_o, got_o, dpp)
    n = dp // 2
    bits = (dp - 1).bit_length()
    masks = [2 * bit_reverse(p, bits - 1) for p in range(n)]
    parts = [folded[0]] + [swap_dp(folded[p], masks[p]) for p in range(1, n)]
    turn = tp // 2
    merged = swap_tp(folded[n + 1], turn)
    dpps = {kk: shift_tp(dpp, kk) for kk in rest}

    fr1, dpps[rest[-1]] = lax.optimization_barrier((after(fr, folded[0]), dpps[rest[-1]]))
    fo, fg, ld = call_fwd(tp, turn, own_len, frames, scal, w, fr1, og, fo, fg)
    lds = [ld[:, 0]] + [
        jnp.sum(x[C : C + 16, 0].astype(F32).reshape(2, 8), axis=0) for x in [result, *results.values()]
    ]

    ready, *near = lax.optimization_barrier((parts[0], ld, *parts[1:], *[dpps[kk] for kk in rest]))
    parts = [ready] + near[1:n]
    dpps.update(zip(rest, near[n:]))
    turned = call_rotate(tp, basis_pieces, parts)
    rotated = [turned[0]] + [swap_tp(turned[x], x) for x in range(1, tp)]
    size = 3 * (3 * units)
    merged = after(merged, ld)
    others = [
        plus(folded[n][i * size : (i + 1) * size], merged[own_len // 128 * HALF + i * size :][:size])
        for i in range(turn)
    ]
    others = [others[0], swap_tp(after(others[1], turned[0]), 1)]
    fo, fg = call_assemble(
        tp, rest, turn, own_len, scal, w, [results[kk] for kk in rest], [dpps[kk] for kk in rest],
        after(fr, turned[0]), og, merged, fo, fg,
    )
    total = plus(others[0], after(others[1], fg))
    steps = [1 << bit for bit in range(1, bits)]
    got = swap_dp(total, steps[0])
    conv_m, conv_v, direction = call_moments(
        tp,
        rows,
        [rotated[0]] + [after(x, fg) for x in rotated[1:]],
        jnp.transpose(conv_moment, (0, 2, 1)),
        jnp.transpose(conv_square, (0, 2, 1)),
    )
    directions = [direction] + [swap_tp(direction, x) for x in range(1, tp)]
    total = plus(total, after(got, direction))
    for mask in steps[1:]:
        total = plus(total, swap_dp(total, mask))
    other = swap_dp(total, 1)
    updated = call_small(
        tp,
        total,
        other,
        [
            small_params, small_moment, small_square,
            mix, mix_moment, mix_square,
            pre_weight, pre_moment, pre_square,
            conv_bias, conv_bias_moment, conv_bias_square,
            res_skip, res_skip_moment, res_skip_square,
            end_weight, end_moment, end_square,
        ],
    )
    directions = [direction] + [after(x, updated[0]) for x in directions[1:]]
    conv_new = call_back(tp, rows, basis_pieces, directions, cw)
    logdet = w.extra[8:, 0] + sum(lds) / lengths.astype(F32)

    def conv_out(x):
        return jnp.transpose(x.reshape(LAYERS, 2, units, rows), (0, 3, 1, 2))

    (small_new, small_m, small_v, mix_new, mix_m, mix_v, pre_new, pre_m, pre_v, bias_new, bias_m, bias_v,
     rs_new, rs_m, rs_v, end_new, end_m, end_v) = updated
    return (
        fo.T,
        logdet,
        fg.T,
        small_new,
        small_m,
        small_v,
        mix_new,
        mix_m,
        mix_v,
        pre_new,
        pre_m,
        pre_v,
        conv_out(conv_new),
        jnp.transpose(conv_m, (0, 2, 1)),
        jnp.transpose(conv_v, (0, 2, 1)),
        bias_new,
        bias_m,
        bias_v,
        rs_new,
        rs_m,
        rs_v,
        end_new,
        end_m,
        end_v,
    )


def solution(mesh):
    return jax.shard_map(
        local,
        mesh=mesh,
        in_specs=(
            P("dp", None),
            P("dp", None),
            P("dp"),
            P("dp"),
            P("dp"),
            P(),
            P(),
            P(),
            P(),
            P(),
            P(),
            P(),
            P(),
            P(),
            P(),
            P(None, "dp", None, "tp"),
            P(None, "dp", "tp"),
            P(None, "dp", "tp"),
            P(None, None, None, "tp"),
            P(None, None, "tp"),
            P(None, None, "tp"),
            P(None, None, "tp"),
            P(None, "tp", None),
            P(None, "tp", None),
            P(None, "tp", None),
            P("tp", None),
            P("tp", None),
            P("tp", None),
        ),
        out_specs=(
            P("dp", None),
            P("dp"),
            P("dp", None),
            P(),
            P(),
            P(),
            P(),
            P(),
            P(),
            P(),
            P(),
            P(),
            P(None, "dp", None, "tp"),
            P(None, "dp", "tp"),
            P(None, "dp", "tp"),
            P(None, None, "tp"),
            P(None, None, "tp"),
            P(None, None, "tp"),
            P(None, "tp", None),
            P(None, "tp", None),
            P(None, "tp", None),
            P("tp", None),
            P("tp", None),
            P("tp", None),
        ),
        check_vma=False,
    )
```

```python
import functools
import types
import jax
import jax.numpy as jnp
from jax import lax
from jax.experimental import pallas as pl
from jax.experimental.pallas import tpu as pltpu
from jax.sharding import PartitionSpec as P

C = 160
HALF = 80
HID = 192
KER = 5
LAYERS = 4
STEP = 5
HALO = 128
MAX_PACKED = 1024
VMEM_BYTES = 62 * 1024 * 1024

BETA = 0.5
EPSILON = 1e-08
DECAY = 0.01
RATE_SMALL = 0.1
RATE_MIX = 0.3
RATE_PRE = 0.1
RATE_CONV = 0.03
RATE_BIAS = 0.3
RATE_RESSKIP = 0.07
RATE_END = 0.04
PRECISE = lax.Precision.HIGHEST
BF = jnp.bfloat16
TP = "tp"
DP = "dp"
F32 = jnp.float32


class Names:
    def __init__(self):
        self.found = []

    def __getattr__(self, name):
        self.found.append(name)


def names_of(select):
    got = Names()
    select(got)
    return got.found


def space(names, values):
    return types.SimpleNamespace(**dict(zip(names, values)))


CONST_W = names_of(
    lambda w: (w.a_hi, w.a_lo, w.at_b, w.cvec, w.pre_t, w.pre_b, w.ebias, w.mixfull, w.rows, w.extra, w.basis)
)


def nn(a, b, precision=None):
    return lax.dot_general(a, b, (((1,), (0,)), ((), ())), precision=precision, preferred_element_type=F32)


def nt(a, b, precision=None):
    return lax.dot_general(a, b, (((1,), (1,)), ((), ())), precision=precision, preferred_element_type=F32)


def tn(a, b, precision=None):
    return lax.dot_general(a, b, (((0,), (0,)), ((), ())), precision=precision, preferred_element_type=F32)


def sigmoid(x):
    return 0.5 * jnp.tanh(0.5 * x) + 0.5


def vm():
    return pl.BlockSpec(memory_space=pltpu.VMEM)


def sm():
    return pl.BlockSpec(memory_space=pltpu.SMEM)


def hb():
    return pl.BlockSpec(memory_space=pl.ANY)


def bit_reverse(value, bits):
    out = value * 0
    for i in range(bits):
        out = out | (((value >> i) & 1) << (bits - 1 - i))
    return out


def axis(name):
    return lax.axis_index(name)


def from_left(me, kk, n):
    return lax.rem(me - kk + n, n)


def column(scalars, dtype, rows=8):
    index = lax.broadcasted_iota(jnp.int32, (rows, 1), 0)
    out = jnp.zeros((rows, 1), dtype)
    for u in range(rows):
        out = jnp.where(index == u, scalars[u], out)
    return out


def to_column(row):
    n = row.shape[1]
    eye = lax.broadcasted_iota(jnp.int32, (n, n), 0) == lax.broadcasted_iota(jnp.int32, (n, n), 1)
    return jnp.sum(jnp.where(eye, jnp.broadcast_to(row, (n, n)), 0.0), axis=1, keepdims=True)


def pack_kernel(rows, units, conv, res, end, bias, packed, later, full):
    zero = jnp.zeros((2 * units, 128 - rows), BF)
    for layer in range(LAYERS):
        dst = packed if layer < 2 else later
        here = slice((layer % 2) * 2 * units, (layer % 2 + 1) * 2 * units)
        dst[here, 0:rows] = conv[layer].astype(BF)
        dst[here, rows:128] = zero
    core = jnp.bitwise_and(axis(DP), 1)
    for layer in range(LAYERS):
        full[layer, :, 0:HID] = res[LAYERS - 1 + layer].astype(BF)
        if layer < LAYERS - 1:
            full[layer, :, HID : 2 * HID] = res[layer].astype(BF)
    full[LAYERS - 1, :, HID : HID + C] = end[...].astype(BF)
    flat = jnp.concatenate([bias[layer] for layer in range(LAYERS)], axis=0).T
    hi = flat.astype(BF)
    lo = (flat - hi.astype(F32)).astype(BF)
    full[LAYERS - 1, :, HID + C : 2 * HID] = jnp.concatenate(
        [hi, lo, jnp.zeros((units, HID - C - 16), BF)], axis=1
    )
    for i in range(2):
        for c in range(3):
            lo = 4 * units + (3 * i + c) * units
            packed[lo : lo + units, :] = full[2 * core + i, :, c * 128 : (c + 1) * 128]


def call_pack(rows, units, conv, res, end, bias):
    return pl.pallas_call(
        functools.partial(pack_kernel, rows, units),
        out_shape=[
            jax.ShapeDtypeStruct((10 * units, 128), BF),
            jax.ShapeDtypeStruct((4 * units, 128), BF),
        ],
        in_specs=[vm()] * 4,
        out_specs=[vm()] * 2,
        scratch_shapes=[pltpu.VMEM((LAYERS, units, 2 * HID), BF)],
        name="pack",
    )(conv, res, end, bias)


def minor_det(m, r, left, right):
    return m[r, left] * m[r + 1, right] - m[r + 1, left] * m[r, right]


def consts_kernel(mix, lg, small, pre, basis, a_hi, a_lo, at_b, cvec, pre_t, pre_b, ebias, mixfull, rows_out, extra, basis_out):
    core = jnp.bitwise_and(axis(DP), 1)
    for i in range(2):
        basis_out[i] = basis[2 * core + i].T.astype(BF)
    m = [[mix[i, j] for j in range(4)] for i in range(4)]
    ch_r = lax.broadcasted_iota(jnp.int32, (C, 1), 0)
    ch_c = lax.broadcasted_iota(jnp.int32, (1, C), 1)

    def pair(ch):
        return 2 * (ch >= HALF).astype(jnp.int32) + jnp.bitwise_and(ch, 1)

    def group(ch):
        return lax.shift_right_logical(ch - jnp.where(ch >= HALF, HALF, 0), 1)

    same = group(ch_r) == group(ch_c)
    pr, pc = pair(ch_r), pair(ch_c)
    full = jnp.zeros((C, C), F32)
    turned = jnp.zeros((C, C), F32)
    for p in range(4):
        row = jnp.zeros((1, C), F32)
        row_t = jnp.zeros((1, C), F32)
        for q in range(4):
            row = jnp.where(pc == q, m[p][q], row)
            row_t = jnp.where(pc == q, m[q][p], row_t)
        full = jnp.where(pr == p, row, full)
        turned = jnp.where(pr == p, row_t, turned)
    full = jnp.where(same, full, 0.0)
    turned = jnp.where(same, turned, 0.0)
    es = jnp.exp(small[0:1, :])
    at = full * es
    hi = at.astype(BF)
    a_hi[...] = hi
    a_lo[...] = (at - hi.astype(F32)).astype(BF)
    at_b[...] = (turned * to_column(es)).astype(BF)
    cvec[...] = jnp.sum(full * small[1:2, :], axis=1, keepdims=True)
    mixfull[...] = full
    pre_t[...] = pre[...].T.astype(BF)
    pre_b[...] = pre[...].astype(BF)
    ebias[...] = to_column(small[2:3, :])
    pairs = [(0, 1), (0, 2), (0, 3), (1, 2), (1, 3), (2, 3)]
    up = {ab: m[0][ab[0]] * m[1][ab[1]] - m[1][ab[0]] * m[0][ab[1]] for ab in pairs}
    dn = {ab: m[2][ab[0]] * m[3][ab[1]] - m[3][ab[0]] * m[2][ab[1]] for ab in pairs}
    det = (
        up[0, 1] * dn[2, 3]
        - up[0, 2] * dn[1, 3]
        + up[0, 3] * dn[1, 2]
        + up[1, 2] * dn[0, 3]
        - up[1, 3] * dn[0, 2]
        + up[2, 3] * dn[0, 1]
    )

    def minor3(i, j):
        cols = [c for c in range(4) if c != j]
        two = dn if i < 2 else up
        other = m[1 - i] if i < 2 else m[5 - i]
        return (
            other[cols[0]] * two[cols[1], cols[2]]
            - other[cols[1]] * two[cols[0], cols[2]]
            + other[cols[2]] * two[cols[0], cols[1]]
        )

    total = lg[0]
    for u in range(1, lg.shape[0]):
        total = total + lg[u]
    first = jnp.where(axis(TP) == 0, total, 0.0)
    det_v = jnp.full((8, 128), det, F32)
    r = lax.broadcasted_iota(jnp.int32, (8, 128), 0)
    c = lax.broadcasted_iota(jnp.int32, (8, 128), 1)
    cof = jnp.zeros((8, 128), F32)
    for i in range(4):
        for j in range(4):
            sign = 1.0 if (i + j) % 2 == 0 else -1.0
            cof = jnp.where(jnp.logical_and(r == i, c == j), sign * minor3(i, j), cof)
    extra[0:8, :] = first * (C // 4) * cof / det_v
    gain = jnp.sum(small[0:1, :], axis=1, keepdims=True)
    extra[8:16, :] = gain + (C // 4) * jnp.log(det_v)
    rows_out[...] = jnp.concatenate(
        [es, small[1:2, :], jnp.full((1, C), first, F32), jnp.zeros((5, C), F32)], axis=0
    )


def call_consts(mix, lg, small, pre, basis):
    return pl.pallas_call(
        consts_kernel,
        out_shape=[
            jax.ShapeDtypeStruct((C, C), BF),
            jax.ShapeDtypeStruct((C, C), BF),
            jax.ShapeDtypeStruct((C, C), BF),
            jax.ShapeDtypeStruct((C, 1), F32),
            jax.ShapeDtypeStruct((HID, HALF), BF),
            jax.ShapeDtypeStruct((HALF, HID), BF),
            jax.ShapeDtypeStruct((C, 1), F32),
            jax.ShapeDtypeStruct((C, C), F32),
            jax.ShapeDtypeStruct((8, C), F32),
            jax.ShapeDtypeStruct((16, 128), F32),
            jax.ShapeDtypeStruct((2, basis.shape[2], 2 * HID), BF),
        ],
        in_specs=[sm(), sm(), vm(), vm(), vm()],
        out_specs=[vm()] * 11,
        name="consts",
    )(mix, lg, small, pre, basis)


def tap_stack(wide, size, reverse):
    half = KER // 2
    parts = []
    for k in range(KER):
        shift = half - k if not reverse else k - half
        moved = wide if shift == 0 else pltpu.roll(wide, shift % wide.shape[1], 1)
        parts.append(moved[:, 128 : 128 + size])
    return jnp.concatenate(parts, axis=0)


def make_masks(s, scal, t, w0):
    off, length, lg = scal
    o = column(off, jnp.int32)
    n = column(length, jnp.int32)
    pos = lax.broadcasted_iota(jnp.int32, (8, t), 1) + w0
    member = jnp.logical_and(pos >= o, pos < o + n).astype(F32)
    s.member[...] = member
    s.mask[...] = jnp.broadcast_to(jnp.sum(member, axis=0, keepdims=True), (8, t))
    return column(lg, F32) / n.astype(F32)


def zero_edges(ref, lead, t):
    for slot in lead:
        at = ref if slot is None else ref.at[slot]
        z = jnp.zeros((at.shape[0], 128), BF)
        at[:, 0:128] = z
        at[:, t + 128 : t + 256] = z


def mixed_of(w, fr, mask):
    return (nn(w.a_hi[...], fr) + nn(w.a_lo[...], fr) + w.cvec[...]) * mask


def unpack_conv(tp, rows, owners, dp, scratch, wt):
    me_tp, me_dp = axis(TP), axis(DP)
    units = HID // tp

    def layer_body(layer, carry):
        for b in range(dp):
            m = jnp.bitwise_xor(me_dp, owners[b])
            for kk in range(tp):
                src = from_left(me_tp, kk, tp)
                for h in range(2):
                    row = pl.ds(pl.multiple_of(src * units + h * HID, 16), units)
                    lo = pl.multiple_of(layer * 2 * units + h * units, 16)
                    wt[layer, row, b * rows : (b + 1) * rows] = scratch[m, kk, pl.ds(lo, units), 0:rows]
        return carry

    lax.fori_loop(0, 2, layer_body, 0)


def unpack_res(tp, res_pieces, rsb, rsf, end, end_t, bias, scr):
    me_tp = axis(TP)
    core = jnp.bitwise_and(axis(DP), 1)
    units = HID // tp
    for kk in range(tp):
        for i in range(2):
            for c in range(3):
                lo = (3 * i + c) * units
                lanes = slice(c * 128, (c + 1) * 128)
                scr[kk, 2 * core + i, :, lanes] = res_pieces[0][kk, lo : lo + units, :]
                scr[kk, 2 * (1 - core) + i, :, lanes] = res_pieces[1][kk, lo : lo + units, :]
    res_pieces = [scr.at[kk] for kk in range(tp)]
    for kk in range(tp):
        src = from_left(me_tp, kk, tp)
        row = pl.ds(pl.multiple_of(src * units, 16), units)
        for layer in range(LAYERS - 1):
            rsb[layer, row, :] = res_pieces[kk][layer]
        last = res_pieces[kk][LAYERS - 1]
        rsb[LAYERS - 1, row, 0:HID] = last[:, 0:HID]
        rsb[LAYERS - 1, row, HID : 2 * HID] = jnp.zeros((units, HID), BF)
        end[row, :] = last[:, HID : HID + C]
        tail = last[:, HID + C : 2 * HID].astype(F32)
        for layer in range(LAYERS):
            for h in range(2):
                i = layer * 2 + h
                at = pl.ds(pl.multiple_of(src * units + h * HID, 16), units)
                bias[layer, at, :] = tail[:, i : i + 1] + tail[:, 8 + i : 9 + i]
    for layer in range(LAYERS):
        rsf[layer, 0:HID, :] = rsb[layer, :, HID : 2 * HID].astype(F32).T.astype(BF)
        rsf[layer, HID : 2 * HID, :] = rsb[layer, :, 0:HID].astype(F32).T.astype(BF)
    end_t[...] = end[...].astype(F32).T.astype(BF)


def forward_layer(s, t, wt, rsf, bias, mask, here, after, save, before_skip=None):
    g = nn(wt, tap_stack(s.hb[here], t, False)) + bias
    tt = jnp.tanh(g[0:HID])
    ss = sigmoid(g[HID : 2 * HID])
    act = (tt * ss).astype(BF)
    y = nn(rsf, act)
    if before_skip is not None:
        before_skip()
    s.skip[...] += y[HID : 2 * HID]
    hv = (s.h[...] + y[0:HID]) * mask
    s.h[...] = hv
    if save is not None:
        s.tt[save] = tt.astype(BF)
        s.ss[save] = ss.astype(BF)
    s.hb[after, :, 128 : t + 128] = hv.astype(BF)


def start_hidden(s, t, w, mixed, mask):
    hv = nn(w.pre_t[...], mixed[0:HALF].astype(BF)) * mask
    s.h[...] = hv
    s.hb[0, :, 128 : t + 128] = hv.astype(BF)
    s.skip[...] = jnp.zeros((HID, t), F32)


def window_tail(own, t, w, s, mixed, mask, weight, dpp=None):
    skip_low = (s.skip[...] * mask).astype(BF)
    proj = nn(w.end_t[...], skip_low) + w.ebias[...]
    shift = proj[0:HALF]
    log_scale = proj[HALF:C]
    e = jnp.exp(log_scale)
    x0 = mixed[0:HALF]
    x1 = mixed[HALF:C]
    s.fo[0:HALF, :] = x0
    s.fo[HALF:C, :] = (shift + e * x1) * mask
    s.pf[...] = jnp.broadcast_to(jnp.sum(log_scale, axis=0, keepdims=True), (8, t))
    og = s.og[...].astype(F32)
    d_shift = og[HALF:C] * mask
    de = d_shift * e
    first = og[0:HALF] * mask
    if not own and dpp is not None:
        first = first + dpp
    dm = jnp.concatenate([first, de], axis=0).astype(BF)
    if not own:
        s.p1[...] = nn(w.at_b[...], dm)
    if own:
        s.dm[...] = dm
        s.x0b[...] = x0.astype(BF)
        fw = jnp.sum(s.member[...] * weight, axis=0, keepdims=True)
        d_log = de * x1 + fw
        d_proj = jnp.concatenate([d_shift, d_log], axis=0).astype(BF)
        s.dproj[...] = d_proj
        s.skl[...] = skip_low
        s.dsk[...] = (nn(w.end[...], d_proj) * mask).astype(BF)


def logdet_part(s, own):
    part = jnp.sum(s.member[:, own] * s.pf[:, own], axis=1, keepdims=True)
    return jnp.broadcast_to(part, (8, 128))


def backward_layer(s, t, layer, slot, own, own_in, own_len, wt, rsb, mask, ones, put_rs, put_conv):
    carried = s.h[...] * mask
    s.h[...] = carried
    s.d[0:HID, :] = s.dsk[...]
    s.d[HID : 2 * HID, :] = carried.astype(BF)
    da = nn(rsb[layer], s.d[...])
    tt = s.tt[slot].astype(F32)
    ss = s.ss[slot].astype(F32)
    das = da * ss
    s.dg[0:HID, 128 : t + 128] = (das * (1.0 - tt * tt)).astype(BF)
    s.dg[HID : 2 * HID, 128 : t + 128] = (das * tt * (1.0 - ss)).astype(BF)
    act = (s.tt[slot, :, own].astype(F32) * s.ss[slot, :, own].astype(F32)).astype(BF)
    put_rs(layer, nt(act, s.d[:, own]))
    s.smallg[pl.ds(layer, 1), :] = nt(ones, s.dg[:, own_in])[0:1]
    wide = s.hb[slot, :, pl.ds(pl.multiple_of(own_in.start - 128, 128), own_len + 256)]
    s.dw[:, 0 : KER * HID] = nt(s.dg[:, own_in], tap_stack(wide, own_len, False))
    put_conv(slot)
    for k in range(KER):
        s.wd[:, k * 2 * HID : (k + 1) * 2 * HID] = (
            wt[slot, :, k * HID : (k + 1) * HID].astype(F32).T.astype(BF)
        )
    s.h[...] += nn(s.wd[...], tap_stack(s.dg[...], t, True))


def rs_writer(tp, osend, units):
    me_tp, me_dp = axis(TP), axis(DP)
    core = jnp.bitwise_and(me_dp, 1)
    slots = [jnp.bitwise_xor(q, me_tp) for q in range(tp)]

    def put(layer, value):
        half = jnp.where(layer == LAYERS - 1, 1 - core, core)
        row = pl.multiple_of(lax.rem(layer, LAYERS - 1) * units, 16)
        for q in range(tp):
            osend[half, slots[q], pl.ds(row, units), :] = value[q * units : (q + 1) * units].astype(BF)

    return put, slots, 1 - core


def conv_writer(dp, rows, owners, gsend, dw):
    me_dp = axis(DP)
    bits = (dp - 1).bit_length()

    def put(slot):
        if dp * 128 <= MAX_PACKED:
            for b in range(dp):
                p = bit_reverse(jnp.bitwise_xor(me_dp, owners[b]), bits)
                gsend[p, slot, :, 0:rows] = dw[:, b * rows : (b + 1) * rows].astype(BF)
        else:
            gsend[slot] = dw[:, 0 : KER * HID].astype(BF)

    return put


def place(own_len, t, frames, q):
    start = q * own_len
    w0 = jnp.clip(start - HALO, 0, frames - t)
    return pl.multiple_of(w0, 128), pl.multiple_of(start - w0, 128), pl.multiple_of(start, 128)


BASE_W = names_of(lambda w: (w.a_hi, w.a_lo, w.cvec, w.pre_t,))
TAIL_W = names_of(lambda w: (w.a_hi, w.a_lo, w.cvec, w.end_t, w.ebias, w.at_b,))


def own_forward_kernel(dp, tp, rows, own_len, t, frames, npiece, snames, owners, off, length, lg, *refs):
    w = space(BASE_W, refs)
    refs = refs[len(BASE_W) :]
    fr_any = refs[0]
    pieces = refs[1 : 1 + npiece]
    res_pieces = refs[1 + npiece : 3 + npiece]
    outs = refs[3 + npiece :]
    wt_any, rsb, rsf, end, end_t, bias, h_any, skip_any, hb_any, tt_any, ss_any = outs[:11]
    s = space(snames, outs[11:-2])
    piece_sem, sem = outs[-2:]
    w0, _, _ = place(own_len, t, frames, axis(TP))
    copies = [pltpu.make_async_copy(pieces[m], s.pieces.at[m], piece_sem.at[m]) for m in range(npiece)]
    load = pltpu.make_async_copy(fr_any.at[:, pl.ds(w0, t)], s.fr, sem.at[0])
    load.start()
    for c in copies:
        c.start()
    make_masks(s, (off, length, lg), t, w0)
    zero_edges(s.hb, range(3), t)
    unpack_res(tp, res_pieces, rsb, rsf, end, end_t, bias, s.res)
    load.wait()
    mask = s.mask[0:1, :]
    start_hidden(s, t, w, mixed_of(w, s.fr[...], mask), mask)
    for c in copies:
        c.wait()
    if npiece > 1:
        unpack_conv(tp, rows, owners, dp, s.pieces, s.wt)
    else:
        s.wt[...] = s.pieces[0]
    stores = [pltpu.make_async_copy(s.wt, wt_any, sem.at[6])]
    stores[0].start()

    def kept(layer):
        return [
            pltpu.make_async_copy(s.hb.at[layer], hb_any.at[layer], sem.at[7 + layer]),
            pltpu.make_async_copy(s.tt.at[layer], tt_any.at[layer], sem.at[9 + layer]),
            pltpu.make_async_copy(s.ss.at[layer], ss_any.at[layer], sem.at[11 + layer]),
        ]

    def layer_body(layer, carry):
        forward_layer(s, t, s.wt[layer], rsf[layer], bias[layer], s.mask[0:1, :], layer, layer + 1, layer)
        for c in kept(layer):
            c.start()
        return carry

    lax.fori_loop(0, 2, layer_body, 0)
    last = [
        pltpu.make_async_copy(s.h, h_any, sem.at[1]),
        pltpu.make_async_copy(s.skip, skip_any, sem.at[2]),
    ]
    for c in last:
        c.start()
    for c in stores + last + kept(0) + kept(1):
        c.wait()


def call_own_forward(dp, tp, rows, own_len, frames, scal, w, fr, pieces, res_pieces):
    t = min(own_len + 2 * HALO, frames)
    sc = dict(
        member=pltpu.VMEM((8, t), F32),
        mask=pltpu.VMEM((8, t), F32),
        fr=pltpu.VMEM((C, t), BF),
        h=pltpu.VMEM((HID, t), F32),
        skip=pltpu.VMEM((HID, t), F32),
        hb=pltpu.VMEM((3, HID, t + 256), BF),
        tt=pltpu.VMEM((2, HID, t), BF),
        ss=pltpu.VMEM((2, HID, t), BF),
        pieces=pltpu.VMEM((len(pieces),) + pieces[0].shape, BF),
        res=pltpu.VMEM((tp, LAYERS, HID // tp, 2 * HID), BF),
        wt=pltpu.VMEM((2, 2 * HID, KER * HID), BF),
    )
    sds = jax.ShapeDtypeStruct
    return pl.pallas_call(
        functools.partial(own_forward_kernel, dp, tp, rows, own_len, t, frames, len(pieces), list(sc)),
        out_shape=[
            sds((2, 2 * HID, KER * HID), BF),
            sds((LAYERS, HID, 2 * HID), BF),
            sds((LAYERS, 2 * HID, HID), BF),
            sds((HID, C), BF),
            sds((C, HID), BF),
            sds((LAYERS, 2 * HID, 1), F32),
            sds((HID, t), F32),
            sds((HID, t), F32),
            sds((2, HID, t + 256), BF),
            sds((2, HID, t), BF),
            sds((2, HID, t), BF),
        ],
        in_specs=[sm()] * 4 + [vm()] * len(BASE_W) + [hb()] * (1 + len(pieces)) + [vm()] * 2,
        out_specs=[hb()] + [vm()] * 5 + [hb()] * 5,
        scratch_shapes=list(sc.values())
        + [pltpu.SemaphoreType.DMA((len(pieces),)), pltpu.SemaphoreType.DMA((13,))],
        compiler_params=pltpu.CompilerParams(vmem_limit_bytes=VMEM_BYTES),
        cost_estimate=pl.CostEstimate(flops=1000, bytes_accessed=1000, transcendentals=0),
        name="ownfwd",
    )(*scal, *[getattr(w, k) for k in BASE_W], fr, *pieces, *res_pieces)


def conv_shape(dp):
    return (dp, LAYERS, 2 * HID, 128) if dp * 128 <= MAX_PACKED else (LAYERS, 2 * HID, KER * HID)


MID_W = names_of(lambda w: (w.a_hi, w.a_lo, w.cvec, w.end_t, w.ebias, w.at_b, w.end, w.rsf, w.bias,))
MID_STATE = names_of(lambda w: (w.hb, w.tt, w.ss, w.dsk, w.dm, w.x0b,))


def own_middle_kernel(dp, tp, rows, own_len, t, frames, npiece, snames, owners, off, length, lg, *refs):
    w = space(MID_W, refs)
    refs = refs[len(MID_W) :]
    fr_any, og_any, h_in, skip_in = refs[:4]
    pieces = refs[4 : 4 + npiece]
    refs = refs[4 + npiece :]
    wt_any, fo_any, result, d_end_out, ebias_out = refs[:5]
    state = space(MID_STATE, refs[5:11])
    s = space(snames, refs[11:-2])
    piece_sem, sem = refs[-2:]
    w0, off_own, start = place(own_len, t, frames, axis(TP))
    copies = [pltpu.make_async_copy(pieces[m], s.pieces.at[m], piece_sem.at[m]) for m in range(npiece)]
    loads = [
        pltpu.make_async_copy(h_in, s.h, sem.at[0]),
        pltpu.make_async_copy(skip_in, s.skip, sem.at[1]),
        pltpu.make_async_copy(fr_any.at[:, pl.ds(w0, t)], s.fr, sem.at[2]),
        pltpu.make_async_copy(og_any.at[:, pl.ds(w0, t)], s.og, sem.at[3]),
    ]
    for c in loads[:1] + copies + loads[1:]:
        c.start()
    weight = make_masks(s, (off, length, lg), t, w0)
    zero_edges(s.hb, range(3), t)
    loads[0].wait()
    s.hb[0, :, 128 : t + 128] = s.h[...].astype(BF)
    for c in copies:
        c.wait()
    if npiece > 1:
        unpack_conv(tp, rows, owners, dp, s.pieces, s.wt)
    else:
        s.wt[...] = s.pieces[0]
    stores = [pltpu.make_async_copy(s.wt, wt_any, sem.at[11])]
    stores[0].start()

    def kept(layer):
        return [
            pltpu.make_async_copy(s.hb.at[layer], state.hb.at[layer], sem.at[12 + layer]),
            pltpu.make_async_copy(s.tt.at[layer], state.tt.at[layer], sem.at[14 + layer]),
            pltpu.make_async_copy(s.ss.at[layer], state.ss.at[layer], sem.at[16 + layer]),
        ]

    def layer_body(i, carry):
        def skip_here():
            @pl.when(i == 0)
            def _():
                loads[1].wait()

        forward_layer(
            s, t, s.wt[i], w.rsf[i + 2], w.bias[i + 2], s.mask[0:1, :], i, i + 1, i, skip_here
        )
        for c in kept(i):
            c.start()
        return carry

    lax.fori_loop(0, 2, layer_body, 0)
    for c in loads[2:]:
        c.wait()
    mask = s.mask[0:1, :]
    window_tail(True, t, w, s, mixed_of(w, s.fr[...], mask), mask, weight)
    own = pl.ds(off_own, own_len)
    more = [
        pltpu.make_async_copy(s.fo.at[:, own], fo_any.at[:, pl.ds(start, own_len)], sem.at[4]),
        pltpu.make_async_copy(s.dsk, state.dsk, sem.at[8]),
        pltpu.make_async_copy(s.dm, state.dm, sem.at[9]),
        pltpu.make_async_copy(s.x0b, state.x0b, sem.at[10]),
    ]
    for c in more:
        c.start()
    result[0:HALF, :] = s.fo[HALF:C, own].astype(BF)
    result[HALF:C, :] = s.dm[HALF:C, own]
    ld = logdet_part(s, own)
    hi = ld.astype(BF)
    lo = (ld - hi.astype(F32)).astype(BF)
    result[C : C + 16, 0:128] = jnp.concatenate([hi, lo], axis=0)
    ones = jnp.ones((8, own_len), BF)
    d_end_out[...] = nt(s.skl[:, own], s.dproj[:, own])
    ebias_out[...] = nt(ones, s.dproj[:, own])
    for c in stores + more + kept(0) + kept(1):
        c.wait()


def call_own_middle(dp, tp, rows, own_len, frames, scal, w, fr, og, h, skip, pieces):
    t = min(own_len + 2 * HALO, frames)
    sc = dict(
        member=pltpu.VMEM((8, t), F32),
        mask=pltpu.VMEM((8, t), F32),
        pf=pltpu.VMEM((8, t), F32),
        fr=pltpu.VMEM((C, t), BF),
        og=pltpu.VMEM((C, t), BF),
        h=pltpu.VMEM((HID, t), F32),
        skip=pltpu.VMEM((HID, t), F32),
        fo=pltpu.VMEM((C, t), F32),
        hb=pltpu.VMEM((3, HID, t + 256), BF),
        tt=pltpu.VMEM((2, HID, t), BF),
        ss=pltpu.VMEM((2, HID, t), BF),
        pieces=pltpu.VMEM((len(pieces),) + pieces[0].shape, BF),
        dm=pltpu.VMEM((C, t), BF),
        x0b=pltpu.VMEM((HALF, t), BF),
        dproj=pltpu.VMEM((C, t), BF),
        skl=pltpu.VMEM((HID, t), BF),
        dsk=pltpu.VMEM((HID, t), BF),
        wt=pltpu.VMEM((2, 2 * HID, KER * HID), BF),
    )
    sds = jax.ShapeDtypeStruct
    return pl.pallas_call(
        functools.partial(own_middle_kernel, dp, tp, rows, own_len, t, frames, len(pieces), list(sc)),
        out_shape=[
            sds((2, 2 * HID, KER * HID), BF),
            sds((C, frames), F32),
            sds((C + 16, own_len), BF),
            sds((HID, C), F32),
            sds((8, C), F32),
            sds((2, HID, t + 256), BF),
            sds((2, HID, t), BF),
            sds((2, HID, t), BF),
            sds((HID, t), BF),
            sds((C, t), BF),
            sds((HALF, t), BF),
        ],
        in_specs=[sm()] * 4 + [vm()] * len(MID_W) + [hb()] * (4 + len(pieces)),
        out_specs=[hb(), hb(), vm(), vm(), vm()] + [hb()] * 6,
        scratch_shapes=list(sc.values())
        + [pltpu.SemaphoreType.DMA((len(pieces),)), pltpu.SemaphoreType.DMA((18,))],
        compiler_params=pltpu.CompilerParams(vmem_limit_bytes=VMEM_BYTES),
        cost_estimate=pl.CostEstimate(flops=1000, bytes_accessed=1000, transcendentals=0),
        name="ownmid",
    )(*scal, *[getattr(w, k) for k in MID_W], fr, og, h, skip, *pieces)


ASM_W = names_of(lambda w: (w.a_hi, w.a_lo, w.cvec, w.at_b,))


def assemble_kernel(tp, kks, turn, own_len, snames, off, length, lg, *refs):
    w = space(ASM_W, refs)
    refs = refs[len(ASM_W) :]
    n = len(kks)
    dpps, results = refs[:n], refs[n : 2 * n]
    fr_any, og_any, merged, _, fg_in = refs[2 * n : 2 * n + 5]
    fo_any, fg_any = refs[2 * n + 5 : 2 * n + 7]
    s = space(snames, refs[2 * n + 7 : -1])
    sem = refs[-1]
    half = slice(0, HALF)
    blocks = own_len // 128
    turned = pl.ds(pl.multiple_of(from_left(axis(TP), turn, tp) * own_len, 128), own_len)
    tail = [
        pltpu.make_async_copy(merged.at[pl.ds(0, blocks * HALF)], s.dpp, sem.at[n, 0]),
        pltpu.make_async_copy(fg_in.at[:, turned], s.part, sem.at[n, 1]),
    ]
    starts = [pl.multiple_of(from_left(axis(TP), kk, tp) * own_len, 128) for kk in kks]
    loads = [
        [
            pltpu.make_async_copy(fr_any.at[:, pl.ds(start, own_len)], s.fr.at[i], sem.at[i, 0]),
            pltpu.make_async_copy(og_any.at[pl.ds(0, HALF), pl.ds(start, own_len)], s.og.at[i], sem.at[i, 1]),
            pltpu.make_async_copy(results[i].at[pl.ds(0, C)], s.result.at[i], sem.at[i, 2]),
        ]
        for i, start in enumerate(starts)
    ]
    for group in loads + [tail]:
        for c in group:
            c.start()
    stores = []
    for i, start in enumerate(starts):
        make_masks(s, (off, length, lg), own_len, start)
        for c in loads[i]:
            c.wait()
        mask = s.mask[0:1, :]
        fr = s.fr[i]
        where = pl.ds(start, own_len)
        s.fo[i, 0:HALF, :] = (nn(w.a_hi[half, :], fr) + nn(w.a_lo[half, :], fr) + w.cvec[half, :]) * mask
        s.fo[i, HALF:C, :] = s.result[i, 0:HALF, :].astype(F32)
        stores += [pltpu.make_async_copy(s.fo.at[i], fo_any.at[:, where], sem.at[i, 3])]
        stores[-1].start()
        first = s.og[i].astype(F32) * mask + dpps[i][...].astype(F32)
        dm = jnp.concatenate([first.astype(BF), s.result[i, HALF:C, :]], axis=0)
        s.fg[i] = nn(w.at_b[...], dm)
        stores += [pltpu.make_async_copy(s.fg.at[i], fg_any.at[:, where], sem.at[i, 4])]
        stores[-1].start()
    for c in tail:
        c.wait()
    dpp = jnp.concatenate([s.dpp[j * HALF : (j + 1) * HALF, :] for j in range(blocks)], axis=1)
    s.part[...] += nn(w.at_b[:, half], dpp)
    stores += [pltpu.make_async_copy(s.part, fg_any.at[:, turned], sem.at[n, 2])]
    stores[-1].start()
    for c in stores:
        c.wait()


def call_assemble(tp, kks, turn, own_len, scal, w, results, dpps, fr, og, merged, fo, fg):
    n = len(kks)
    sc = dict(
        member=pltpu.VMEM((8, own_len), F32),
        mask=pltpu.VMEM((8, own_len), F32),
        fr=pltpu.VMEM((n, C, own_len), BF),
        og=pltpu.VMEM((n, HALF, own_len), BF),
        result=pltpu.VMEM((n, C, own_len), BF),
        fo=pltpu.VMEM((n, C, own_len), F32),
        fg=pltpu.VMEM((n, C, own_len), F32),
        dpp=pltpu.VMEM((own_len // 128 * HALF, 128), BF),
        part=pltpu.VMEM((C, own_len), F32),
    )
    base = 3 + len(ASM_W) + 2 * n + 3
    return pl.pallas_call(
        functools.partial(assemble_kernel, tp, kks, turn, own_len, list(sc)),
        out_shape=[jax.ShapeDtypeStruct(fo.shape, F32), jax.ShapeDtypeStruct(fg.shape, F32)],
        in_specs=[sm()] * 3 + [vm()] * (len(ASM_W) + n) + [hb()] * (n + 5),
        out_specs=[hb(), hb()],
        input_output_aliases={base: 0, base + 1: 1},
        scratch_shapes=list(sc.values()) + [pltpu.SemaphoreType.DMA((n + 1, 5))],
        compiler_params=pltpu.CompilerParams(vmem_limit_bytes=VMEM_BYTES),
        cost_estimate=pl.CostEstimate(flops=1000, bytes_accessed=1000, transcendentals=0),
        name="assemble",
    )(*scal[1:], *[getattr(w, k) for k in ASM_W], *dpps, *results, fr, og, merged, fo, fg)


LAST_W = names_of(lambda w: (w.rsb, w.pre_b, w.mixfull, w.rows, w.extra, w.at_b, w.d_end, w.d_ebias))


def own_last_kernel(dp, tp, rows, own_len, t, frames, snames, owners, off, length, lg, *refs):
    w = space(LAST_W, refs)
    refs = refs[len(LAST_W) :]
    fr_any, dsk_in, dm_in, x0_in = refs[:4]
    by_layer = [refs[4:8], refs[8:12]]
    gkeep, gsend, okeep, osend_out, dpp, fg_any = refs[12:18]
    s = space(snames, refs[18:-2])
    osend = s.o
    layer_sem, sem = refs[-2:]
    units = HID // tp
    w0, off_own, start = place(own_len, t, frames, axis(TP))
    into = [s.wt, s.tt, s.ss, s.hb]
    first = pltpu.make_async_copy(dsk_in, s.dsk, sem.at[0])
    first.start()
    for layer in reversed(range(LAYERS)):
        for i in (1, 2, 3, 0):
            pltpu.make_async_copy(
                by_layer[layer // 2][i].at[layer % 2], into[i].at[layer], layer_sem.at[i, layer]
            ).start()
    loads = [
        pltpu.make_async_copy(fr_any.at[:, pl.ds(start, own_len)], s.fr, sem.at[5]),
        pltpu.make_async_copy(dm_in, s.dm, sem.at[6]),
        pltpu.make_async_copy(x0_in, s.x0b, sem.at[7]),
    ]
    for c in loads:
        c.start()
    make_masks(s, (off, length, lg), t, w0)
    zero_edges(s.dg, [None], t)
    own = pl.ds(off_own, own_len)
    own_in = pl.ds(pl.multiple_of(off_own + 128, 128), own_len)
    ones = jnp.ones((8, own_len), BF)
    s.smallg[...] = jnp.zeros((16, 2 * HID), F32)
    s.smallg[6:7, 0:C] = w.d_ebias[0:1]
    put_rs, slots, high = rs_writer(tp, osend, units)
    for q in range(tp):
        osend[high, slots[q], units : 2 * units, 0:C] = w.d_end[q * units : (q + 1) * units].astype(BF)
    put_conv = conv_writer(dp, rows, owners, s.g, s.dw)
    s.h[...] = jnp.zeros((HID, t), F32)
    first.wait()

    def back_body(i, carry):
        layer = LAYERS - 1 - i
        for kind in range(4):
            pltpu.make_async_copy(
                by_layer[0][kind].at[0], into[kind].at[layer], layer_sem.at[kind, layer]
            ).wait()
        backward_layer(
            s, t, layer, layer, own, own_in, own_len, s.wt, w.rsb, s.mask[0:1, :], ones, put_rs, put_conv
        )
        return carry

    lax.fori_loop(0, LAYERS, back_body, 0)
    for c in loads:
        c.wait()
    stores = []
    half = s.g.shape[0] // 2
    for ref, lo, i in ((gkeep, 0, 8), (gsend, half, 9)):
        stores += [pltpu.make_async_copy(s.g.at[pl.ds(lo, half)], ref, sem.at[i])]
        stores[-1].start()
    smallg = s.smallg
    d_pre = (s.h[:, own] * s.mask[0:1, own]).astype(BF)
    dpp_v = nn(w.pre_b[...], d_pre).astype(BF)
    dpp[...] = dpp_v
    d_prew = nt(s.x0b[:, own], d_pre)
    dm = s.dm[:, own]
    total = jnp.concatenate([dm[0:HALF].astype(F32) + dpp_v.astype(F32), dm[HALF:C].astype(F32)], axis=0)
    s.fg[...] = nn(w.at_b[...], total.astype(BF))
    stores += [pltpu.make_async_copy(s.fg, fg_any.at[:, pl.ds(start, own_len)], sem.at[10])]
    stores[-1].start()
    fr = s.fr[...]
    qd = nt(dm, fr)
    q0 = nt(dpp_v, fr)
    qd = jnp.concatenate([qd[0:HALF] + q0, qd[HALF:C]], axis=0)
    v = jnp.sum(dm.astype(F32), axis=1, keepdims=True)
    v0 = jnp.sum(dpp_v.astype(F32), axis=1, keepdims=True)
    v = jnp.concatenate([v[0:HALF] + v0, v[HALF:C]], axis=0)
    mixfull = w.mixfull[...]
    es = w.rows[0:1, :]
    bb = w.rows[1:2, :]
    smallg[4:5, 0:C] = es * jnp.sum(mixfull * qd, axis=0, keepdims=True) + w.rows[2:3, :]
    smallg[5:6, 0:C] = jnp.sum(mixfull * v, axis=0, keepdims=True)
    ch_r = lax.broadcasted_iota(jnp.int32, (C, 1), 0)
    ch_c = lax.broadcasted_iota(jnp.int32, (1, C), 1)

    def group(ch):
        return lax.shift_right_logical(ch - jnp.where(ch >= HALF, HALF, 0), 1)

    d2 = jnp.where(group(ch_r) == group(ch_c), v * bb + es * qd, 0.0)
    wide = lax.broadcasted_iota(jnp.int32, (C, 128), 1)
    chan = lax.broadcasted_iota(jnp.int32, (C, 128), 0)
    pair = 2 * (chan >= HALF).astype(jnp.int32) + jnp.bitwise_and(chan, 1)
    one_hot = (pair == wide).astype(F32)
    part = tn(one_hot, d2, PRECISE)
    smallg[8:16, 0:128] = nn(part, one_hot, PRECISE)[0:8] + w.extra[0:8, :]
    small = smallg[...]
    for q in range(tp):
        osend[high, slots[q], units : units + HALF, HID : 2 * HID] = d_prew.astype(BF)
        for h in range(2):
            osend[high, slots[q], 3 * units - 16 : 3 * units, h * units : (h + 1) * units] = small[
                :, h * HID + q * units : h * HID + (q + 1) * units
            ].astype(BF)
        osend[high, slots[q], 3 * units - 12 : 3 * units, 0:C] = small[4:16, 0:C].astype(BF)
    for ref, i in ((okeep, 11), (osend_out, 12)):
        stores += [pltpu.make_async_copy(osend.at[i - 11], ref, sem.at[i])]
        stores[-1].start()
    for c in stores:
        c.wait()


def call_own_last(dp, tp, rows, own_len, frames, scal, w, fr, dsk, dm, x0, kept_a, kept_b):
    shape = conv_shape(dp)
    t = min(own_len + 2 * HALO, frames)
    units = HID // tp
    sc = dict(
        member=pltpu.VMEM((8, t), F32),
        mask=pltpu.VMEM((8, t), F32),
        fr=pltpu.VMEM((C, own_len), BF),
        h=pltpu.VMEM((HID, t), F32),
        wt=pltpu.VMEM((LAYERS, 2 * HID, KER * HID), BF),
        hb=pltpu.VMEM((LAYERS, HID, t + 256), BF),
        tt=pltpu.VMEM((LAYERS, HID, t), BF),
        ss=pltpu.VMEM((LAYERS, HID, t), BF),
        dm=pltpu.VMEM((C, t), BF),
        x0b=pltpu.VMEM((HALF, t), BF),
        dsk=pltpu.VMEM((HID, t), BF),
        d=pltpu.VMEM((2 * HID, t), BF),
        dg=pltpu.VMEM((2 * HID, t + 256), BF),
        dw=pltpu.VMEM((2 * HID, 1024), F32),
        wd=pltpu.VMEM((HID, 2 * KER * HID), BF),
        smallg=pltpu.VMEM((16, 2 * HID), F32),
        g=pltpu.VMEM(shape, BF),
        o=pltpu.VMEM((2, tp, 3 * units, 2 * HID), BF),
        fg=pltpu.VMEM((C, own_len), F32),
    )
    sds = jax.ShapeDtypeStruct
    return pl.pallas_call(
        functools.partial(own_last_kernel, dp, tp, rows, own_len, t, frames, list(sc)),
        out_shape=[
            sds((shape[0] // 2,) + shape[1:], BF),
            sds((shape[0] // 2,) + shape[1:], BF),
            sds((tp, 3 * units, 2 * HID), BF),
            sds((tp, 3 * units, 2 * HID), BF),
            sds((HALF, own_len), BF),
            sds((C, frames), F32),
        ],
        in_specs=[sm()] * 4 + [vm()] * len(LAST_W) + [hb()] * 12,
        out_specs=[hb(), hb(), hb(), hb(), vm(), hb()],
        scratch_shapes=list(sc.values()) + [pltpu.SemaphoreType.DMA((4, LAYERS)), pltpu.SemaphoreType.DMA((13,))],
        compiler_params=pltpu.CompilerParams(vmem_limit_bytes=VMEM_BYTES),
        cost_estimate=pl.CostEstimate(flops=1000, bytes_accessed=1000, transcendentals=0),
        name="ownlast",
    )(*scal, *[getattr(w, k) for k in LAST_W], fr, dsk, dm, x0, *kept_a, *kept_b)


FWD_W = names_of(lambda w: (w.a_hi, w.a_lo, w.cvec, w.pre_t, w.end_t, w.ebias, w.at_b, w.wt_a, w.wt_b, w.rsf, w.bias,))


def fwd_kernel(tp, kk, own_len, t, frames, has_dpp, snames, off, length, lg, *refs):
    w = space(FWD_W, refs)
    refs = refs[len(FWD_W) :]
    fr_any, og_any = refs[:2]
    nd = 1 if has_dpp else 0
    fo_any, p1_any, ld = refs[4 + nd : 7 + nd]
    s = space(snames, refs[7 + nd : -1])
    sem = refs[-1]
    w0, off_own, start = place(own_len, t, frames, from_left(axis(TP), kk, tp))
    dpp = None
    if has_dpp:
        s.dpp[...] = jnp.zeros((HALF, t), BF)
        s.dpp[:, pl.ds(off_own, own_len)] = refs[4][...]
        dpp = s.dpp
    c0 = pltpu.make_async_copy(fr_any.at[:, pl.ds(w0, t)], s.fr, sem.at[0])
    c1 = pltpu.make_async_copy(og_any.at[:, pl.ds(w0, t)], s.og, sem.at[1])
    c0.start()
    c1.start()
    make_masks(s, (off, length, lg), t, w0)
    zero_edges(s.hb, range(2), t)
    c0.wait()
    mask = s.mask[0:1, :]
    mixed = mixed_of(w, s.fr[...], mask)
    s.mixed[...] = mixed
    start_hidden(s, t, w, mixed, mask)
    for half in range(2):
        wt = w.wt_a if half == 0 else w.wt_b

        def layer_body(i, carry):
            layer = 2 * half + i
            forward_layer(
                s, t, wt[i], w.rsf[layer], w.bias[layer], s.mask[0:1, :], i, 1 - i, None
            )
            return carry

        lax.fori_loop(0, 2, layer_body, 0)
    c1.wait()
    dpp = None if dpp is None else dpp[...].astype(F32)
    window_tail(False, t, w, s, s.mixed[...], s.mask[0:1, :], None, dpp)
    own = pl.ds(off_own, own_len)
    o0 = pltpu.make_async_copy(s.fo.at[:, own], fo_any.at[:, pl.ds(start, own_len)], sem.at[2])
    o1 = pltpu.make_async_copy(s.p1.at[:, own], p1_any.at[:, pl.ds(start, own_len)], sem.at[3])
    o0.start()
    o1.start()
    ld[...] = logdet_part(s, own)
    o0.wait()
    o1.wait()


def call_fwd(tp, kk, own_len, frames, scal, w, fr, og, fo, p1, dpp=None):
    t = min(own_len + 2 * HALO, frames)
    sc = dict(
        member=pltpu.VMEM((8, t), F32),
        mask=pltpu.VMEM((8, t), F32),
        pf=pltpu.VMEM((8, t), F32),
        fr=pltpu.VMEM((C, t), BF),
        og=pltpu.VMEM((C, t), BF),
        mixed=pltpu.VMEM((C, t), F32),
        h=pltpu.VMEM((HID, t), F32),
        skip=pltpu.VMEM((HID, t), F32),
        fo=pltpu.VMEM((C, t), F32),
        p1=pltpu.VMEM((C, t), F32),
        hb=pltpu.VMEM((2, HID, t + 256), BF),
    )
    n = len(FWD_W)
    more = [] if dpp is None else [dpp]
    if more:
        sc.update(dpp=pltpu.VMEM((HALF, t), BF))
    return pl.pallas_call(
        functools.partial(fwd_kernel, tp, kk, own_len, t, frames, dpp is not None, list(sc)),
        out_shape=(
            jax.ShapeDtypeStruct((C, frames), F32),
            jax.ShapeDtypeStruct((C, frames), F32),
            jax.ShapeDtypeStruct((8, 128), F32),
        ),
        in_specs=[sm()] * 3 + [vm()] * n + [hb()] * 4 + [vm()] * len(more),
        out_specs=(hb(), hb(), vm()),
        input_output_aliases={n + 5: 0, n + 6: 1},
        scratch_shapes=list(sc.values()) + [pltpu.SemaphoreType.DMA((4,))],
        compiler_params=pltpu.CompilerParams(vmem_limit_bytes=VMEM_BYTES),
        cost_estimate=pl.CostEstimate(flops=1000, bytes_accessed=1000, transcendentals=0),
        name="fwd",
    )(*scal[1:], *[getattr(w, k) for k in FWD_W], fr, og, fo, p1, *more)


def moments(moment, square, grad):
    new_moment = BETA * moment + (1.0 - BETA) * grad
    new_square = BETA * square + (1.0 - BETA) * grad * grad
    correction = 1.0 - BETA**STEP
    direction = new_moment / correction / (jnp.sqrt(new_square / correction) + EPSILON)
    return (new_moment, new_square, direction)


def adam_update(weight, moment, square, grad, rate):
    new_moment, new_square, direction = moments(moment, square, grad)
    return (weight - rate * (direction + DECAY * weight), new_moment, new_square)


def fold_kernel(n, tp, *refs):
    keep_a, got_a, keep_o, got_o, dpp = refs[:5]
    outs = refs[5:]
    for m in range(n):
        outs[m][...] = (keep_a[m].astype(F32) + got_a[m].astype(F32)).astype(BF)
    keep, merged = outs[n:]
    blocks = dpp.shape[1] // 128
    for j in range(blocks):
        merged[j * HALF : (j + 1) * HALF, :] = dpp[:, j * 128 : (j + 1) * 128]
    half = tp // 2
    size = keep_o.shape[1]
    for q in range(tp):
        value = (keep_o[q].astype(F32) + got_o[q].astype(F32)).astype(BF)
        for j in range(3):
            lo = ((q % half) * 3 + j) * size
            part = value[:, j * 128 : (j + 1) * 128]
            if q < half:
                keep[lo : lo + size, :] = part
            else:
                merged[blocks * HALF + lo : blocks * HALF + lo + size, :] = part


def call_fold(keep_a, got_a, keep_o, got_o, dpp):
    n, tp, size = keep_a.shape[0], keep_o.shape[0], keep_o.shape[1]
    other = (tp // 2) * 3 * size
    sds = jax.ShapeDtypeStruct
    return pl.pallas_call(
        functools.partial(fold_kernel, n, tp),
        out_shape=[sds((LAYERS,) + keep_a.shape[2:], BF)] * n
        + [sds((other, 128), BF), sds((dpp.shape[1] // 128 * HALF + other, 128), BF)],
        in_specs=[vm()] * 5,
        out_specs=[vm()] * (n + 2),
        compiler_params=pltpu.CompilerParams(vmem_limit_bytes=VMEM_BYTES),
        cost_estimate=pl.CostEstimate(flops=1000, bytes_accessed=1000, transcendentals=0),
        name="fold",
    )(keep_a, got_a, keep_o, got_o, dpp)


def join_basis(own, other, scratch):
    core = jnp.bitwise_and(axis(DP), 1)
    for kk in range(own.shape[0]):
        for i in range(2):
            scratch[kk, 2 * core + i] = own[kk, i]
            scratch[kk, 2 * (1 - core) + i] = other[kk, i]


def rotate_kernel(n, tp, *refs):
    parts = refs[2 : 2 + n]
    outs = refs[2 + n : -1]
    basis = refs[-1]
    join_basis(refs[0], refs[1], basis)
    for layer in range(LAYERS):
        total = parts[0][layer].astype(F32)
        for m in range(1, n):
            total = total + parts[m][layer].astype(F32)
        total = total.astype(BF)
        for kk in range(tp):
            outs[kk][layer] = nn(basis[kk, layer], total).astype(BF)


def call_rotate(tp, basis, parts):
    cols = basis[0].shape[2]
    n = len(parts)
    return pl.pallas_call(
        functools.partial(rotate_kernel, n, tp),
        out_shape=[jax.ShapeDtypeStruct((LAYERS, cols, 128), BF)] * tp,
        in_specs=[vm()] * (2 + n),
        out_specs=[vm()] * tp,
        scratch_shapes=[pltpu.VMEM((tp, LAYERS, cols, 2 * HID), BF)],
        compiler_params=pltpu.CompilerParams(vmem_limit_bytes=8 * 2**20),
        cost_estimate=pl.CostEstimate(flops=1000, bytes_accessed=1000, transcendentals=0),
        name="rotate",
    )(*basis, *parts)


def moment_kernel(tp, rows, *refs):
    parts = refs[:tp]
    moment, square, new_moment, new_square, direction = refs[tp:]
    total = parts[0][...].astype(F32)
    for kk in range(1, tp):
        total = total + parts[kk][...].astype(F32)
    grad = total[:, :, 0:rows]
    m, v, d = moments(moment[...], square[...], grad)
    new_moment[...] = m
    new_square[...] = v
    direction[:, :, 0:rows] = d.astype(BF)
    if rows < 128:
        direction[:, :, rows:128] = jnp.zeros(d.shape[:2] + (128 - rows,), BF)


def call_moments(tp, rows, parts, moment, square):
    shape = moment.shape
    return pl.pallas_call(
        functools.partial(moment_kernel, tp, rows),
        out_shape=[
            jax.ShapeDtypeStruct(shape, F32),
            jax.ShapeDtypeStruct(shape, F32),
            jax.ShapeDtypeStruct(shape[:2] + (128,), BF),
        ],
        in_specs=[vm()] * (tp + 2),
        out_specs=[vm()] * 3,
        name="moments",
    )(*parts, moment, square)


def back_kernel(tp, rows, *refs):
    directions = refs[2 : 2 + tp]
    weight, out, scratch, basis = refs[2 + tp :]
    join_basis(refs[0], refs[1], basis)
    units = HID // tp
    me_tp = axis(TP)
    for layer in range(LAYERS):
        total = tn(basis[0, layer], directions[0][layer])
        for kk in range(1, tp):
            total = total + tn(basis[kk, layer], directions[kk][layer])
        scratch[layer] = total
    for layer in range(LAYERS):
        for h in range(2):
            row = pl.ds(pl.multiple_of(h * HID + me_tp * units, 16), units)
            back = scratch[layer, row, 0:rows]
            here = slice(h * units, (h + 1) * units)
            value = weight[layer, here, :]
            out[layer, here, :] = value - RATE_CONV * (back + DECAY * value)


def call_back(tp, rows, basis, directions, weight):
    return pl.pallas_call(
        functools.partial(back_kernel, tp, rows),
        out_shape=jax.ShapeDtypeStruct(weight.shape, F32),
        in_specs=[vm()] * (tp + 3),
        out_specs=vm(),
        scratch_shapes=[
            pltpu.VMEM((LAYERS, 2 * HID, 128), F32),
            pltpu.VMEM((tp, LAYERS, basis[0].shape[2], 2 * HID), BF),
        ],
        cost_estimate=pl.CostEstimate(flops=1000, bytes_accessed=1000, transcendentals=0),
        name="back",
    )(*basis, *directions, weight)


def small_kernel(tp, *refs):
    ins = refs[2:20]
    outs = refs[20:-1]
    scratch = refs[-1]
    size = scratch.shape[1]
    for i in range(2):
        for j in range(3):
            scratch[i, :, j * 128 : (j + 1) * 128] = refs[i][j * size : (j + 1) * size, :]
    lows, highs = scratch.at[0], scratch.at[1]
    units = HID // tp
    core = jnp.bitwise_and(axis(DP), 1)

    def put(i, grad, rate, index=None):
        if index is None:
            new = adam_update(ins[3 * i][...], ins[3 * i + 1][...], ins[3 * i + 2][...], grad, rate)
            for k in range(3):
                outs[3 * i + k][...] = new[k]
        else:
            new = adam_update(ins[3 * i][index], ins[3 * i + 1][index], ins[3 * i + 2][index], grad, rate)
            for k in range(3):
                outs[3 * i + k][index] = new[k]

    def rows(half, lo, size, c0, c1):
        a = lows[lo : lo + size, c0:c1].astype(F32)
        b = highs[lo : lo + size, c0:c1].astype(F32)
        return jnp.where(core == half, a, b)

    tail = rows(1, 3 * units - 16, 16, 0, 2 * HID)
    put(0, tail[4:7, 0:C], RATE_SMALL)
    put(1, tail[8:12, 0:4], RATE_MIX)
    put(2, rows(1, units, HALF, HID, 2 * HID), RATE_PRE)
    for h in range(2):
        put(3, tail[0:LAYERS, h * units : (h + 1) * units], RATE_BIAS, (slice(None), h, slice(None)))
    for layer in range(LAYERS):
        half = 1 if layer == LAYERS - 1 else 0
        lo = 0 if layer == LAYERS - 1 else layer * units
        put(4, rows(half, lo, units, 0, HID), RATE_RESSKIP, LAYERS - 1 + layer)
        if layer < LAYERS - 1:
            put(4, rows(half, lo, units, HID, 2 * HID), RATE_RESSKIP, layer)
    put(5, rows(1, units, units, 0, C), RATE_END)


def call_small(tp, low, high, ins):
    return pl.pallas_call(
        functools.partial(small_kernel, tp),
        out_shape=[jax.ShapeDtypeStruct(x.shape, F32) for x in ins],
        in_specs=[vm()] * (2 + len(ins)),
        out_specs=[vm()] * len(ins),
        scratch_shapes=[pltpu.VMEM((2, low.shape[0] // 3, 2 * HID), BF)],
        name="smallupd",
    )(low, high, *ins)


def local(
    frames_in,
    out_grad,
    logdet_grad,
    lengths,
    offsets,
    owners,
    small_params,
    small_moment,
    small_square,
    mix,
    mix_moment,
    mix_square,
    pre_weight,
    pre_moment,
    pre_square,
    conv_weight,
    conv_moment,
    conv_square,
    conv_basis,
    conv_bias,
    conv_bias_moment,
    conv_bias_square,
    res_skip,
    res_skip_moment,
    res_skip_square,
    end_weight,
    end_moment,
    end_square,
):
    dp = lax.axis_size("dp")
    tp = lax.axis_size("tp")
    frames = frames_in.shape[0]
    rows = conv_weight.shape[1]
    units = conv_weight.shape[3]
    own_len = frames // tp
    packed = dp * 128 <= MAX_PACKED

    def shift_tp(x, kk):
        return lax.ppermute(x, "tp", [(i, (i + kk) % tp) for i in range(tp)])

    def swap_dp(x, mask):
        return lax.ppermute(x, "dp", [(i, i ^ mask) for i in range(dp)])

    def swap_tp(x, mask):
        return lax.ppermute(x, TP, [(i, i ^ mask) for i in range(tp)])

    def plus(x, y):
        return (x.astype(F32) + y.astype(F32)).astype(BF)

    def gather_tp(x):
        return [x] + [shift_tp(x, kk) for kk in range(1, tp)]

    def after(value, *deps):
        return lax.optimization_barrier((value, *deps))[0]

    cw = jnp.transpose(conv_weight, (0, 2, 3, 1)).reshape(LAYERS, 2 * units, rows)
    shard, shard_b = call_pack(rows, units, cw, res_skip, end_weight, conv_bias)
    basis_all = conv_basis.reshape(LAYERS, 2 * HID, -1)
    w = space(CONST_W, call_consts(mix, logdet_grad, small_params, pre_weight, basis_all))
    basis_t = w.basis

    def chips(col):
        return {m: (col if m == 0 else swap_dp(col, m)) for m in range(0, dp, 2)}

    def cores(pieces):
        pieces = dict(pieces)
        for m in range(0, dp, 2):
            pieces[m + 1] = swap_dp(pieces[m], 1)
        pieces = [pieces[m] for m in range(dp)]
        if not packed:
            slot = jnp.bitwise_xor(lax.axis_index("dp"), owners)
            column_of = lax.rem(lax.axis_index("tp") - jnp.arange(tp) + tp, tp)
            stacked = jnp.stack(pieces)[slot][:, column_of]
            stacked = stacked.reshape(dp, tp, 2, 2, units, 128)[..., :rows]
            pieces = [jnp.transpose(stacked, (2, 3, 1, 4, 0, 5)).reshape(2, 2 * HID, KER * HID)]
        return pieces

    both = gather_tp(shard)
    col_a = after(jnp.stack([x[: 4 * units] for x in both]), w.rows)
    res_own = jnp.stack([x[4 * units :] for x in both])
    half_a = chips(col_a)
    res_pieces = [res_own, swap_dp(res_own, 1)]
    pieces_a = cores(half_a)
    col_b = jnp.stack(gather_tp(after(shard_b, w.rows)))
    half_b = chips(after(col_b, half_a[dp - 2]))
    basis_t = after(basis_t, *[half_a[m] for m in range(2, dp, 2)])[None]
    basis_near = swap_tp(basis_t, 1)
    scal = [owners, offsets, lengths, logdet_grad]
    fr = frames_in.T
    og = out_grad.T

    (wt_a, rsb, rsf, end, end_t, bias, h, skip, hbs, tt, ss) = call_own_forward(
        dp, tp, rows, own_len, frames, scal, w, fr, pieces_a, res_pieces
    )
    w.wt_a = wt_a
    w.rsb = rsb
    w.rsf = rsf
    w.end = end
    w.end_t = end_t
    w.bias = bias
    pieces_b = cores(after(half_b, h))
    basis_col = jnp.concatenate([basis_t, after(basis_near, h)])
    basis_far = swap_tp(basis_col, 2)
    (wt_b, fo, result, d_end, d_ebias, hbs_b, tt_b, ss_b, dsk, dm, x0) = call_own_middle(
        dp, tp, rows, own_len, frames, scal, w, fr, og, h, skip, pieces_b
    )
    w.wt_b = wt_b
    basis_far, result = lax.optimization_barrier((basis_far, result))
    basis_col = jnp.concatenate([basis_col, basis_far])
    basis_pieces = [basis_col, swap_dp(basis_col, 1)]
    turn = tp // 2
    rest = [kk for kk in range(1, tp) if kk != turn]
    results = {kk: shift_tp(result, kk) for kk in rest}
    w.d_end = d_end
    w.d_ebias = d_ebias
    (keep_a, send_a, keep_o, send_o, dpp, fg) = call_own_last(
        dp, tp, rows, own_len, frames, scal, w, fr, dsk, dm, x0, [wt_a, tt, ss, hbs], [wt_b, tt_b, ss_b, hbs_b]
    )

    def order(keep, send):
        if packed:
            return keep, send
        gsend = jnp.concatenate([keep, send])
        where = jnp.bitwise_xor(lax.axis_index("dp"), bit_reverse(jnp.arange(dp), (dp - 1).bit_length()))
        block = jnp.argsort(owners)[where]
        gsend = jnp.transpose(gsend.reshape(LAYERS, 2 * HID, dp, rows), (2, 0, 1, 3))[block]
        gsend = jnp.pad(gsend, ((0, 0), (0, 0), (0, 0), (0, 128 - rows)))
        return gsend[: dp // 2], gsend[dp // 2 :]

    send_a, send_o, basis_pieces[1], *gone = lax.optimization_barrier(
        (send_a, send_o, basis_pieces[1], *results.values())
    )
    results = dict(zip(results, gone))
    keep_a, send_a = order(keep_a, send_a)
    got_a = swap_dp(send_a, 1)
    got_o = swap_dp(send_o, 1)
    folded = call_fold(keep_a, got_a, keep_o, got_o, dpp)
    n = dp // 2
    bits = (dp - 1).bit_length()
    masks = [2 * bit_reverse(p, bits - 1) for p in range(n)]
    parts = [folded[0]] + [swap_dp(folded[p], masks[p]) for p in range(1, n)]
    turn = tp // 2
    merged = swap_tp(folded[n + 1], turn)
    dpps = {kk: shift_tp(dpp, kk) for kk in rest}

    fr1, dpps[rest[-1]] = lax.optimization_barrier((after(fr, folded[0]), dpps[rest[-1]]))
    fo, fg, ld = call_fwd(tp, turn, own_len, frames, scal, w, fr1, og, fo, fg)
    lds = [ld[:, 0]] + [
        jnp.sum(x[C : C + 16, 0].astype(F32).reshape(2, 8), axis=0) for x in [result, *results.values()]
    ]

    ready, *near = lax.optimization_barrier((parts[0], ld, *parts[1:], *[dpps[kk] for kk in rest]))
    parts = [ready] + near[1:n]
    dpps.update(zip(rest, near[n:]))
    turned = call_rotate(tp, basis_pieces, parts)
    rotated = [turned[0]] + [swap_tp(turned[x], x) for x in range(1, tp)]
    size = 3 * (3 * units)
    merged = after(merged, ld)
    others = [
        plus(folded[n][i * size : (i + 1) * size], merged[own_len // 128 * HALF + i * size :][:size])
        for i in range(turn)
    ]
    others = [others[0], swap_tp(after(others[1], turned[0]), 1)]
    fo, fg = call_assemble(
        tp, rest, turn, own_len, scal, w, [results[kk] for kk in rest], [dpps[kk] for kk in rest],
        after(fr, turned[0]), og, merged, fo, fg,
    )
    total = plus(others[0], after(others[1], fg))
    steps = [1 << bit for bit in range(1, bits)]
    got = swap_dp(total, steps[0])
    conv_m, conv_v, direction = call_moments(
        tp,
        rows,
        [rotated[0]] + [after(x, fg) for x in rotated[1:]],
        jnp.transpose(conv_moment, (0, 2, 1)),
        jnp.transpose(conv_square, (0, 2, 1)),
    )
    directions = [direction] + [swap_tp(direction, x) for x in range(1, tp)]
    total = plus(total, after(got, direction))
    for mask in steps[1:]:
        total = plus(total, swap_dp(total, mask))
    other = swap_dp(total, 1)
    updated = call_small(
        tp,
        total,
        other,
        [
            small_params, small_moment, small_square,
            mix, mix_moment, mix_square,
            pre_weight, pre_moment, pre_square,
            conv_bias, conv_bias_moment, conv_bias_square,
            res_skip, res_skip_moment, res_skip_square,
            end_weight, end_moment, end_square,
        ],
    )
    directions = [direction] + [after(x, updated[0]) for x in directions[1:]]
    conv_new = call_back(tp, rows, basis_pieces, directions, cw)
    logdet = w.extra[8:, 0] + sum(lds) / lengths.astype(F32)

    def conv_out(x):
        return jnp.transpose(x.reshape(LAYERS, 2, units, rows), (0, 3, 1, 2))

    (small_new, small_m, small_v, mix_new, mix_m, mix_v, pre_new, pre_m, pre_v, bias_new, bias_m, bias_v,
     rs_new, rs_m, rs_v, end_new, end_m, end_v) = updated
    return (
        fo.T,
        logdet,
        fg.T,
        small_new,
        small_m,
        small_v,
        mix_new,
        mix_m,
        mix_v,
        pre_new,
        pre_m,
        pre_v,
        conv_out(conv_new),
        jnp.transpose(conv_m, (0, 2, 1)),
        jnp.transpose(conv_v, (0, 2, 1)),
        bias_new,
        bias_m,
        bias_v,
        rs_new,
        rs_m,
        rs_v,
        end_new,
        end_m,
        end_v,
    )


def solution(mesh):
    return jax.shard_map(
        local,
        mesh=mesh,
        in_specs=(
            P("dp", None),
            P("dp", None),
            P("dp"),
            P("dp"),
            P("dp"),
            P(),
            P(),
            P(),
            P(),
            P(),
            P(),
            P(),
            P(),
            P(),
            P(),
            P(None, "dp", None, "tp"),
            P(None, "dp", "tp"),
            P(None, "dp", "tp"),
            P(None, None, None, "tp"),
            P(None, None, "tp"),
            P(None, None, "tp"),
            P(None, None, "tp"),
            P(None, "tp", None),
            P(None, "tp", None),
            P(None, "tp", None),
            P("tp", None),
            P("tp", None),
            P("tp", None),
        ),
        out_specs=(
            P("dp", None),
            P("dp"),
            P("dp", None),
            P(),
            P(),
            P(),
            P(),
            P(),
            P(),
            P(),
            P(),
            P(),
            P(None, "dp", None, "tp"),
            P(None, "dp", "tp"),
            P(None, "dp", "tp"),
            P(None, None, "tp"),
            P(None, None, "tp"),
            P(None, None, "tp"),
            P(None, "tp", None),
            P(None, "tp", None),
            P(None, "tp", None),
            P("tp", None),
            P("tp", None),
            P("tp", None),
        ),
        check_vma=False,
    )
```
